32 devices in a mesh: seq: 4 (over z), fsdp: 4 (over y, core), replica: 2 (over x).
Axes of the slice: x: 2, y: 2, z: 4, core: 2. Of those that a mesh axis runs over, the one named last changes fastest.
Arguments:
- tokens: bfloat16 [8, 512, 1600], P(('fsdp', 'replica'), 'seq'), may hold values from -6 to 6
- cotangent: bfloat16 [8, 512, 1600], P(('fsdp', 'replica'), 'seq'), may hold values from -6 to 6
- segments: int32 [8, 512], P(('fsdp', 'replica'), 'seq'), may hold values from 0 to 3, never falling along the last dimension, each value on 1 to 256 neighbouring positions
- norm1_gain: bfloat16 [2, 1600], P(None, ('seq', 'fsdp')), may hold values from 0.099609375 to 1.8984375
- norm1_shift: bfloat16 [2, 1600], P(None, ('seq', 'fsdp')), may hold values from -3 to 3
- w_qkv: bfloat16 [2, 1600, 4800], P(None, ('seq', 'fsdp')), may hold values from -0.15625 to 0.15625
- b_query: bfloat16 [2, 1600], P(None, ('seq', 'fsdp')), may hold values from -3 to 3
- b_value: bfloat16 [2, 1600], P(None, ('seq', 'fsdp')), may hold values from -3 to 3
- w_out: bfloat16 [2, 1600, 1600], P(None, ('seq', 'fsdp')), may hold values from -1.25 to 1.25
- b_out: bfloat16 [2, 1600], P(None, ('seq', 'fsdp')), may hold values from -3 to 3
- norm2_gain: bfloat16 [2, 1600], P(None, ('seq', 'fsdp')), may hold values from 0.099609375 to 1.8984375
- norm2_shift: bfloat16 [2, 1600], P(None, ('seq', 'fsdp')), may hold values from -3 to 3
- w_up: bfloat16 [2, 1600, 6400], P(None, ('seq', 'fsdp')), may hold values from -0.15625 to 0.15625
- b_up: bfloat16 [2, 6400], P(None, ('seq', 'fsdp')), may hold values from -3 to 3
- w_down: bfloat16 [2, 6400, 1600], P(None, ('seq', 'fsdp')), may hold values from -0.109375 to 0.109375
- b_down: bfloat16 [2, 1600], P(None, ('seq', 'fsdp')), may hold values from -3 to 3
Outputs:
- output: float32 [8, 512, 1600], P(('fsdp', 'replica'), 'seq')
- grad_tokens: float32 [8, 512, 1600], P(('fsdp', 'replica'), 'seq')
- grad_norm1_gain: float32 [2, 1600], P(None, ('seq', 'fsdp'))
- grad_norm1_shift: float32 [2, 1600], P(None, ('seq', 'fsdp'))
- grad_w_qkv: float32 [2, 1600, 4800], P(None, ('seq', 'fsdp'))
- grad_b_query: float32 [2, 1600], P(None, ('seq', 'fsdp'))
- grad_b_value: float32 [2, 1600], P(None, ('seq', 'fsdp'))
- grad_w_out: float32 [2, 1600, 1600], P(None, ('seq', 'fsdp'))
- grad_b_out: float32 [2, 1600], P(None, ('seq', 'fsdp'))
- grad_norm2_gain: float32 [2, 1600], P(None, ('seq', 'fsdp'))
- grad_norm2_shift: float32 [2, 1600], P(None, ('seq', 'fsdp'))
- grad_w_up: float32 [2, 1600, 6400], P(None, ('seq', 'fsdp'))
- grad_b_up: float32 [2, 6400], P(None, ('seq', 'fsdp'))
- grad_w_down: float32 [2, 6400, 1600], P(None, ('seq', 'fsdp'))
- grad_b_down: float32 [2, 1600], P(None, ('seq', 'fsdp'))
The draws below stay inside these ranges and needn't reach their ends.
Inputs may be any that keep to these rules, and one draw needn't show every extreme that they name: `segments`: segment numbers never fall along a sequence; each document has at most 256 tokens.
All inputs are finite; a program needn't handle non-finite values.
Results may differ from the reference program's by a relative error of at most 0.019.
Values may be sent and summed in bfloat16 or wider, within the bound.
No kernel may reach another device: no remote copies, remote signals or barrier semaphores. Data moves between devices by JAX's collectives and lax.ppermute only.
A program may use at most 448 MiB of HBM per device.

```python
import math
import jax
import jax.numpy as jnp
import numpy as np
from jax import lax

D = 1600
HEADS = 25
HD = 64
FF = 6400
LAYERS = 2
LEN = 512
NSEQ = 8


def level_of(key, shape, pieces, low, top_value):
    def one(dim, parts):
        heights = jax.random.uniform(jax.random.fold_in(jax.random.fold_in(key, 6), dim), (parts,), jnp.float32, low / len(pieces), top_value / len(pieces))
        return jnp.repeat(jnp.exp(heights), shape[dim] // parts).reshape((-1,) + (1,) * (len(shape) - dim - 1))

    loudness = one(*pieces[0])
    for cut in pieces[1:]:
        loudness = loudness * one(*cut)
    return loudness


def split_up(count, total, limit, lean):
    loads = [(1 << 20) // math.isqrt(rank ** lean) + 1 for rank in range(2, count + 1)]
    spare, counts = total - limit - (count - 1), [1] * (count - 1)
    while spare > 0:
        free = [i for i in range(count - 1) if counts[i] < limit]
        mass, left = sum([loads[i] for i in free]), spare
        for i in free:
            more = min(limit - counts[i], max(1, left * loads[i] // mass), spare)
            counts[i] = counts[i] + more
            spare = spare - more
    return np.array([limit] + counts)


def ragged_sizes(rng, amount, total, limit, skew):
    if amount == 2:
        one = jax.random.randint(rng, (), max(1, total - limit), min(limit, total - 1) + 1)
        return jnp.stack([one, total - one])
    sizes = jnp.asarray(split_up(amount, total, limit, skew), jnp.int32)
    pairs = (amount - 1) // 2
    giver, sink = sizes[1:1 + 2 * pairs:2], sizes[2:2 + 2 * pairs:2]
    slack = jnp.minimum(giver - 1, limit - sink)
    passed = jax.random.randint(jax.random.fold_in(rng, 1), (pairs,), 0, 1 << 20) % (slack + 1)
    sizes = sizes.at[1:1 + 2 * pairs:2].set(giver - passed).at[2:2 + 2 * pairs:2].set(sink + passed)
    return sizes[jax.random.permutation(jax.random.fold_in(rng, 2), amount)]


def gaussian(stream_key, dims, deviation, bound, cuts=(), kind=jnp.bfloat16):
    drawn = jax.random.normal(stream_key, dims, jnp.float32) * deviation
    if len(cuts) > 0:
        drawn = level_of(stream_key, dims, cuts, -0.22, 0.18) * drawn
    return jnp.clip(drawn, min=-bound, max=bound).astype(kind)


def setup_inputs(seed: int = 0) -> dict:
    key_list = jax.random.split(jax.random.key(seed), 17)
    return {
        "tokens": gaussian(key_list[0], (NSEQ, LEN, D), 1.0, 6.0, ((0, 8), (1, 4))),
        "cotangent": gaussian(key_list[1], (NSEQ, LEN, D), 1.0, 6.0, ((0, 8), (1, 4))),
        "segments": jax.vmap(lambda own: jnp.searchsorted(jnp.cumsum(ragged_sizes(own, 4, LEN, LEN // 2, 2)), jnp.arange(LEN), side="right"))(jax.random.split(key_list[2], NSEQ)).reshape((NSEQ, LEN)).astype(jnp.int32),
        "norm1_gain": jnp.clip(1.0 + 0.18 * jax.random.normal(key_list[3], (LAYERS, D), jnp.float32), 0.099609375, 1.8984375).astype(jnp.bfloat16),
        "norm1_shift": gaussian(key_list[4], (LAYERS, D), 0.5, 3.0, ((1, 16),)),
        "w_qkv": gaussian(key_list[5], (LAYERS, D, 3 * D), D ** -0.5, 0.15625, ((1, 16),)),
        "b_query": gaussian(key_list[6], (LAYERS, D), 0.5, 3.0, ((1, 16),)),
        "b_value": gaussian(key_list[7], (LAYERS, D), 0.5, 3.0, ((1, 16),)),
        "w_out": gaussian(key_list[8], (LAYERS, D, D), (max(D // 64, 4)) ** -0.5, 1.25, ((1, 16),)),
        "b_out": gaussian(key_list[9], (LAYERS, D), 0.5, 3.0, ((1, 16),)),
        "norm2_gain": jnp.clip(1.0 + 0.18 * jax.random.normal(key_list[10], (LAYERS, D), jnp.float32), 0.099609375, 1.8984375).astype(jnp.bfloat16),
        "norm2_shift": gaussian(key_list[11], (LAYERS, D), 0.5, 3.0, ((1, 16),)),
        "w_up": gaussian(key_list[12], (LAYERS, D, FF), D ** -0.5, 0.15625, ((1, 16),)),
        "b_up": gaussian(key_list[13], (LAYERS, FF), 0.5, 3.0, ((1, 16),)),
        "w_down": gaussian(key_list[14], (LAYERS, FF, D), (FF // 2) ** -0.5, 0.109375, ((1, 16),)),
        "b_down": gaussian(key_list[15], (LAYERS, D), 0.5, 3.0, ((1, 16),)),
    }


@jax.custom_vjp
def low(v):
    return lax.optimization_barrier(v.astype(jnp.bfloat16)).astype(jnp.float32)

@jax.custom_vjp
def low_back(v):
    return v

def low_keep(v):
    return (low(v), None)

def low_pass(kept, grad):
    return (grad,)

def back_keep(v):
    return (v, None)

def back_low(kept, grad):
    return (low(grad),)
low.defvjp(low_keep, low_pass)
low_back.defvjp(back_keep, back_low)

def both_ways(value):
    return low_back(low(value))

def layer_norm(hidden, gain, shift):
    mean = lax.optimization_barrier(jnp.mean(hidden, axis=-1, keepdims=True))
    centred = hidden - mean
    spread = lax.optimization_barrier(jnp.mean(centred * centred, axis=-1, keepdims=True))
    return centred * lax.rsqrt(spread + 1e-05) * gain + shift

def gelu_tanh(value):
    return 0.5 * value * (1.0 + jnp.tanh(0.7978845608028654 * (value + 0.044715 * value * value * value)))

def matmul(left, right):
    return jnp.dot(left, right, precision=lax.Precision.HIGHEST)

def block(hidden, segment, params):
    norm1_gain, norm1_shift, w_qkv, b_query, b_value, w_out, b_out, norm2_gain, norm2_shift, w_up, b_up, w_down, b_down = params
    length = hidden.shape[0]
    normed = low(layer_norm(hidden, norm1_gain, norm1_shift))
    packed = matmul(normed, w_qkv)
    queries = both_ways(packed[:, :D] + b_query)
    keys = both_ways(packed[:, D:2 * D])
    values = both_ways(packed[:, 2 * D:] + b_value)
    query_heads = queries.reshape(length, HEADS, HD)
    key_heads = keys.reshape(length, HEADS, HD)
    value_heads = values.reshape(length, HEADS, HD)
    raw = jnp.einsum('qhd,khd->hqk', query_heads, key_heads, precision=lax.Precision.HIGHEST)
    scores = low_back(raw * (1.0 / math.sqrt(HD)))
    position = jnp.arange(length, dtype=jnp.int32)
    allowed = (segment[:, None] == segment[None, :]) & (position[None, :] <= position[:, None])
    scores = jnp.where(allowed[None], scores, -1e+30)
    top = lax.optimization_barrier(jnp.max(scores, axis=-1, keepdims=True))
    expo = jnp.exp(scores - top)
    probs = low(expo / lax.optimization_barrier(jnp.sum(expo, axis=-1, keepdims=True)))
    mixed = jnp.einsum('hqk,khd->qhd', probs, value_heads, precision=lax.Precision.HIGHEST)
    mixed = both_ways(mixed.reshape(length, D))
    attended = low_back(matmul(mixed, w_out) + b_out)
    middle = hidden + attended
    normed_two = low(layer_norm(middle, norm2_gain, norm2_shift))
    lifted = low_back(matmul(normed_two, w_up) + b_up)
    activated = low(gelu_tanh(lifted))
    lowered = low_back(matmul(activated, w_down) + b_down)
    return middle + lowered

def reference(tokens, cotangent, segments, norm1_gain, norm1_shift, w_qkv, b_query, b_value, w_out, b_out, norm2_gain, norm2_shift, w_up, b_up, w_down, b_down):
    params = tuple((array.astype(jnp.float32) for array in (norm1_gain, norm1_shift, w_qkv, b_query, b_value, w_out, b_out, norm2_gain, norm2_shift, w_up, b_up, w_down, b_down)))

    def forward(inputs, weights):

        def one_sequence(pair):
            hidden, segment = pair
            for layer in range(LAYERS):
                hidden = block(hidden, segment, tuple((weight[layer] for weight in weights)))
            return hidden
        return lax.map(jax.checkpoint(one_sequence), (inputs, segments))
    output, pullback = jax.vjp(forward, tokens.astype(jnp.float32), params)
    input_grad, grads = pullback(cotangent.astype(jnp.float32))
    return (output, input_grad, grads[0], grads[1], grads[2], grads[3], grads[4], grads[5], grads[6], grads[7], grads[8], grads[9], grads[10], grads[11], grads[12])
```

```python
import functools
import math

import jax
import jax.numpy as jnp
from jax import lax
from jax.sharding import PartitionSpec as P

HEADS = 25
HD = 64
BF = jnp.bfloat16
F32 = jnp.float32
ALL = ("seq", "fsdp", "replica")
GROUP = ("fsdp", "replica")
OWNERS = ("seq", "fsdp")


def dot(a, b, ca, cb):
    return lax.dot_general(a, b, (((ca,), (cb,)), ((), ())), preferred_element_type=F32)


def norm_parts(v):
    mean = jnp.mean(v, axis=-1, keepdims=True)
    centred = v - mean
    spread = jnp.mean(centred * centred, axis=-1, keepdims=True)
    inv = lax.rsqrt(spread + 1e-05)
    return centred * inv, inv


def norm_pull(grad, unit, inv, gain):
    scaled = grad * gain
    first = jnp.mean(scaled, axis=-1, keepdims=True)
    second = jnp.mean(scaled * unit, axis=-1, keepdims=True)
    return inv * (scaled - first - unit * second)


def gelu_tanh(value):
    return (
        0.5
        * value
        * (1.0 + jnp.tanh(0.7978845608028654 * (value + 0.044715 * value * value * value)))
    )


def gelu_slope(value):
    inner = 0.7978845608028654 * (value + 0.044715 * value * value * value)
    tanh = jnp.tanh(inner)
    slope = 0.7978845608028654 * (1.0 + 3.0 * 0.044715 * value * value)
    return 0.5 * (1.0 + tanh) + 0.5 * value * (1.0 - tanh * tanh) * slope


class Plan:
    def __init__(self, mesh):
        self.nz = mesh.shape["seq"]
        self.nf = mesh.shape["fsdp"]
        self.nr = mesh.shape["replica"]
        self.group = self.nf * self.nr
        self.cube = self.nf == 4 and self.nr == 2
        self.heads = 2 * -(-HEADS // (2 * self.group))

    def rank_of(self, f, r):
        half = self.group // 2
        if self.nf % 2:
            return f * self.nr + r
        return (f % 2) * half + (f // 2) * self.nr + r

    def rank(self):
        return self.rank_of(lax.axis_index("fsdp"), lax.axis_index("replica"))

    def order(self):
        members = [(self.rank_of(f, r), f * self.nr + r) for f in range(self.nf) for r in range(self.nr)]
        return [member for _, member in sorted(members)]

    def regroup(self, v):
        place = {}
        for f in range(self.nf):
            for r in range(self.nr):
                place[self.rank_of(f, r)] = f * self.nr + r
        pairs = []
        for z in range(self.nz):
            for g in range(self.group):
                slot = (g // self.nz) * self.nz + z
                pairs.append((z * self.group + place[g], (g % self.nz) * self.group + place[slot]))
        return lax.ppermute(v, ALL, pairs)

    def swap_core(self, v):
        return lax.ppermute(v, "fsdp", [(f, f ^ 1) for f in range(self.nf)])

    def swap_y(self, v):
        return lax.ppermute(v, "fsdp", [(f, f ^ 2) for f in range(self.nf)])

    def swap_x(self, v):
        return lax.ppermute(v, "replica", [(r, r ^ 1) for r in range(self.nr)])

    def swap_xy(self, v):
        pairs = [
            (f * self.nr + r, (f ^ 2) * self.nr + (r ^ 1))
            for f in range(self.nf)
            for r in range(self.nr)
        ]
        return lax.ppermute(v, GROUP, pairs)

    def bits(self):
        f = lax.axis_index("fsdp")
        return f % 2, f // 2, lax.axis_index("replica")

    def gather_rows(self, v):
        if not self.cube:
            full = lax.all_gather(v, GROUP, axis=0, tiled=False)
            return full[jnp.array(self.order())].reshape(-1, v.shape[1])
        half = v.shape[0] // 2
        if v.shape[0] % 32:
            from_x = self.swap_x(v)
            four = jnp.concatenate([v, from_x, self.swap_y(jnp.concatenate([v, from_x]))])
        else:
            from_x = self.swap_x(v)
            from_y = self.swap_y(v)
            corner_a = self.swap_y(from_x[:half])
            corner_b = self.swap_x(from_y[half:])
            four = jnp.concatenate([v, from_x, from_y, corner_a, corner_b])
        return jnp.concatenate([four, self.swap_core(four)])

    def scatter_rows(self, v):
        rows = v.shape[0] // self.group
        if not self.cube:
            blocks = v.astype(BF).reshape(self.group, rows, -1)
            back = [0] * self.group
            for rank, member in enumerate(self.order()):
                back[member] = rank
            blocks = blocks[jnp.array(back)].reshape(v.shape)
            return lax.psum_scatter(blocks, GROUP, scatter_dimension=0, tiled=True).astype(F32)
        half = rows // 2
        mine, other = v[: 4 * rows], v[4 * rows :]
        four = mine + self.swap_core(other.astype(BF)).astype(F32)
        own, to_x, to_y, corner = (four[i * rows : (i + 1) * rows] for i in range(4))
        corner = corner.astype(BF)
        add_x = self.swap_y(corner[:half]).astype(F32)
        add_y = self.swap_x(corner[half:]).astype(F32)
        to_x = jnp.concatenate([to_x[:half] + add_x, to_x[half:]]).astype(BF)
        to_y = jnp.concatenate([to_y[:half], to_y[half:] + add_y]).astype(BF)
        return own + self.swap_x(to_x).astype(F32) + self.swap_y(to_y).astype(F32)

    def working_to_rank(self, v, axis):
        if not self.cube:
            return v
        core, y, x = self.bits()
        shape = v.shape
        v = v.reshape(shape[:axis] + (2, 2, 2) + shape[axis + 1 :])
        v = jnp.where(core == 1, jnp.flip(v, axis), v)
        v = jnp.where(y == 1, jnp.flip(v, axis + 1), v)
        v = jnp.where(x == 1, jnp.flip(v, axis + 2), v)
        return v.reshape(shape)

    def exchange(self, v):
        if not self.cube:
            back = [0] * self.group
            for rank, member in enumerate(self.order()):
                back[member] = rank
            v = lax.all_to_all(v[jnp.array(back)], GROUP, split_axis=0, concat_axis=0, tiled=True)
            return v[jnp.array(self.order())]
        near = v[:4]
        far = self.swap_core(v[4:])
        both = jnp.stack([near, far])
        own = both[:, 0]
        from_x = self.swap_x(both[:, 1])
        from_y = self.swap_y(both[:, 2])
        from_xy = self.swap_xy(both[:, 3])
        return jnp.stack([own, from_x, from_y, from_xy], axis=1).reshape(v.shape)

    def exchange_fsdp(self, v):
        if not self.cube:
            return lax.all_to_all(v, "fsdp", split_axis=0, concat_axis=0, tiled=True)
        core, y, _ = self.bits()
        shape = v.shape

        def flips(u):
            u = u.reshape((2, 2) + shape[1:])
            u = jnp.where(y == 1, jnp.flip(u, 0), u)
            u = jnp.where(core == 1, jnp.flip(u, 1), u)
            return u

        v = flips(v)
        other = self.swap_core(v[:, 1])
        both = jnp.stack([v[:, 0], other], axis=1)
        far = self.swap_y(both[1])
        return flips(jnp.stack([both[0], far])).reshape(shape)

    def gather_replica(self, v, axis):
        if self.nr != 2:
            return lax.all_gather(v, "replica", axis=axis, tiled=True)
        x = lax.axis_index("replica")
        other = self.swap_x(v)
        return jnp.concatenate(
            [jnp.where(x == 0, v, other), jnp.where(x == 0, other, v)], axis=axis
        )


def gather_seq(v):
    return lax.all_gather(v, "seq", axis=0, tiled=True)


def scatter_seq(v):
    return lax.psum_scatter(v, "seq", scatter_dimension=0, tiled=True)


def heads_of(v, plan, total):
    return v.reshape(-1, total, plan.heads, HD)


def attend(packed, codes, plan, total, scale):
    width = plan.heads * HD
    q, k, v = (heads_of(packed[:, i * width : (i + 1) * width], plan, total) for i in range(3))
    code = codes.reshape(-1, total)
    low = (code // 65536) * 65536
    allowed = (code[:, None, :] <= code[:, :, None]) & (code[:, None, :] >= low[:, :, None])
    scores = jnp.einsum("sqhd,skhd->shqk", q, k, preferred_element_type=F32) * scale
    scores = jnp.where(allowed[:, None], scores, -1e30)
    top = jnp.max(scores, axis=-1, keepdims=True)
    expo = jnp.exp(scores - top)
    denom = jnp.sum(expo, axis=-1, keepdims=True)
    lse = top + jnp.log(denom)
    probs = (expo / denom).astype(BF)
    mixed = jnp.einsum("shqk,skhd->sqhd", probs, v, preferred_element_type=F32)
    return mixed.reshape(-1, width).astype(BF), lse


def attend_back(packed, codes, lse, g_mixed, plan, total, scale):
    width = plan.heads * HD
    q, k, v = (heads_of(packed[:, i * width : (i + 1) * width], plan, total) for i in range(3))
    gm = heads_of(g_mixed, plan, total)
    code = codes.reshape(-1, total)
    low = (code // 65536) * 65536
    allowed = (code[:, None, :] <= code[:, :, None]) & (code[:, None, :] >= low[:, :, None])
    scores = jnp.einsum("sqhd,skhd->shqk", q, k, preferred_element_type=F32) * scale
    probs = jnp.exp(jnp.where(allowed[:, None], scores, -1e30) - lse)
    g_probs = jnp.einsum("sqhd,skhd->shqk", gm, v, preferred_element_type=F32)
    g_v = jnp.einsum("shqk,sqhd->skhd", probs.astype(BF), gm, preferred_element_type=F32)
    row = jnp.sum(g_probs * probs, axis=-1, keepdims=True)
    g_s = (probs * (g_probs - row)).astype(BF)
    g_q = jnp.einsum("shqk,skhd->sqhd", g_s, k, preferred_element_type=F32) * scale
    g_k = jnp.einsum("shqk,sqhd->skhd", g_s, q, preferred_element_type=F32) * scale
    return jnp.concatenate([u.reshape(-1, width).astype(BF) for u in (g_q, g_k, g_v)], axis=1)


def shards(
    plan,
    tokens,
    cotangent,
    segments,
    norm1_gain,
    norm1_shift,
    w_qkv,
    b_query,
    b_value,
    w_out,
    b_out,
    norm2_gain,
    norm2_shift,
    w_up,
    b_up,
    w_down,
    b_down,
):
    nz, nf, nr, group = plan.nz, plan.nf, plan.nr, plan.group
    layers, own_rows, triple = w_qkv.shape
    width = triple // 3
    own_hidden = w_down.shape[1]
    piece = own_hidden // nr
    length = tokens.shape[1]
    total = length * nz
    hpr = plan.heads
    span = hpr * HD
    scale = 1.0 / math.sqrt(HD)
    fsdp = lax.axis_index("fsdp")
    replica = lax.axis_index("replica")
    seq = lax.axis_index("seq")
    rank = plan.rank()

    def head_columns(v):
        rows = v.shape[0]
        v = v.reshape(rows, 3, width)
        v = jnp.pad(v, ((0, 0), (0, 0), (0, group * span - width)))
        v = v.reshape(rows, 3, group, span)
        ranks = jnp.array([[plan.rank_of(f, r) for f in range(nf)] for r in range(nr)])
        v = jnp.take(v, ranks[replica], axis=2)
        return v.transpose(2, 0, 1, 3).reshape(nf, rows, 3 * span)

    def fetch(layer):
        qkv = plan.exchange_fsdp(head_columns(w_qkv[layer]))
        qkv = gather_seq(qkv.reshape(nf * own_rows, 3 * span))
        half = width // nr
        out = lax.dynamic_slice_in_dim(w_out[layer], replica * half, half, 1)
        out = gather_seq(out)
        up = w_up[layer].reshape(own_rows, nz, nf, nr, piece)
        up = lax.dynamic_index_in_dim(up, replica, 3, keepdims=False)
        up = up.transpose(2, 0, 1, 3).reshape(nf, own_rows, nz * piece)
        up = gather_seq(plan.exchange_fsdp(up).reshape(nf * own_rows, nz * piece))
        down = lax.dynamic_slice_in_dim(w_down[layer], replica * piece, piece, 0)
        down = gather_seq(down)
        out = plan.gather_replica(out, 1)
        out = out.reshape(nz, 1, own_rows, width)
        if plan.cube:
            core, y, _ = plan.bits()
            other = plan.swap_core(out)
            out = jnp.concatenate(
                [jnp.where(core == 0, out, other), jnp.where(core == 0, other, out)], axis=1
            )
            other = plan.swap_y(out)
            out = jnp.concatenate(
                [jnp.where(y == 0, out, other), jnp.where(y == 0, other, out)], axis=1
            )
        else:
            out = lax.all_gather(out, "fsdp", axis=1, tiled=True)
        out = out.reshape(width, width)
        return qkv, out, up, down

    small = jnp.concatenate(
        [norm1_gain, norm1_shift, b_query, b_value, b_out, norm2_gain, norm2_shift, b_down, b_up],
        axis=1,
    )
    small = lax.all_gather(small, OWNERS, axis=0, tiled=False)

    def vectors(layer):
        each = [
            small[:, layer, i * own_rows : (i + 1) * own_rows].reshape(width).astype(F32)
            for i in range(8)
        ]
        bias_up = small[:, layer, 8 * own_rows :].reshape(nz, nf, nr, piece)
        bias_up = lax.dynamic_index_in_dim(bias_up, fsdp, 1, keepdims=False)
        bias_up = lax.dynamic_index_in_dim(bias_up, replica, 1, keepdims=False)

        def mine(v):
            return lax.dynamic_slice_in_dim(
                jnp.pad(v, (0, group * span - width)), rank * span, span
            )

        bias_qkv = jnp.concatenate([mine(each[2]), jnp.zeros((span,), F32), mine(each[3])])
        return each, bias_qkv, bias_up.reshape(nz * piece).astype(F32)

    vecs = [vectors(layer) for layer in range(layers)]
    weights = [fetch(layer) for layer in range(layers)]

    hidden = plan.regroup(tokens[0]).astype(F32)
    codes = segments[0] * 65536 + seq * length + jnp.arange(length, dtype=jnp.int32)
    codes = plan.regroup(codes[None])
    codes = plan.gather_rows(codes)
    grad = plan.regroup(cotangent[0]).astype(F32)

    kept = []
    for layer in range(layers):
        qkv_w, out_w, up_w, down_w = weights[layer]
        (gain1, shift1, _, _, bias_out, gain2, shift2, bias_down), bias_qkv, bias_up = vecs[layer]
        unit1, inv1 = norm_parts(hidden)
        normed = plan.gather_rows((unit1 * gain1 + shift1).astype(BF))
        packed = (dot(normed, qkv_w, 1, 0) + bias_qkv).astype(BF)
        mixed, lse = attend(packed, codes, plan, total, scale)
        mixed = plan.exchange(mixed.reshape(group, length, span))
        mixed = plan.working_to_rank(mixed, 0)
        mixed = mixed.transpose(1, 0, 2).reshape(length, group * span)[:, :width]
        middle = hidden + (dot(mixed, out_w, 1, 0) + bias_out)
        unit2, inv2 = norm_parts(middle)
        normed_two = plan.gather_rows((unit2 * gain2 + shift2).astype(BF))
        lifted = dot(normed_two, up_w, 1, 0) + bias_up
        activated = gelu_tanh(lifted).astype(BF)
        lowered = plan.scatter_rows(dot(activated, down_w, 1, 0))
        kept.append(
            (unit1, inv1, normed, packed, lse, mixed, unit2, inv2, normed_two, lifted, activated)
        )
        hidden = middle + (lowered + bias_down)
    output = plan.regroup(hidden)

    def own_piece_columns(v):
        rows = v.shape[1]
        v = plan.gather_replica(v[..., None, :], 2)
        v = v.reshape(nf, rows, nr, nz, piece).transpose(1, 3, 0, 2, 4)
        return v.reshape(rows, nz * nf * nr * piece)

    results = [None] * layers
    smalls = [None] * layers
    for layer in reversed(range(layers)):
        qkv_w, out_w, up_w, down_w = weights[layer]
        (gain1, _, _, _, _, gain2, _, _), _, _ = vecs[layer]
        unit1, inv1, normed, packed, lse, mixed, unit2, inv2, normed_two, lifted, activated = kept[
            layer
        ]
        g_low = grad.astype(BF)
        g_full = plan.gather_rows(g_low)
        g_act = dot(g_full, down_w, 1, 1)
        g_lift32 = gelu_slope(lifted) * g_act
        g_lift = g_lift32.astype(BF)
        grad_down = dot(activated, g_full, 0, 0).astype(BF)
        grad_up = dot(normed_two, g_lift, 0, 0).astype(BF)
        g_n2 = plan.scatter_rows(dot(g_lift, up_w, 1, 1))
        grad_b_up = jnp.sum(g_lift.astype(F32), axis=0)
        g_mid = grad + norm_pull(g_n2, unit2, inv2, gain2)
        g_att = g_mid.astype(BF)
        g_mixed = dot(g_att, out_w, 1, 1).astype(BF)
        grad_out = dot(mixed, g_att, 0, 0)
        g_mixed = jnp.pad(g_mixed, ((0, 0), (0, group * span - width)))
        g_mixed = g_mixed.reshape(length, group, span).transpose(1, 0, 2)
        g_mixed = plan.exchange(plan.working_to_rank(g_mixed, 0))
        g_packed = attend_back(
            packed, codes, lse, g_mixed.reshape(group * length, span), plan, total, scale
        )
        grad_qkv = dot(normed, g_packed, 0, 0).astype(BF)
        g_n1 = plan.scatter_rows(dot(g_packed, qkv_w, 1, 1))
        g_b = jnp.sum(g_packed.astype(F32), axis=0)
        vector_grads = (
            jnp.sum(g_n1 * unit1, axis=0),
            jnp.sum(g_n1, axis=0),
            g_b,
            jnp.sum(g_att.astype(F32), axis=0),
            jnp.sum(g_n2 * unit2, axis=0),
            jnp.sum(g_n2, axis=0),
            jnp.sum(g_low.astype(F32), axis=0),
            grad_b_up,
        )
        grad = g_mid + norm_pull(g_n1, unit1, inv1, gain1)

        down = scatter_seq(grad_down)
        up = scatter_seq(grad_up)
        rows4 = grad_out.reshape(nz, nf, own_rows, width)
        if plan.cube:
            core, y, x = plan.bits()
            rows4 = rows4.reshape(nz, 2, 2, own_rows, width)

            def halve(v, bit, axis, swap):
                a = lax.index_in_dim(v, 0, axis, keepdims=False)
                b = lax.index_in_dim(v, 1, axis, keepdims=False)
                keep = jnp.where(bit == 0, a, b)
                send = jnp.where(bit == 0, b, a)
                return keep + swap(send.astype(BF)).astype(F32)

            rows4 = halve(rows4, core, 2, plan.swap_core)
            rows4 = halve(rows4, y, 1, plan.swap_y)
            rows4 = rows4.reshape(nz, own_rows, 2, width // 2)
            rows4 = halve(rows4, x, 2, plan.swap_x)
            outs = rows4.reshape(nz * own_rows, width // nr).astype(BF)
        else:
            outs = lax.psum_scatter(
                rows4.astype(BF), "fsdp", scatter_dimension=1, tiled=False
            ).reshape(nz * own_rows, width)
            outs = lax.psum_scatter(outs, "replica", scatter_dimension=1, tiled=True)
        part = width // (4 * nr)
        outs = outs.reshape(nz, own_rows, 4, part).transpose(0, 2, 1, 3)
        outs = scatter_seq(outs.reshape(nz * 4 * own_rows, part))
        outs = outs.reshape(4, own_rows, part).transpose(1, 0, 2).reshape(own_rows, 4 * part)
        qkv = scatter_seq(grad_qkv)

        down = plan.gather_replica(down, 0).astype(F32)
        up = own_piece_columns(plan.exchange_fsdp(up.reshape(nf, own_rows, nz * piece)))
        outs = plan.gather_replica(outs, 1).astype(F32)
        qkv = plan.exchange_fsdp(qkv.reshape(nf, own_rows, 3 * span))
        qkv = plan.gather_replica(qkv[..., None, :], 2)
        qkv = qkv.reshape(nf, own_rows, nr, 3, span)
        where = [None] * group
        for f in range(nf):
            for r in range(nr):
                where[plan.rank_of(f, r)] = qkv[f, :, r]
        qkv = jnp.concatenate(where, axis=2)[:, :, :width].reshape(own_rows, triple)
        results[layer] = (qkv.astype(F32), outs, up.astype(F32), down)
        smalls[layer] = vector_grads
    grad_tokens = plan.regroup(grad)

    def scattered(layer):
        n1g, n1s, g_b, b_o, n2g, n2s, b_d, b_u = smalls[layer]

        def place(v):
            full = lax.dynamic_update_slice_in_dim(
                jnp.zeros((group * span,), F32), v, rank * span, 0
            )
            return full[:width]

        b_u = lax.dynamic_update_slice(
            jnp.zeros((nz, nf, nr, piece), F32),
            b_u.reshape(nz, 1, 1, piece),
            (0, fsdp, replica, 0),
        )
        rows = [n1g, n1s, place(g_b[:span]), place(g_b[2 * span :]), b_o, n2g, n2s, b_d]
        return jnp.concatenate(
            [v.reshape(nz * nf, own_rows) for v in rows] + [b_u.reshape(nz * nf, own_hidden)],
            axis=1,
        )

    flat = jnp.concatenate([scattered(layer) for layer in range(layers)], axis=1)
    flat = lax.psum_scatter(flat, OWNERS, scatter_dimension=0, tiled=True)
    flat = lax.psum(flat, "replica").reshape(layers, -1)
    vec = [flat[:, i * own_rows : (i + 1) * own_rows] for i in range(8)]
    grad_b_up = flat[:, 8 * own_rows :]
    mats = [jnp.stack([results[layer][i] for layer in range(layers)]) for i in range(4)]
    return (
        output[None],
        grad_tokens[None],
        vec[0],
        vec[1],
        mats[0],
        vec[2],
        vec[3],
        mats[1],
        vec[4],
        vec[5],
        vec[6],
        mats[2],
        grad_b_up,
        mats[3],
        vec[7],
    )


def solution(mesh):
    plan = Plan(mesh)
    data = P(("fsdp", "replica"), "seq", None)
    vector = P(None, ("seq", "fsdp"))
    matrix = P(None, ("seq", "fsdp"), None)
    weights = (
        vector,
        vector,
        matrix,
        vector,
        vector,
        matrix,
        vector,
        vector,
        vector,
        matrix,
        vector,
        matrix,
        vector,
    )
    in_specs = (data, data, P(("fsdp", "replica"), "seq")) + weights
    out_specs = (data, data) + weights
    return jax.shard_map(
        functools.partial(shards, plan),
        mesh=mesh,
        in_specs=in_specs,
        out_specs=out_specs,
        check_vma=False,
    )
```

```python
import functools
import math

import jax
import jax.numpy as jnp
from jax import lax
from jax.experimental import pallas as pl
from jax.experimental.pallas import tpu as pltpu
from jax.sharding import PartitionSpec as P


HEADS = 25
HD = 64
BF = jnp.bfloat16
F32 = jnp.float32
ALL = ("seq", "fsdp", "replica")
GROUP = ("fsdp", "replica")
OWNERS = ("seq", "fsdp")
CODE = 65536
LOW = -1e30


def dot(a, b, ca=1, cb=0):
    return lax.dot_general(a, b, (((ca,), (cb,)), ((), ())), preferred_element_type=F32)


def norm_parts(v):
    mean = jnp.mean(v, axis=-1, keepdims=True)
    centred = v - mean
    spread = jnp.mean(centred * centred, axis=-1, keepdims=True)
    inv = lax.rsqrt(spread + 1e-05)
    return centred * inv, inv


def norm_pull(grad, unit, inv, gain):
    scaled = grad * gain
    first = jnp.mean(scaled, axis=-1, keepdims=True)
    second = jnp.mean(scaled * unit, axis=-1, keepdims=True)
    return inv * (scaled - first - unit * second)


def gelu_both(value):
    tanh = jnp.tanh(0.7978845608028654 * (value + 0.044715 * value * value * value))
    inner = 0.7978845608028654 * (1.0 + 3.0 * 0.044715 * value * value)
    half = 0.5 * (1.0 + tanh)
    return value * half, half + 0.5 * value * (1.0 - tanh * tanh) * inner


class Plan:
    def __init__(self, mesh):
        self.nz = mesh.shape["seq"]
        self.nf = mesh.shape["fsdp"]
        self.nr = mesh.shape["replica"]
        self.group = self.nf * self.nr
        self.cube = self.nf == 4 and self.nr == 2
        self.heads = 2 * -(-HEADS // (2 * self.group))
        self.span = self.heads * HD
        order = sorted(
            (self.rank_of(f, r), f * self.nr + r) for f in range(self.nf) for r in range(self.nr)
        )
        self.place = [member for _, member in order]
        self.back = [0] * self.group
        for rank, member in order:
            self.back[member] = rank

    def rank_of(self, f, r):
        half = self.group // 2
        if self.nf % 2:
            return f * self.nr + r
        return (f % 2) * half + (f // 2) * self.nr + r

    def rank(self):
        return self.rank_of(lax.axis_index("fsdp"), lax.axis_index("replica"))

    def regroup(self, v, back=False):
        nz = self.nz
        pairs = []
        for z in range(nz):
            for g in range(self.group):
                goal = g % nz
                slot = (g // nz) * nz + (z ^ goal if nz & (nz - 1) == 0 else z)
                pairs.append((z * self.group + self.place[g], goal * self.group + self.place[slot]))
        if back:
            pairs = [(there, here) for here, there in pairs]
        return lax.ppermute(v, ALL, pairs)

    def swap_core(self, v):
        return lax.ppermute(v, "fsdp", [(f, f ^ 1) for f in range(self.nf)])

    def swap_y(self, v):
        return lax.ppermute(v, "fsdp", [(f, f ^ 2) for f in range(self.nf)])

    def swap_x(self, v):
        return lax.ppermute(v, "replica", [(r, r ^ 1) for r in range(self.nr)])

    def swap_xy(self, v):
        pairs = [
            (f * self.nr + r, (f ^ 2) * self.nr + (r ^ 1))
            for f in range(self.nf)
            for r in range(self.nr)
        ]
        return lax.ppermute(v, GROUP, pairs)

    def source(self):
        base = jnp.arange(self.group, dtype=jnp.int32)
        return base ^ self.rank() if self.cube else base

    def gather_pieces(self, v):
        if not self.cube:
            full = lax.all_gather(v, GROUP, axis=0, tiled=False)
            return [full[member] for member in self.place]
        near = [v, self.swap_x(v), self.swap_y(v), self.swap_xy(v)]
        return near + [self.swap_core(piece) for piece in near]

    def gather_doubling(self, v):
        if not self.cube:
            return jnp.concatenate(self.gather_pieces(v))
        for swap in (self.swap_x, self.swap_y, self.swap_core):
            v = jnp.concatenate([v, swap(v)])
        return v

    def scatter_parts(self, near, far):
        if not self.cube:
            blocks = jnp.concatenate([near.astype(BF), far])
            rows = blocks.shape[0] // self.group
            blocks = blocks.reshape(self.group, rows, -1)[jnp.array(self.back)]
            blocks = blocks.reshape(self.group * rows, -1)
            return lax.psum_scatter(blocks, GROUP, scatter_dimension=0, tiled=True).astype(F32)
        rows, columns = near.shape[0] // 4, near.shape[1]
        own, to_x, to_y, to_xy = call(
            fold_kernel,
            [sds((rows, columns), F32)] + [sds((rows, lanes(columns)), BF)] * 3,
            [],
            0,
            [near, self.swap_core(far)],
        )
        parts = self.swap_xy(to_xy), self.swap_x(to_x), self.swap_y(to_y)
        parts = [part[:, :columns].astype(F32) for part in parts]
        return own + parts[0] + parts[1] + parts[2]

    def exchange(self, v):
        if not self.cube:
            v = v.reshape(self.group, -1, v.shape[1])[jnp.array(self.back)]
            v = lax.all_to_all(v, GROUP, split_axis=0, concat_axis=0, tiled=True)
            return [v[member] for member in self.place]
        rows = v.shape[0] // 8
        half = 4 * rows
        far = self.swap_core(v[half:])
        out = [[v[:rows], far[:rows]]]
        for i, swap in ((1, self.swap_x), (2, self.swap_y), (3, self.swap_xy)):
            both = swap(
                jnp.concatenate([v[i * rows : (i + 1) * rows], far[i * rows : (i + 1) * rows]])
            )
            out.append([both[:rows], both[rows:]])
        return [pair[0] for pair in out] + [pair[1] for pair in out]

    def flips(self, v):
        f = lax.axis_index("fsdp")
        v = v.reshape((2, 2) + v.shape[1:])
        v = jnp.where(f // 2 == 1, jnp.flip(v, 0), v)
        return jnp.where(f % 2 == 1, jnp.flip(v, 1), v)

    def gather_owners(self, v):
        if not self.cube or self.nz != 4:
            return lax.all_gather(v, OWNERS, axis=0, tiled=False)
        z, f = lax.axis_index("seq"), lax.axis_index("fsdp")
        far = [
            lax.ppermute(v, "seq", [(i, i ^ d) for i in range(4)]) if d else v for d in range(4)
        ]
        v = jnp.stack(far).reshape((2, 2) + v.shape)
        v = jnp.where(z // 2 == 1, jnp.flip(v, 0), v)
        v = jnp.where(z % 2 == 1, jnp.flip(v, 1), v)
        other = self.swap_core(v)
        v = jnp.stack([jnp.where(f % 2 == 0, v, other), jnp.where(f % 2 == 0, other, v)], axis=2)
        other = self.swap_y(v)
        v = jnp.stack([jnp.where(f // 2 == 0, v, other), jnp.where(f // 2 == 0, other, v)], axis=2)
        return v.reshape((16,) + v.shape[4:])

    def exchange_fsdp(self, v):
        if not self.cube:
            return lax.all_to_all(v, "fsdp", split_axis=0, concat_axis=0, tiled=True)
        shape = v.shape
        v = self.flips(v)
        both = jnp.stack([v[:, 0], self.swap_core(v[:, 1])], axis=1)
        return self.flips(jnp.stack([both[0], self.swap_y(both[1])]).reshape(shape)).reshape(shape)

    def scatter_small(self, v):
        if not self.cube or self.nz != 4:
            return lax.psum_scatter(v, "seq", scatter_dimension=0, tiled=False)
        z = lax.axis_index("seq")
        total = lax.dynamic_index_in_dim(v, z, 0, keepdims=False)
        for d in range(1, 4):
            other = lax.dynamic_index_in_dim(v, z ^ d, 0, keepdims=False)
            total = total + lax.ppermute(other, "seq", [(i, i ^ d) for i in range(4)])
        return total

    def to_owners_small(self, v):
        if not self.cube:
            v = lax.all_to_all(v, "fsdp", split_axis=0, concat_axis=0, tiled=True)
            v = lax.all_gather(v, "replica", axis=1, tiled=False)
            return jnp.stack([v[m // self.nr, m % self.nr] for m in self.place])
        v = self.flips(v)
        far = self.swap_core(v[:, 1])
        here = jnp.stack([v[0, 0], far[0]])
        there = jnp.stack([v[1, 0], far[1]])
        return jnp.stack(
            [here, self.swap_x(here), self.swap_y(there), self.swap_xy(there)], axis=1
        ).reshape((8,) + v.shape[2:])

    def to_owners(self, v):
        if not self.cube:
            return self.to_owners_small(v)
        nf, rows, columns = v.shape
        f = lax.axis_index("fsdp")
        pick = (f ^ jnp.arange(nf, dtype=jnp.int32)).astype(jnp.int32)
        pair = sds((2, rows, columns), BF)
        near, far = pl.pallas_call(
            pick_kernel,
            grid_spec=pltpu.PrefetchScalarGridSpec(
                num_scalar_prefetch=1,
                grid=(1,),
                in_specs=[pl.BlockSpec(v.shape, lambda i, s: (0, 0, 0))],
                out_specs=[pl.BlockSpec(pair.shape, lambda i, s: (0, 0, 0))] * 2,
            ),
            out_shape=[pair] * 2,
            compiler_params=pltpu.CompilerParams(vmem_limit_bytes=44 * 1024 * 1024),
        )(pick, v)
        here, there = call(pair_kernel, [pair] * 2, [], 0, [near, self.swap_core(far)])
        return [here, self.swap_x(here), self.swap_y(there), self.swap_xy(there)]


def pick_kernel(order, v, near, far):
    for y in range(2):
        near[y] = v[order[2 * y]]
        far[y] = v[order[2 * y + 1]]


def pair_kernel(near, far, here, there):
    for y, out in enumerate((here, there)):
        out[0] = near[y]
        out[1] = far[y]


def gather_seq(v, lead=False):
    if lead:
        return lax.all_gather(v[None], "seq", axis=1, tiled=True)[0]
    return lax.all_gather(v, "seq", axis=0, tiled=True)


def scatter_seq(v, lead=False):
    if lead:
        return lax.psum_scatter(v[None], "seq", scatter_dimension=1, tiled=True)[0]
    return lax.psum_scatter(v, "seq", scatter_dimension=0, tiled=True)


def call(kernel, outs, scratch, flops, operands, **more):
    params = pltpu.CompilerParams(vmem_limit_bytes=44 * 1024 * 1024)
    size = sum(math.prod(o.shape) * o.dtype.itemsize for o in list(outs) + list(operands))
    return pl.pallas_call(
        kernel,
        out_shape=tuple(outs),
        scratch_shapes=scratch,
        compiler_params=params,
        cost_estimate=pl.CostEstimate(
            flops=int(flops), bytes_accessed=int(size), transcendentals=0
        ),
        **more,
    )(*operands)


def lanes(columns):
    return -(-columns // 128) * 128


def widen(v):
    return jnp.pad(v, ((0, 0), (0, lanes(v.shape[1]) - v.shape[1])))


def sds(shape, dtype):
    return jax.ShapeDtypeStruct(shape, dtype)


def fold_kernel(near, far, own, to_x, to_y, to_xy):
    rows, columns = own.shape
    own[...] = near[:rows, :] + far[:rows, :columns].astype(F32)
    for i, out in ((1, to_x), (2, to_y), (3, to_xy)):
        at = slice(i * rows, (i + 1) * rows)
        out[:, :columns] = (near[at, :] + far[at, :columns].astype(F32)).astype(BF)


def wgrad_kernel(left, right, out):
    tall = out.shape[0]
    block = 256

    def body(i, carry):
        at = pl.ds(pl.multiple_of(i * block, block), block)
        out[at, :] = dot(left[:, at], right[...], 0, 0).astype(BF)
        return carry

    whole = tall // block
    lax.fori_loop(0, whole, body, 0)
    if tall % block:
        out[whole * block :, :] = dot(left[:, whole * block :], right[...], 0, 0).astype(BF)


def wgrad(plan, left, right):
    if not plan.cube:
        return dot(left, right, 0, 0).astype(BF)
    tall, width = left.shape[1], right.shape[1]
    return call(
        wgrad_kernel, [sds((tall, width), BF)], [], 2 * left.size * width, [left, right]
    )[0]


def after(v, other):
    return lax.optimization_barrier((v, other))[0]


def first_half(shape):
    return lax.broadcasted_iota(jnp.int32, shape, 1) < HD


def attend_kernel(count, total, span, scale, *refs):
    pieces = refs[:count]
    w, bias, code_col, code_row, full, packed, lse, mixed = refs[count:]
    rows = pieces[0].shape[0]
    for i, piece in enumerate(pieces):
        full[i * rows : (i + 1) * rows, :] = piece[:, : full.shape[1]]
    block = 2 * rows

    def project(i, carry):
        at = pl.ds(pl.multiple_of(i * block, block), block)
        packed[at, :] = (dot(full[at, :], w[...]) + bias[...]).astype(BF)
        return carry

    lax.fori_loop(0, count // 2, project, 0)
    blocks = total // rows
    left = first_half((rows, 2 * HD))
    lane = lax.broadcasted_iota(jnp.int32, (rows, 128), 1)

    def queries(i, carry):
        at = pl.ds(pl.multiple_of(i * rows, rows), rows)
        seq = i // blocks
        keys_at = pl.ds(pl.multiple_of(seq * total, total), total)
        code_q = code_col[at, :]
        code_k = code_row[pl.ds(seq, 1), :]
        allowed = (code_k <= code_q) & (code_k >= (code_q // CODE) * CODE)
        stats = jnp.zeros((rows, 128), F32)
        for pair in range(span // 128):
            q = packed[at, pair * 128 : pair * 128 + 128]
            k = packed[keys_at, span + pair * 128 : span + pair * 128 + 128]
            v = packed[keys_at, 2 * span + pair * 128 : 2 * span + pair * 128 + 128]
            both = []
            for side in range(2):
                own = left if side == 0 else ~left
                scores = dot(jnp.where(own, q, jnp.zeros_like(q)), k, 1, 1) * scale
                scores = jnp.where(allowed, scores, LOW)
                top = jnp.max(scores, axis=1, keepdims=True)
                expo = jnp.exp(scores - top)
                denom = jnp.sum(expo, axis=1, keepdims=True)
                probs = (expo * (1.0 / denom)).astype(BF)
                both.append(dot(probs, v))
                stats = jnp.where(lane == 2 * pair + side, top + jnp.log(denom), stats)
            mixed[at, pair * 128 : pair * 128 + 128] = jnp.where(left, both[0], both[1]).astype(BF)
        lse[:, at] = stats.T[: lse.shape[0], :]
        return carry

    lax.fori_loop(0, count, queries, 0)


def attend(plan, pieces, w, bias, codes, total, scale):
    rows, width = pieces[0].shape[0], w.shape[0]
    count, span = plan.group, plan.span
    if not plan.cube:
        full = jnp.concatenate(pieces)[:, :width]
        packed = (dot(full, w) + bias).astype(BF)
        q, k, v = (
            packed[:, i * span : (i + 1) * span].reshape(-1, total, plan.heads, HD)
            for i in range(3)
        )
        allowed = mask_of(codes, total)
        scores = jnp.einsum("sqhd,skhd->shqk", q, k, preferred_element_type=F32) * scale
        scores = jnp.where(allowed[:, None], scores, LOW)
        top = jnp.max(scores, axis=-1, keepdims=True)
        expo = jnp.exp(scores - top)
        denom = jnp.sum(expo, axis=-1, keepdims=True)
        probs = (expo / denom).astype(BF)
        mixed = jnp.einsum("shqk,skhd->sqhd", probs, v, preferred_element_type=F32)
        return full, packed, top + jnp.log(denom), mixed.reshape(-1, span).astype(BF)
    tall = count * rows
    return call(
        functools.partial(attend_kernel, count, total, span, scale),
        [
            sds((tall, width), BF),
            sds((tall, 3 * span), BF),
            sds((8, tall), F32),
            sds((tall, span), BF),
        ],
        [],
        2 * tall * width * 3 * span + 8 * tall * total * span,
        [*pieces, w, bias[None], codes.reshape(-1, 1), codes.reshape(-1, total)],
    )


def mask_of(codes, total):
    code = codes.reshape(-1, total)
    low = (code // CODE) * CODE
    return (code[:, None, :] <= code[:, :, None]) & (code[:, None, :] >= low[:, :, None])


def attend_back_kernel(count, total, span, scale, *refs):
    pieces = refs[:count]
    packed, lse, code_col, code_row, w, g_packed, g_bias, near, far, gm, g_k, g_v = refs[count:]
    rows = pieces[0].shape[0]
    for i, piece in enumerate(pieces):
        gm[i * rows : (i + 1) * rows, :] = piece[...]
    blocks = total // rows
    left = first_half((rows, 2 * HD))

    def sequence(seq, carry):
        keys_at = pl.ds(pl.multiple_of(seq * total, total), total)
        code_k = code_col[keys_at, :]
        for pair in range(span // 128):
            lanes = slice(pair * 128, pair * 128 + 128)
            k_lanes = slice(span + pair * 128, span + pair * 128 + 128)
            v_lanes = slice(2 * span + pair * 128, 2 * span + pair * 128 + 128)
            k = packed[keys_at, k_lanes]
            v = packed[keys_at, v_lanes]
            g_k[...] = jnp.zeros_like(g_k)
            g_v[...] = jnp.zeros_like(g_v)

            def queries(i, inner):
                at = pl.ds(pl.multiple_of(seq * total + i * rows, rows), rows)
                code_q = code_row[pl.ds(seq * blocks + i, 1), :]
                allowed = (code_k <= code_q) & (code_k >= (code_q // CODE) * CODE)
                q = packed[at, lanes]
                g = gm[at, lanes]
                both = []
                for side in range(2):
                    own = left if side == 0 else ~left
                    q_own = jnp.where(own, q, jnp.zeros_like(q))
                    g_own = jnp.where(own, g, jnp.zeros_like(g))
                    scores = dot(k, q_own, 1, 1) * scale
                    row = 2 * pair + side
                    probs = jnp.exp(jnp.where(allowed, scores, LOW) - lse[row : row + 1, at])
                    g_probs = dot(v, g_own, 1, 1)
                    each = jnp.sum(g_probs * probs, axis=0, keepdims=True)
                    g_scores = (probs * (g_probs - each)).astype(BF)
                    g_v[...] += dot(probs.astype(BF), g_own)
                    g_k[...] += dot(g_scores, q_own)
                    both.append(dot(g_scores, k, 0, 0))
                g_packed[at, lanes] = (jnp.where(left, both[0], both[1]) * scale).astype(BF)
                return inner

            lax.fori_loop(0, blocks, queries, 0)
            g_packed[keys_at, k_lanes] = (g_k[...] * scale).astype(BF)
            g_packed[keys_at, v_lanes] = g_v[...].astype(BF)
        return carry

    lax.fori_loop(0, count // blocks, sequence, 0)
    g_bias[...] = jnp.sum(g_packed[...].astype(F32), axis=0, keepdims=True)
    spread_out(g_packed, w, near, far, 2 * rows)


def spread_out(left, right, near, far, block):
    half = near.shape[0]

    def first(i, carry):
        at = pl.ds(pl.multiple_of(i * block, block), block)
        near[at, :] = dot(left[at, :], right[...], 1, 1)
        return carry

    def second(i, carry):
        at = pl.ds(pl.multiple_of(i * block, block), block)
        far[at, : near.shape[1]] = dot(
            left[pl.ds(pl.multiple_of(half + i * block, block), block), :], right[...], 1, 1
        ).astype(BF)
        return carry

    lax.fori_loop(0, half // block, first, 0)
    lax.fori_loop(0, half // block, second, 0)


def halves(v):
    half = v.shape[0] // 2
    return v[:half], v[half:].astype(BF)


def attend_back(plan, pieces, packed, lse, codes, w, total, scale):
    count, span = plan.group, plan.span
    rows = pieces[0].shape[0]
    width = w.shape[0]
    if not plan.cube:
        q, k, v = (
            packed[:, i * span : (i + 1) * span].reshape(-1, total, plan.heads, HD)
            for i in range(3)
        )
        gm = jnp.concatenate(pieces).reshape(-1, total, plan.heads, HD)
        allowed = mask_of(codes, total)
        scores = jnp.einsum("sqhd,skhd->shqk", q, k, preferred_element_type=F32) * scale
        probs = jnp.exp(jnp.where(allowed[:, None], scores, LOW) - lse)
        g_probs = jnp.einsum("sqhd,skhd->shqk", gm, v, preferred_element_type=F32)
        g_v = jnp.einsum("shqk,sqhd->skhd", probs.astype(BF), gm, preferred_element_type=F32)
        row = jnp.sum(g_probs * probs, axis=-1, keepdims=True)
        g_s = (probs * (g_probs - row)).astype(BF)
        g_q = jnp.einsum("shqk,skhd->sqhd", g_s, k, preferred_element_type=F32) * scale
        g_k = jnp.einsum("shqk,sqhd->skhd", g_s, q, preferred_element_type=F32) * scale
        g_packed = jnp.concatenate(
            [u.reshape(-1, span).astype(BF) for u in (g_q, g_k, g_v)], axis=1
        )
        near, far = halves(dot(g_packed, w, 1, 1))
        return g_packed, jnp.sum(g_packed.astype(F32), axis=0), near, far
    tall = count * rows
    g_packed, g_bias, near, far = call(
        functools.partial(attend_back_kernel, count, total, span, scale),
        [
            sds((tall, 3 * span), BF),
            sds((1, 3 * span), F32),
            sds((tall // 2, width), F32),
            sds((tall // 2, lanes(width)), BF),
        ],
        [pltpu.VMEM((tall, span), BF)] + [pltpu.VMEM((total, 128), F32)] * 2,
        2 * tall * width * 3 * span + 20 * tall * total * span,
        [*pieces, packed, lse, codes.reshape(-1, 1), codes.reshape(-1, rows), w],
    )
    return g_packed, g_bias[0], near, far


def hidden_kernel(count, *refs):
    pieces = refs[:count]
    up, bias, down, full, slope, activated, near, far = refs[count:]
    rows = pieces[0].shape[0]
    for i, piece in enumerate(pieces):
        full[i * rows : (i + 1) * rows, :] = piece[:, : full.shape[1]]
    block = 2 * rows
    half = near.shape[0]

    def lift(at):
        value, pull = gelu_both(dot(full[at, :], up[...]) + bias[...])
        value = value.astype(BF)
        activated[at, :] = value
        slope[at, :] = pull.astype(BF)
        return dot(value, down[...])

    def first(i, carry):
        at = pl.ds(pl.multiple_of(i * block, block), block)
        near[at, :] = lift(at)
        return carry

    def second(i, carry):
        at = pl.ds(pl.multiple_of(i * block, block), block)
        out = lift(pl.ds(pl.multiple_of(half + i * block, block), block))
        far[at, : near.shape[1]] = out.astype(BF)
        return carry

    lax.fori_loop(0, half // block, first, 0)
    lax.fori_loop(0, half // block, second, 0)


def hidden_units(plan, pieces, up, bias, down):
    rows, width = pieces[0].shape[0], up.shape[0]
    if not plan.cube:
        full = jnp.concatenate(pieces)[:, :width]
        value, pull = gelu_both(dot(full, up) + bias)
        value = value.astype(BF)
        return (full, pull.astype(BF), value) + halves(dot(value, down))
    tall, units = plan.group * rows, up.shape[1]
    return call(
        functools.partial(hidden_kernel, plan.group),
        [
            sds((tall, width), BF),
            sds((tall, units), BF),
            sds((tall, units), BF),
            sds((tall // 2, width), F32),
            sds((tall // 2, lanes(width)), BF),
        ],
        [],
        4 * tall * width * units,
        [*pieces, up, bias[None], down],
    )


def hidden_back_kernel(count, *refs):
    pieces = refs[:count]
    slope, down, up, g_lift, g_bias, near, far, full = refs[count:]
    rows = pieces[0].shape[0]
    for i, piece in enumerate(pieces):
        full[i * rows : (i + 1) * rows, :] = piece[:, : full.shape[1]]
    block = 2 * rows

    def pull(i, carry):
        at = pl.ds(pl.multiple_of(i * block, block), block)
        g_lift[at, :] = (dot(full[at, :], down[...], 1, 1) * slope[at, :].astype(F32)).astype(BF)
        return carry

    lax.fori_loop(0, count // 2, pull, 0)
    spread_out(g_lift, up, near, far, block)
    g_bias[...] = jnp.sum(g_lift[...].astype(F32), axis=0, keepdims=True)


def hidden_back(plan, pieces, slope, down, up):
    rows, width = pieces[0].shape[0], up.shape[0]
    if not plan.cube:
        full = jnp.concatenate(pieces)[:, :width]
        g_lift = (dot(full, down, 1, 1) * slope.astype(F32)).astype(BF)
        return (g_lift, jnp.sum(g_lift.astype(F32), axis=0)) + halves(dot(g_lift, up, 1, 1))
    tall, units = plan.group * rows, up.shape[1]
    g_lift, g_bias, near, far = call(
        functools.partial(hidden_back_kernel, plan.group),
        [
            sds((tall, units), BF),
            sds((1, units), F32),
            sds((tall // 2, width), F32),
            sds((tall // 2, lanes(width)), BF),
        ],
        [pltpu.VMEM((tall, width), BF)],
        4 * tall * width * units,
        [*pieces, slope, down, up],
    )
    return g_lift, g_bias[0], near, far


def down_grad_kernel(count, *refs):
    left, out, full = refs[count:]
    rows = refs[0].shape[0]
    for i, piece in enumerate(refs[:count]):
        full[i * rows : (i + 1) * rows, :] = piece[:, : full.shape[1]]
    wgrad_kernel(left, full, out)


def down_grad(plan, left, pieces, width):
    if not plan.cube:
        return dot(left, jnp.concatenate(pieces)[:, :width], 0, 0).astype(BF)
    tall, units = left.shape
    return call(
        functools.partial(down_grad_kernel, plan.group),
        [sds((units, width), BF)],
        [pltpu.VMEM((tall, width), BF)],
        2 * left.size * width,
        [*pieces, left],
    )[0]


def head_columns_kernel(nf, ranks, span, x_ref, w_ref, out, wide):
    width = w_ref.shape[2] // 3
    padded = wide.shape[1] // 3
    w = w_ref[0].astype(F32)
    for i in range(3):
        wide[:, i * padded : i * padded + width] = w[:, i * width : (i + 1) * width]
        if padded > width:
            wide[:, i * padded + width : (i + 1) * padded] = jnp.zeros(
                (wide.shape[0], padded - width), F32
            )
    for x, row in enumerate(ranks):

        @pl.when(x_ref[0] == x)
        def _():
            for f in range(nf):
                for i in range(3):
                    start = i * padded + row[f] * span
                    out[0, f, :, i * span : (i + 1) * span] = wide[:, start : start + span].astype(
                        BF
                    )


def unit_columns_kernel(nz, nf, nr, piece, piece_rows, x_ref, w_ref, out):
    w = w_ref[0].astype(F32)
    for x in range(nr):

        @pl.when(x_ref[0] == x)
        def _():
            for f in range(nf):
                part = []
                for z in range(nz):
                    start = ((z * nf + f) * nr + x) * piece
                    part.append(w[:, start : start + piece])
                    if piece_rows > piece:
                        part.append(jnp.zeros((w.shape[0], piece_rows - piece), F32))
                out[0, f] = jnp.concatenate(part, axis=1).astype(BF)


def layered(kernel, x, w, columns, nf, scratch):
    layers, rows, full = w.shape
    return pl.pallas_call(
        kernel,
        grid_spec=pltpu.PrefetchScalarGridSpec(
            num_scalar_prefetch=1,
            grid=(layers,),
            in_specs=[pl.BlockSpec((1, rows, full), lambda i, s: (i, 0, 0))],
            out_specs=pl.BlockSpec((1, nf, rows, columns), lambda i, s: (i, 0, 0, 0)),
            scratch_shapes=scratch,
        ),
        out_shape=sds((layers, nf, rows, columns), BF),
        compiler_params=pltpu.CompilerParams(vmem_limit_bytes=44 * 1024 * 1024),
        cost_estimate=pl.CostEstimate(flops=0, bytes_accessed=4 * w.size, transcendentals=0),
    )(x, w)


def head_columns(plan, w):
    layers, rows, triple = w.shape
    nf, nr, span, group = plan.nf, plan.nr, plan.span, plan.group
    ranks = [[plan.rank_of(f, r) for f in range(nf)] for r in range(nr)]
    x = lax.axis_index("replica")
    if not plan.cube:
        width = triple // 3
        v = w.reshape(layers, rows, 3, width)
        v = jnp.pad(v, ((0, 0), (0, 0), (0, 0), (0, group * span - width)))
        v = jnp.take(v.reshape(layers, rows, 3, group, span), jnp.array(ranks)[x], axis=3)
        return v.transpose(0, 3, 1, 2, 4).reshape(layers, nf, rows, 3 * span)
    return layered(
        functools.partial(head_columns_kernel, nf, ranks, span),
        x.astype(jnp.int32).reshape(1),
        w,
        3 * span,
        nf,
        [pltpu.VMEM((rows, 3 * group * span), F32)],
    )


def unit_columns(plan, w, piece, piece_rows):
    layers, rows, _ = w.shape
    nz, nf, nr = plan.nz, plan.nf, plan.nr
    x = lax.axis_index("replica")
    if not plan.cube:
        v = w.reshape(layers, rows, nz, nf, nr, piece)
        v = lax.dynamic_index_in_dim(v, x, 4, keepdims=False)
        v = jnp.pad(v, ((0, 0),) * 4 + ((0, piece_rows - piece),))
        return v.transpose(0, 3, 1, 2, 4).reshape(layers, nf, rows, nz * piece_rows)
    return layered(
        functools.partial(unit_columns_kernel, nz, nf, nr, piece, piece_rows),
        x.astype(jnp.int32).reshape(1),
        w,
        nz * piece_rows,
        nf,
        [],
    )


def stacked(pairs, block):
    for i, pair in enumerate(pairs):
        for core in range(2):
            block[4 * core + i] = pair[core]


def heads_back_kernel(group, span, src_ref, *refs):
    out, wide, v_ref = refs[-3:]
    stacked(refs[:4], v_ref)
    width = out.shape[2] // 3
    padded = group * span
    for rank in range(group):
        block = v_ref[src_ref[rank]].astype(F32)
        for i in range(3):
            wide[:, i * padded + rank * span : i * padded + (rank + 1) * span] = block[
                :, i * span : (i + 1) * span
            ]
    for i in range(3):
        out[0, :, i * width : (i + 1) * width] = wide[:, i * padded : i * padded + width]


def units_back_kernel(nz, nf, nr, piece, piece_rows, ranks, src_ref, *refs):
    out, v_ref = refs[-2:]
    stacked(refs[:4], v_ref)
    for f in range(nf):
        blocks = [v_ref[src_ref[ranks[f][r]]].astype(F32) for r in range(nr)]
        for z in range(nz):
            part = [block[:, z * piece_rows : z * piece_rows + piece] for block in blocks]
            start = (z * nf + f) * nr * piece
            out[0, :, start : start + nr * piece] = jnp.concatenate(part, axis=1)


def into_layer(kernel, plan, pairs, shape, layer, previous, scratch):
    operands = [plan.source().astype(jnp.int32), *pairs]
    in_specs = [pl.BlockSpec(v.shape, lambda i, s: (0, 0, 0)) for v in pairs]
    scratch = scratch + [pltpu.VMEM((8,) + pairs[0].shape[1:], BF)]
    aliases = {}
    if previous is not None:
        operands.append(previous)
        in_specs.append(pl.BlockSpec(memory_space=pl.ANY))
        aliases = {5: 0}
    return pl.pallas_call(
        kernel,
        grid_spec=pltpu.PrefetchScalarGridSpec(
            num_scalar_prefetch=1,
            grid=(1,),
            in_specs=in_specs,
            out_specs=pl.BlockSpec((1,) + shape[1:], lambda i, s: (layer, 0, 0)),
            scratch_shapes=scratch,
        ),
        out_shape=sds(shape, F32),
        input_output_aliases=aliases,
        compiler_params=pltpu.CompilerParams(vmem_limit_bytes=44 * 1024 * 1024),
        cost_estimate=pl.CostEstimate(flops=0, bytes_accessed=48 * pairs[0].size, transcendentals=0),
    )(*operands)


def rows_back_kernel(kept, x_ref, own, other, own_out, other_out, *refs):
    down, out = refs[-2:]
    units = down.shape[1] // 2
    for x in range(2):

        @pl.when(x_ref[0] == x)
        def _():
            first, second = (own, other) if x == 0 else (other, own)
            down[0, :units, :] = first[:units, :].astype(F32)
            down[0, units:, :] = second[:units, :].astype(F32)
            first, second = (own_out, other_out) if x == 0 else (other_out, own_out)
            out[0] = jnp.concatenate(
                [first[...].astype(F32)[:kept], second[...].astype(F32)[:kept]]
            )


def shards(
    plan,
    tokens,
    cotangent,
    segments,
    norm1_gain,
    norm1_shift,
    w_qkv,
    b_query,
    b_value,
    w_out,
    b_out,
    norm2_gain,
    norm2_shift,
    w_up,
    b_up,
    w_down,
    b_down,
):
    nz, nf, nr, group, span = plan.nz, plan.nf, plan.nr, plan.group, plan.span
    layers, own_rows, triple = w_qkv.shape
    width = triple // 3
    own_hidden = w_down.shape[1]
    piece = own_hidden // nr
    part = -(-own_rows // nr)
    part_rows = -(-part // 16) * 16
    piece_rows = -(-piece // 16) * 16
    units = nz * piece_rows
    length = tokens.shape[1]
    total = length * nz
    scale = 1.0 / math.sqrt(HD)
    fsdp = lax.axis_index("fsdp")
    replica = lax.axis_index("replica")
    seq = lax.axis_index("seq")
    rank = plan.rank()

    def rest_of(down, out):
        down = lax.dynamic_slice_in_dim(down, replica * piece, piece, 0)
        down = jnp.pad(down, ((0, piece_rows - piece), (0, 0)))
        out = jnp.pad(out, ((0, nr * part + part_rows - own_rows), (0, 0)))
        out = lax.dynamic_slice_in_dim(out, replica * part, part_rows, 0)
        valid = lax.broadcasted_iota(jnp.int32, out.shape, 0)
        valid = (valid < part) & (valid + replica * part < own_rows)
        return jnp.concatenate([down, jnp.where(valid, out, jnp.zeros_like(out))])

    qkv_send = head_columns(plan, w_qkv)
    first = plan.exchange_fsdp(qkv_send[0]).reshape(nf * own_rows, 3 * span)
    both = plan.regroup(jnp.concatenate([tokens[0], cotangent[0]]))
    small = jnp.concatenate(
        [norm1_gain, norm1_shift, b_query, b_value, b_out, norm2_gain, norm2_shift, b_down, b_up],
        axis=1,
    )
    each_small = small.shape[1]
    small = small.reshape(-1)
    flat_rows = -(-small.shape[0] // 2048) * 16
    small = jnp.pad(small, (0, flat_rows * 128 - small.shape[0])).reshape(flat_rows, 128)
    small = plan.gather_owners(small)
    small = small.reshape(nz * nf, flat_rows * 128)[:, : layers * each_small]
    small = small.reshape(nz * nf, layers, each_small)

    codes = segments[0] * CODE + seq * length + jnp.arange(length, dtype=jnp.int32)
    codes = plan.gather_doubling(plan.regroup(codes[None]))

    first, both, qkv_send, w_up, w_down, w_out, small, codes = lax.optimization_barrier(
        (first, both, qkv_send, w_up, w_down, w_out, small, codes)
    )
    hidden = both[:length].astype(F32)
    grad = both[length:].astype(F32)
    up_send = unit_columns(plan, w_up, piece, piece_rows)
    prepared = []
    for layer in range(layers):
        qkv = first
        if layer:
            qkv = plan.exchange_fsdp(qkv_send[layer]).reshape(nf * own_rows, 3 * span)
        up = plan.exchange_fsdp(up_send[layer]).reshape(nf * own_rows, units)
        prepared.append((qkv, up, rest_of(w_down[layer], w_out[layer])))
    early = [prepared[0][1:], prepared[1:]]
    codes, early = lax.optimization_barrier((codes, early))
    prepared = [(first, *early[0])] + early[1]

    def fetch(layer):
        qkv, up, rest = prepared[layer]
        qkv = gather_seq(qkv)
        rest = gather_seq(rest, lead=layer % 2 == 0)
        up = gather_seq(up)
        return qkv, rest, up

    def unpack(rest):
        rest = rest.reshape(nz, piece_rows + part_rows, width)
        down = rest[:, :piece_rows].reshape(units, width)
        out = rest[:, piece_rows:].reshape(nz * part_rows, width)
        return jnp.concatenate(plan.gather_pieces(out)), down

    source = plan.source()
    feature_heads = (source[:, None] * span + jnp.arange(span, dtype=jnp.int32)).reshape(-1)
    fs = jnp.array(plan.place, dtype=jnp.int32)[source]
    inner = jnp.arange(part_rows, dtype=jnp.int32)
    within = (fs % nr)[:, None, None] * part + inner
    feature_rows = (
        jnp.arange(nz, dtype=jnp.int32)[None, :, None] * (nf * own_rows)
        + (fs // nr)[:, None, None] * own_rows
        + within
    )
    feature_rows = jnp.where((inner < part) & (within < own_rows), feature_rows, -1).reshape(-1)
    select = (feature_heads[:, None] == feature_rows[None, :]).astype(BF)

    def vectors(layer):
        each = [
            small[:, layer, i * own_rows : (i + 1) * own_rows].reshape(width).astype(F32)
            for i in range(8)
        ]
        bias_up = small[:, layer, 8 * own_rows :].reshape(nz, nf, nr, piece)
        bias_up = lax.dynamic_index_in_dim(bias_up, fsdp, 1, keepdims=False)
        bias_up = lax.dynamic_index_in_dim(bias_up, replica, 1, keepdims=False)

        def mine(v):
            return lax.dynamic_slice_in_dim(
                jnp.pad(v, (0, group * span - width)), rank * span, span
            )

        bias_qkv = jnp.concatenate([mine(each[2]), jnp.zeros((span,), F32), mine(each[3])])
        bias_up = jnp.pad(bias_up, ((0, 0), (0, piece_rows - piece)))
        return each, bias_qkv, bias_up.reshape(units).astype(F32)

    vecs = [vectors(layer) for layer in range(layers)]

    weights = [fetch(layer) for layer in range(layers)]

    kept = []
    for layer in range(layers):
        qkv_w, rest, up_w = weights[layer]
        (gain1, shift1, _, _, bias_out, gain2, shift2, bias_down), bias_qkv, bias_up = vecs[layer]
        unit1, inv1 = norm_parts(hidden)
        pieces = plan.gather_pieces(widen((unit1 * gain1 + shift1).astype(BF)))
        if layer == layers - 1:
            grad_pieces = plan.gather_pieces(widen(grad.astype(BF)))
            pieces, grad_pieces = lax.optimization_barrier((pieces, grad_pieces))
        normed, packed, lse, mixed = attend(
            plan, pieces, qkv_w, bias_qkv, codes, total, scale
        )
        out_w, down_w = unpack(after(rest, packed))
        weights[layer] = qkv_w, out_w, up_w, down_w
        mixed = jnp.concatenate(plan.exchange(mixed), axis=1)
        mixed = dot(mixed, select).astype(BF)
        block = nz * part_rows
        mixed_own = plan.exchange(
            jnp.concatenate([mixed[:, i * block : (i + 1) * block] for i in range(group)])
        )
        middle = hidden + (dot(mixed, out_w) + bias_out)
        unit2, inv2 = norm_parts(middle)
        pieces = plan.gather_pieces(widen((unit2 * gain2 + shift2).astype(BF)))
        normed_two, slope, activated, near, far = hidden_units(plan, pieces, up_w, bias_up, down_w)
        kept.append(
            (
                unit1,
                inv1,
                normed,
                packed,
                lse,
                jnp.concatenate(mixed_own),
                unit2,
                inv2,
                normed_two,
                slope,
                activated,
            )
        )
        if layer < layers - 1:
            hidden = middle + (plan.scatter_parts(near, far) + bias_down)
    hidden = middle + (plan.scatter_parts(near, far) + bias_down)
    output = plan.regroup(hidden.astype(BF), back=True)

    def late_up(layer, up, rest, qkv):
        up = plan.to_owners(up)
        if plan.cube:
            ranks = [[plan.rank_of(f, r) for r in range(nr)] for f in range(nf)]
            return into_layer(
                functools.partial(units_back_kernel, nz, nf, nr, piece, piece_rows, ranks),
                plan,
                up,
                (layers, own_rows, nf * nz * nr * piece),
                layer,
                into_up,
                [],
            )
        up = jnp.stack([up[plan.back[m]] for m in range(group)])
        up = up.reshape(nf, nr, own_rows, nz, piece_rows)[..., :piece].transpose(2, 3, 0, 1, 4)
        up = up.reshape(1, own_rows, -1).astype(F32)
        return up if into_up is None else jnp.concatenate([up, into_up])

    def late_qkv(layer, up, rest, qkv):
        qkv = plan.to_owners(qkv)
        if plan.cube:
            return into_layer(
                functools.partial(heads_back_kernel, group, span),
                plan,
                qkv,
                (layers, own_rows, triple),
                layer,
                into_qkv,
                [pltpu.VMEM((own_rows, 3 * group * span), F32)],
            )
        qkv = qkv.reshape(group, own_rows, 3, span).transpose(1, 2, 0, 3)
        qkv = qkv.reshape(own_rows, 3, group * span)[:, :, :width]
        qkv = qkv.reshape(1, own_rows, triple).astype(F32)
        return qkv if into_qkv is None else jnp.concatenate([qkv, into_qkv])

    def late_rest(layer, up, rest, qkv):
        down, out = rest
        if not plan.cube:
            down = lax.all_gather(down, "replica", axis=0, tiled=False)
            out = lax.all_gather(out, "replica", axis=0, tiled=False)
            down = down[:, :piece].reshape(1, own_hidden, width).astype(F32)
            out = out[:, :part].reshape(nr * part, width)[None, :own_rows].astype(F32)
            if into_down is None:
                return down, out
            return jnp.concatenate([down, into_down]), jnp.concatenate([out, into_out])
        operands = [down, plan.swap_x(down), out, plan.swap_x(out)]
        in_specs = [pl.BlockSpec(v.shape, lambda i, s: (0, 0)) for v in operands]
        operands = [replica.astype(jnp.int32).reshape(1)] + operands
        aliases = {}
        if into_down is not None:
            operands += [into_down, into_out]
            in_specs += [pl.BlockSpec(memory_space=pl.ANY)] * 2
            aliases = {5: 0, 6: 1}
        return pl.pallas_call(
            functools.partial(rows_back_kernel, part),
            grid_spec=pltpu.PrefetchScalarGridSpec(
                num_scalar_prefetch=1,
                grid=(1,),
                in_specs=in_specs,
                out_specs=[
                    pl.BlockSpec((1, own_hidden, width), lambda i, s: (layer, 0, 0)),
                    pl.BlockSpec((1, own_rows, width), lambda i, s: (layer, 0, 0)),
                ],
            ),
            out_shape=[
                sds((layers, own_hidden, width), F32),
                sds((layers, own_rows, width), F32),
            ],
            input_output_aliases=aliases,
            compiler_params=pltpu.CompilerParams(vmem_limit_bytes=44 * 1024 * 1024),
            cost_estimate=pl.CostEstimate(
                flops=0, bytes_accessed=12 * down.size, transcendentals=0
            ),
        )(*operands)

    into_qkv = into_up = into_down = into_out = None
    smalls = [None] * layers
    late = None
    for layer in reversed(range(layers)):
        qkv_w, out_w, up_w, down_w = weights[layer]
        (gain1, _, _, _, _, gain2, _, _), _, _ = vecs[layer]
        unit1, inv1, normed, packed, lse, mixed, unit2, inv2, normed_two, slope, activated = kept[
            layer
        ]
        g_low = grad.astype(BF)
        grad_down = down_grad(plan, activated, grad_pieces, width)
        if late is not None:
            out = scatter_seq(down_grad(plan, *late[2][1], width))
            late = (late[0], late[1], (late[2][0], out), late[3])
            into_up = late_up(*late)
            into_down, into_out = late_rest(*late)
        if late is None:
            grad_pieces, grad_down = lax.optimization_barrier((grad_pieces, grad_down))
        down = scatter_seq(grad_down, lead=True)
        g_lift, grad_b_up, near, far = hidden_back(
            plan, grad_pieces, slope, down_w, up_w
        )
        grad_up = wgrad(plan, normed_two, g_lift)
        g_n2 = plan.scatter_parts(near, far)
        up = scatter_seq(grad_up).reshape(nf, own_rows, units)
        g_mid = grad + norm_pull(g_n2, unit2, inv2, gain2)
        g_att = g_mid.astype(BF)
        g_mixed = dot(g_att, out_w, 1, 1).astype(BF)
        g_mixed = dot(g_mixed, select, 1, 1).astype(BF)
        g_mixed = jnp.concatenate(
            [g_mixed[:, i * span : (i + 1) * span] for i in range(group)]
        )
        g_mixed = plan.exchange(g_mixed)
        att_pieces = plan.gather_pieces(widen(g_att))
        g_packed, g_b, near, far = attend_back(
            plan, g_mixed, packed, lse, codes, qkv_w, total, scale
        )
        grad_qkv = wgrad(plan, normed, g_packed)
        g_n1 = plan.scatter_parts(near, far)
        qkv = scatter_seq(grad_qkv)
        qkv = qkv.reshape(nf, own_rows, 3 * span)
        if late is not None:
            into_qkv = late_qkv(*late[:3], after(late[3], g_n1))
        late = (layer, up, (down, (after(mixed, g_n1), att_pieces)), qkv)
        smalls[layer] = (
            jnp.sum(g_n1 * unit1, axis=0),
            jnp.sum(g_n1, axis=0),
            g_b,
            jnp.sum(g_att.astype(F32), axis=0),
            jnp.sum(g_n2 * unit2, axis=0),
            jnp.sum(g_n2, axis=0),
            jnp.sum(g_low.astype(F32), axis=0),
            grad_b_up,
        )
        grad = g_mid + norm_pull(g_n1, unit1, inv1, gain1)
        if layer:
            grad_pieces = plan.gather_pieces(widen(grad.astype(BF)))
    out = scatter_seq(down_grad(plan, *late[2][1], width))
    late = (late[0], late[1], (late[2][0], out), late[3])
    grad_tokens = plan.regroup(grad.astype(BF), back=True).astype(F32)
    output = after(output, grad).astype(F32)
    into_up = late_up(*late)
    into_down, into_out = late_rest(*late)
    into_qkv = late_qkv(*late)

    def scattered(layer):
        n1g, n1s, g_b, b_o, n2g, n2s, b_d, b_u = smalls[layer]

        def place(v):
            full = lax.dynamic_update_slice_in_dim(
                jnp.zeros((group * span,), F32), v, rank * span, 0
            )
            return full[:width]

        b_u = lax.dynamic_update_slice(
            jnp.zeros((nz, nf, nr, piece), F32),
            b_u.reshape(nz, 1, 1, piece_rows)[..., :piece],
            (0, fsdp, replica, 0),
        )
        rows = [n1g, n1s, place(g_b[:span]), place(g_b[2 * span :]), b_o, n2g, n2s, b_d]
        return jnp.concatenate(
            [v.reshape(nz * nf, own_rows) for v in rows] + [b_u.reshape(nz * nf, own_hidden)],
            axis=1,
        )

    flat = jnp.concatenate([scattered(layer) for layer in range(layers)], axis=1)
    wide = lanes(-(-flat.shape[1] // 2))
    flat = jnp.pad(flat, ((0, 0), (0, 2 * wide - flat.shape[1])))
    flat = plan.scatter_small(flat.reshape(nz, nf, 2, wide))
    flat = jnp.sum(plan.to_owners_small(flat), axis=0).reshape(-1)
    flat = flat[: layers * each_small].reshape(layers, each_small)
    vec = [flat[:, i * own_rows : (i + 1) * own_rows] for i in range(8)]
    return (
        output[None],
        grad_tokens[None],
        vec[0],
        vec[1],
        into_qkv,
        vec[2],
        vec[3],
        into_out,
        vec[4],
        vec[5],
        vec[6],
        into_up,
        flat[:, 8 * own_rows :],
        into_down,
        vec[7],
    )


def solution(mesh):
    plan = Plan(mesh)
    data = P(("fsdp", "replica"), "seq", None)
    vector = P(None, ("seq", "fsdp"))
    matrix = P(None, ("seq", "fsdp"), None)
    weights = (
        vector,
        vector,
        matrix,
        vector,
        vector,
        matrix,
        vector,
        vector,
        vector,
        matrix,
        vector,
        matrix,
        vector,
    )
    in_specs = (data, data, P(("fsdp", "replica"), "seq")) + weights
    out_specs = (data, data) + weights
    return jax.shard_map(
        functools.partial(shards, plan),
        mesh=mesh,
        in_specs=in_specs,
        out_specs=out_specs,
        check_vma=False,
    )
```

```python
import functools
import math

import jax
import jax.numpy as jnp
from jax import lax
from jax.experimental import pallas as pl
from jax.experimental.pallas import tpu as pltpu
from jax.sharding import PartitionSpec as P


HEADS = 25
HD = 64
BF = jnp.bfloat16
F32 = jnp.float32
ALL = ("seq", "fsdp", "replica")
GROUP = ("fsdp", "replica")
OWNERS = ("seq", "fsdp")
CODE = 65536
LOW = -1e30


def dot(a, b, ca=1, cb=0):
    return lax.dot_general(a, b, (((ca,), (cb,)), ((), ())), preferred_element_type=F32)


def norm_parts(v):
    mean = jnp.mean(v, axis=-1, keepdims=True)
    centred = v - mean
    spread = jnp.mean(centred * centred, axis=-1, keepdims=True)
    inv = lax.rsqrt(spread + 1e-05)
    return centred * inv, inv


def norm_pull(grad, unit, inv, gain):
    scaled = grad * gain
    first = jnp.mean(scaled, axis=-1, keepdims=True)
    second = jnp.mean(scaled * unit, axis=-1, keepdims=True)
    return inv * (scaled - first - unit * second)


def gelu_both(value):
    tanh = jnp.tanh(0.7978845608028654 * (value + 0.044715 * value * value * value))
    inner = 0.7978845608028654 * (1.0 + 3.0 * 0.044715 * value * value)
    half = 0.5 * (1.0 + tanh)
    return value * half, half + 0.5 * value * (1.0 - tanh * tanh) * inner


class Plan:
    def __init__(self, mesh):
        self.nz = mesh.shape["seq"]
        self.nf = mesh.shape["fsdp"]
        self.nr = mesh.shape["replica"]
        self.group = self.nf * self.nr
        self.cube = self.nf == 4 and self.nr == 2
        self.heads = 2 * -(-HEADS // (2 * self.group))
        self.span = self.heads * HD
        order = sorted(
            (self.rank_of(f, r), f * self.nr + r) for f in range(self.nf) for r in range(self.nr)
        )
        self.place = [member for _, member in order]
        self.back = [0] * self.group
        for rank, member in order:
            self.back[member] = rank

    def rank_of(self, f, r):
        half = self.group // 2
        if self.nf % 2:
            return f * self.nr + r
        return (f % 2) * half + (f // 2) * self.nr + r

    def rank(self):
        return self.rank_of(lax.axis_index("fsdp"), lax.axis_index("replica"))

    def regroup(self, v, back=False):
        nz = self.nz
        pairs = []
        for z in range(nz):
            for g in range(self.group):
                goal = g % nz
                slot = (g // nz) * nz + (z ^ goal if nz & (nz - 1) == 0 else z)
                pairs.append((z * self.group + self.place[g], goal * self.group + self.place[slot]))
        if back:
            pairs = [(there, here) for here, there in pairs]
        return lax.ppermute(v, ALL, pairs)

    def swap_core(self, v):
        return lax.ppermute(v, "fsdp", [(f, f ^ 1) for f in range(self.nf)])

    def swap_y(self, v):
        return lax.ppermute(v, "fsdp", [(f, f ^ 2) for f in range(self.nf)])

    def swap_x(self, v):
        return lax.ppermute(v, "replica", [(r, r ^ 1) for r in range(self.nr)])

    def swap_xy(self, v):
        pairs = [
            (f * self.nr + r, (f ^ 2) * self.nr + (r ^ 1))
            for f in range(self.nf)
            for r in range(self.nr)
        ]
        return lax.ppermute(v, GROUP, pairs)

    def source(self):
        base = jnp.arange(self.group, dtype=jnp.int32)
        return base ^ self.rank() if self.cube else base

    def gather_pieces(self, v):
        if not self.cube:
            full = lax.all_gather(v, GROUP, axis=0, tiled=False)
            return [full[member] for member in self.place]
        near = [v, self.swap_x(v), self.swap_y(v), self.swap_xy(v)]
        return near + [self.swap_core(piece) for piece in near]

    def gather_doubling(self, v):
        if not self.cube:
            return jnp.concatenate(self.gather_pieces(v))
        for swap in (self.swap_x, self.swap_y, self.swap_core):
            v = jnp.concatenate([v, swap(v)])
        return v

    def scatter_parts(self, near, far):
        if not self.cube:
            blocks = jnp.concatenate([near.astype(BF), far])
            rows = blocks.shape[0] // self.group
            blocks = blocks.reshape(self.group, rows, -1)[jnp.array(self.back)]
            blocks = blocks.reshape(self.group * rows, -1)
            return lax.psum_scatter(blocks, GROUP, scatter_dimension=0, tiled=True).astype(F32)
        rows, columns = near.shape[0] // 4, near.shape[1]
        own, to_x, to_y, to_xy = call(
            fold_kernel,
            [sds((rows, columns), F32)] + [sds((rows, lanes(columns)), BF)] * 3,
            [],
            0,
            [near, self.swap_core(far)],
        )
        parts = self.swap_xy(to_xy), self.swap_x(to_x), self.swap_y(to_y)
        parts = [part[:, :columns].astype(F32) for part in parts]
        return own + parts[0] + parts[1] + parts[2]

    def exchange(self, v):
        if not self.cube:
            v = v.reshape(self.group, -1, v.shape[1])[jnp.array(self.back)]
            v = lax.all_to_all(v, GROUP, split_axis=0, concat_axis=0, tiled=True)
            return [v[member] for member in self.place]
        rows = v.shape[0] // 8
        half = 4 * rows
        far = self.swap_core(v[half:])
        out = [[v[:rows], far[:rows]]]
        for i, swap in ((1, self.swap_x), (2, self.swap_y), (3, self.swap_xy)):
            both = swap(
                jnp.concatenate([v[i * rows : (i + 1) * rows], far[i * rows : (i + 1) * rows]])
            )
            out.append([both[:rows], both[rows:]])
        return [pair[0] for pair in out] + [pair[1] for pair in out]

    def flips(self, v):
        f = lax.axis_index("fsdp")
        v = v.reshape((2, 2) + v.shape[1:])
        v = jnp.where(f // 2 == 1, jnp.flip(v, 0), v)
        return jnp.where(f % 2 == 1, jnp.flip(v, 1), v)

    def gather_owners(self, v):
        if not self.cube or self.nz != 4:
            return lax.all_gather(v, OWNERS, axis=0, tiled=False)
        z, f = lax.axis_index("seq"), lax.axis_index("fsdp")
        far = [
            lax.ppermute(v, "seq", [(i, i ^ d) for i in range(4)]) if d else v for d in range(4)
        ]
        v = jnp.stack(far).reshape((2, 2) + v.shape)
        v = jnp.where(z // 2 == 1, jnp.flip(v, 0), v)
        v = jnp.where(z % 2 == 1, jnp.flip(v, 1), v)
        other = self.swap_core(v)
        v = jnp.stack([jnp.where(f % 2 == 0, v, other), jnp.where(f % 2 == 0, other, v)], axis=2)
        other = self.swap_y(v)
        v = jnp.stack([jnp.where(f // 2 == 0, v, other), jnp.where(f // 2 == 0, other, v)], axis=2)
        return v.reshape((16,) + v.shape[4:])

    def exchange_fsdp(self, v):
        if not self.cube:
            return lax.all_to_all(v, "fsdp", split_axis=0, concat_axis=0, tiled=True)
        shape = v.shape
        v = self.flips(v)
        both = jnp.stack([v[:, 0], self.swap_core(v[:, 1])], axis=1)
        return self.flips(jnp.stack([both[0], self.swap_y(both[1])]).reshape(shape)).reshape(shape)

    def scatter_small(self, v):
        if not self.cube or self.nz != 4:
            return lax.psum_scatter(v, "seq", scatter_dimension=0, tiled=False)
        z = lax.axis_index("seq")
        total = lax.dynamic_index_in_dim(v, z, 0, keepdims=False)
        for d in range(1, 4):
            other = lax.dynamic_index_in_dim(v, z ^ d, 0, keepdims=False)
            total = total + lax.ppermute(other, "seq", [(i, i ^ d) for i in range(4)])
        return total

    def to_owners_small(self, v):
        if not self.cube:
            v = lax.all_to_all(v, "fsdp", split_axis=0, concat_axis=0, tiled=True)
            v = lax.all_gather(v, "replica", axis=1, tiled=False)
            return jnp.stack([v[m // self.nr, m % self.nr] for m in self.place])
        v = self.flips(v)
        far = self.swap_core(v[:, 1])
        here = jnp.stack([v[0, 0], far[0]])
        there = jnp.stack([v[1, 0], far[1]])
        return jnp.stack(
            [here, self.swap_x(here), self.swap_y(there), self.swap_xy(there)], axis=1
        ).reshape((8,) + v.shape[2:])

    def to_owners(self, v):
        if not self.cube:
            return self.to_owners_small(v)
        nf, rows, columns = v.shape
        f = lax.axis_index("fsdp")
        pick = (f ^ jnp.arange(nf, dtype=jnp.int32)).astype(jnp.int32)
        pair = sds((2, rows, columns), BF)
        near, far = pl.pallas_call(
            pick_kernel,
            grid_spec=pltpu.PrefetchScalarGridSpec(
                num_scalar_prefetch=1,
                grid=(1,),
                in_specs=[pl.BlockSpec(v.shape, lambda i, s: (0, 0, 0))],
                out_specs=[pl.BlockSpec(pair.shape, lambda i, s: (0, 0, 0))] * 2,
            ),
            out_shape=[pair] * 2,
            compiler_params=pltpu.CompilerParams(vmem_limit_bytes=44 * 1024 * 1024),
        )(pick, v)
        here, there = call(pair_kernel, [pair] * 2, [], 0, [near, self.swap_core(far)])
        return [here, self.swap_x(here), self.swap_y(there), self.swap_xy(there)]


def pick_kernel(order, v, near, far):
    for y in range(2):
        near[y] = v[order[2 * y]]
        far[y] = v[order[2 * y + 1]]


def pair_kernel(near, far, here, there):
    for y, out in enumerate((here, there)):
        out[0] = near[y]
        out[1] = far[y]


def gather_seq(v, lead=False):
    if lead:
        return lax.all_gather(v[None], "seq", axis=1, tiled=True)[0]
    return lax.all_gather(v, "seq", axis=0, tiled=True)


def scatter_seq(v, lead=False):
    if lead:
        return lax.psum_scatter(v[None], "seq", scatter_dimension=1, tiled=True)[0]
    return lax.psum_scatter(v, "seq", scatter_dimension=0, tiled=True)


def call(kernel, outs, scratch, flops, operands, **more):
    params = pltpu.CompilerParams(vmem_limit_bytes=44 * 1024 * 1024)
    size = sum(math.prod(o.shape) * o.dtype.itemsize for o in list(outs) + list(operands))
    return pl.pallas_call(
        kernel,
        out_shape=tuple(outs),
        scratch_shapes=scratch,
        compiler_params=params,
        cost_estimate=pl.CostEstimate(
            flops=int(flops), bytes_accessed=int(size), transcendentals=0
        ),
        **more,
    )(*operands)


def lanes(columns):
    return -(-columns // 128) * 128


def widen(v):
    return jnp.pad(v, ((0, 0), (0, lanes(v.shape[1]) - v.shape[1])))


def sds(shape, dtype):
    return jax.ShapeDtypeStruct(shape, dtype)


def fold_kernel(near, far, own, to_x, to_y, to_xy):
    rows, columns = own.shape
    own[...] = near[:rows, :] + far[:rows, :columns].astype(F32)
    for i, out in ((1, to_x), (2, to_y), (3, to_xy)):
        at = slice(i * rows, (i + 1) * rows)
        out[:, :columns] = (near[at, :] + far[at, :columns].astype(F32)).astype(BF)


def wgrad_kernel(left, right, out):
    tall = out.shape[0]
    block = 256

    def body(i, carry):
        at = pl.ds(pl.multiple_of(i * block, block), block)
        out[at, :] = dot(left[:, at], right[...], 0, 0).astype(BF)
        return carry

    whole = tall // block
    lax.fori_loop(0, whole, body, 0)
    if tall % block:
        out[whole * block :, :] = dot(left[:, whole * block :], right[...], 0, 0).astype(BF)


def wgrad(plan, left, right):
    if not plan.cube:
        return dot(left, right, 0, 0).astype(BF)
    tall, width = left.shape[1], right.shape[1]
    return call(
        wgrad_kernel, [sds((tall, width), BF)], [], 2 * left.size * width, [left, right]
    )[0]


def after(v, other):
    return lax.optimization_barrier((v, other))[0]


def first_half(shape):
    return lax.broadcasted_iota(jnp.int32, shape, 1) < HD


def attend_kernel(count, total, span, scale, *refs):
    pieces = refs[:count]
    w, bias, code_col, code_row, full, packed, lse, mixed = refs[count:]
    rows = pieces[0].shape[0]
    for i, piece in enumerate(pieces):
        full[i * rows : (i + 1) * rows, :] = piece[:, : full.shape[1]]
    block = 2 * rows

    def project(i, carry):
        at = pl.ds(pl.multiple_of(i * block, block), block)
        packed[at, :] = (dot(full[at, :], w[...]) + bias[...]).astype(BF)
        return carry

    lax.fori_loop(0, count // 2, project, 0)
    blocks = total // rows
    left = first_half((rows, 2 * HD))
    lane = lax.broadcasted_iota(jnp.int32, (rows, 128), 1)

    def queries(i, carry):
        at = pl.ds(pl.multiple_of(i * rows, rows), rows)
        seq = i // blocks
        keys_at = pl.ds(pl.multiple_of(seq * total, total), total)
        code_q = code_col[at, :]
        code_k = code_row[pl.ds(seq, 1), :]
        allowed = (code_k <= code_q) & (code_k >= (code_q // CODE) * CODE)
        stats = jnp.zeros((rows, 128), F32)
        for pair in range(span // 128):
            q = packed[at, pair * 128 : pair * 128 + 128]
            k = packed[keys_at, span + pair * 128 : span + pair * 128 + 128]
            v = packed[keys_at, 2 * span + pair * 128 : 2 * span + pair * 128 + 128]
            both = []
            for side in range(2):
                own = left if side == 0 else ~left
                scores = dot(jnp.where(own, q, jnp.zeros_like(q)), k, 1, 1) * scale
                scores = jnp.where(allowed, scores, LOW)
                top = jnp.max(scores, axis=1, keepdims=True)
                expo = jnp.exp(scores - top)
                denom = jnp.sum(expo, axis=1, keepdims=True)
                probs = (expo * (1.0 / denom)).astype(BF)
                both.append(dot(probs, v))
                stats = jnp.where(lane == 2 * pair + side, top + jnp.log(denom), stats)
            mixed[at, pair * 128 : pair * 128 + 128] = jnp.where(left, both[0], both[1]).astype(BF)
        lse[:, at] = stats.T[: lse.shape[0], :]
        return carry

    lax.fori_loop(0, count, queries, 0)


def attend(plan, pieces, w, bias, codes, total, scale):
    rows, width = pieces[0].shape[0], w.shape[0]
    count, span = plan.group, plan.span
    if not plan.cube:
        full = jnp.concatenate(pieces)[:, :width]
        packed = (dot(full, w) + bias).astype(BF)
        q, k, v = (
            packed[:, i * span : (i + 1) * span].reshape(-1, total, plan.heads, HD)
            for i in range(3)
        )
        allowed = mask_of(codes, total)
        scores = jnp.einsum("sqhd,skhd->shqk", q, k, preferred_element_type=F32) * scale
        scores = jnp.where(allowed[:, None], scores, LOW)
        top = jnp.max(scores, axis=-1, keepdims=True)
        expo = jnp.exp(scores - top)
        denom = jnp.sum(expo, axis=-1, keepdims=True)
        probs = (expo / denom).astype(BF)
        mixed = jnp.einsum("shqk,skhd->sqhd", probs, v, preferred_element_type=F32)
        return full, packed, top + jnp.log(denom), mixed.reshape(-1, span).astype(BF)
    tall = count * rows
    return call(
        functools.partial(attend_kernel, count, total, span, scale),
        [
            sds((tall, width), BF),
            sds((tall, 3 * span), BF),
            sds((8, tall), F32),
            sds((tall, span), BF),
        ],
        [],
        2 * tall * width * 3 * span + 8 * tall * total * span,
        [*pieces, w, bias[None], codes.reshape(-1, 1), codes.reshape(-1, total)],
    )


def mask_of(codes, total):
    code = codes.reshape(-1, total)
    low = (code // CODE) * CODE
    return (code[:, None, :] <= code[:, :, None]) & (code[:, None, :] >= low[:, :, None])


def attend_back_kernel(count, total, span, scale, *refs):
    pieces = refs[:count]
    packed, lse, code_col, code_row, w, g_packed, g_bias, near, far, gm, g_k, g_v = refs[count:]
    rows = pieces[0].shape[0]
    for i, piece in enumerate(pieces):
        gm[i * rows : (i + 1) * rows, :] = piece[...]
    blocks = total // rows
    left = first_half((rows, 2 * HD))

    def sequence(seq, carry):
        keys_at = pl.ds(pl.multiple_of(seq * total, total), total)
        code_k = code_col[keys_at, :]
        for pair in range(span // 128):
            lanes = slice(pair * 128, pair * 128 + 128)
            k_lanes = slice(span + pair * 128, span + pair * 128 + 128)
            v_lanes = slice(2 * span + pair * 128, 2 * span + pair * 128 + 128)
            k = packed[keys_at, k_lanes]
            v = packed[keys_at, v_lanes]
            g_k[...] = jnp.zeros_like(g_k)
            g_v[...] = jnp.zeros_like(g_v)

            def queries(i, inner):
                at = pl.ds(pl.multiple_of(seq * total + i * rows, rows), rows)
                code_q = code_row[pl.ds(seq * blocks + i, 1), :]
                allowed = (code_k <= code_q) & (code_k >= (code_q // CODE) * CODE)
                q = packed[at, lanes]
                g = gm[at, lanes]
                both = []
                for side in range(2):
                    own = left if side == 0 else ~left
                    q_own = jnp.where(own, q, jnp.zeros_like(q))
                    g_own = jnp.where(own, g, jnp.zeros_like(g))
                    scores = dot(k, q_own, 1, 1) * scale
                    row = 2 * pair + side
                    probs = jnp.exp(jnp.where(allowed, scores, LOW) - lse[row : row + 1, at])
                    g_probs = dot(v, g_own, 1, 1)
                    each = jnp.sum(g_probs * probs, axis=0, keepdims=True)
                    g_scores = (probs * (g_probs - each)).astype(BF)
                    g_v[...] += dot(probs.astype(BF), g_own)
                    g_k[...] += dot(g_scores, q_own)
                    both.append(dot(g_scores, k, 0, 0))
                g_packed[at, lanes] = (jnp.where(left, both[0], both[1]) * scale).astype(BF)
                return inner

            lax.fori_loop(0, blocks, queries, 0)
            g_packed[keys_at, k_lanes] = (g_k[...] * scale).astype(BF)
            g_packed[keys_at, v_lanes] = g_v[...].astype(BF)
        return carry

    lax.fori_loop(0, count // blocks, sequence, 0)
    g_bias[...] = jnp.sum(g_packed[...].astype(F32), axis=0, keepdims=True)
    spread_out(g_packed, w, near, far, 2 * rows)


def spread_out(left, right, near, far, block):
    half = near.shape[0]

    def first(i, carry):
        at = pl.ds(pl.multiple_of(i * block, block), block)
        near[at, :] = dot(left[at, :], right[...], 1, 1)
        return carry

    def second(i, carry):
        at = pl.ds(pl.multiple_of(i * block, block), block)
        far[at, : near.shape[1]] = dot(
            left[pl.ds(pl.multiple_of(half + i * block, block), block), :], right[...], 1, 1
        ).astype(BF)
        return carry

    lax.fori_loop(0, half // block, first, 0)
    lax.fori_loop(0, half // block, second, 0)


def halves(v):
    half = v.shape[0] // 2
    return v[:half], v[half:].astype(BF)


def attend_back(plan, pieces, packed, lse, codes, w, total, scale):
    count, span = plan.group, plan.span
    rows = pieces[0].shape[0]
    width = w.shape[0]
    if not plan.cube:
        q, k, v = (
            packed[:, i * span : (i + 1) * span].reshape(-1, total, plan.heads, HD)
            for i in range(3)
        )
        gm = jnp.concatenate(pieces).reshape(-1, total, plan.heads, HD)
        allowed = mask_of(codes, total)
        scores = jnp.einsum("sqhd,skhd->shqk", q, k, preferred_element_type=F32) * scale
        probs = jnp.exp(jnp.where(allowed[:, None], scores, LOW) - lse)
        g_probs = jnp.einsum("sqhd,skhd->shqk", gm, v, preferred_element_type=F32)
        g_v = jnp.einsum("shqk,sqhd->skhd", probs.astype(BF), gm, preferred_element_type=F32)
        row = jnp.sum(g_probs * probs, axis=-1, keepdims=True)
        g_s = (probs * (g_probs - row)).astype(BF)
        g_q = jnp.einsum("shqk,skhd->sqhd", g_s, k, preferred_element_type=F32) * scale
        g_k = jnp.einsum("shqk,sqhd->skhd", g_s, q, preferred_element_type=F32) * scale
        g_packed = jnp.concatenate(
            [u.reshape(-1, span).astype(BF) for u in (g_q, g_k, g_v)], axis=1
        )
        near, far = halves(dot(g_packed, w, 1, 1))
        return g_packed, jnp.sum(g_packed.astype(F32), axis=0), near, far
    tall = count * rows
    g_packed, g_bias, near, far = call(
        functools.partial(attend_back_kernel, count, total, span, scale),
        [
            sds((tall, 3 * span), BF),
            sds((1, 3 * span), F32),
            sds((tall // 2, width), F32),
            sds((tall // 2, lanes(width)), BF),
        ],
        [pltpu.VMEM((tall, span), BF)] + [pltpu.VMEM((total, 128), F32)] * 2,
        2 * tall * width * 3 * span + 20 * tall * total * span,
        [*pieces, packed, lse, codes.reshape(-1, 1), codes.reshape(-1, rows), w],
    )
    return g_packed, g_bias[0], near, far


def hidden_kernel(count, *refs):
    pieces = refs[:count]
    up, bias, down, full, slope, activated, near, far = refs[count:]
    rows = pieces[0].shape[0]
    for i, piece in enumerate(pieces):
        full[i * rows : (i + 1) * rows, :] = piece[:, : full.shape[1]]
    block = 2 * rows
    half = near.shape[0]

    def lift(at):
        value, pull = gelu_both(dot(full[at, :], up[...]) + bias[...])
        value = value.astype(BF)
        activated[at, :] = value
        slope[at, :] = pull.astype(BF)
        return dot(value, down[...])

    def first(i, carry):
        at = pl.ds(pl.multiple_of(i * block, block), block)
        near[at, :] = lift(at)
        return carry

    def second(i, carry):
        at = pl.ds(pl.multiple_of(i * block, block), block)
        out = lift(pl.ds(pl.multiple_of(half + i * block, block), block))
        far[at, : near.shape[1]] = out.astype(BF)
        return carry

    lax.fori_loop(0, half // block, first, 0)
    lax.fori_loop(0, half // block, second, 0)


def lift_kernel(count, *refs):
    pieces = refs[:count]
    up, bias, full, slope, activated = refs[count:]
    rows = pieces[0].shape[0]
    for i, piece in enumerate(pieces):
        full[i * rows : (i + 1) * rows, :] = piece[:, : full.shape[1]]
    block = 2 * rows

    def lift(i, carry):
        at = pl.ds(pl.multiple_of(i * block, block), block)
        value, pull = gelu_both(dot(full[at, :], up[...]) + bias[...])
        activated[at, :] = value.astype(BF)
        slope[at, :] = pull.astype(BF)
        return carry

    lax.fori_loop(0, count // 2, lift, 0)


def lift_units(plan, pieces, up, bias):
    rows, width = pieces[0].shape[0], up.shape[0]
    if not plan.cube:
        full = jnp.concatenate(pieces)[:, :width]
        value, pull = gelu_both(dot(full, up) + bias)
        return full, pull.astype(BF), value.astype(BF)
    tall, units = plan.group * rows, up.shape[1]
    return call(
        functools.partial(lift_kernel, plan.group),
        [sds((tall, width), BF), sds((tall, units), BF), sds((tall, units), BF)],
        [],
        2 * tall * width * units,
        [*pieces, up, bias[None]],
    )


def lower_kernel(block, left, right, near, far):
    half, width = near.shape

    def first(i, carry):
        at = pl.ds(pl.multiple_of(i * block, block), block)
        near[at, :] = dot(left[at, :], right[...])
        return carry

    def second(i, carry):
        at = pl.ds(pl.multiple_of(i * block, block), block)
        rows = left[pl.ds(pl.multiple_of(half + i * block, block), block), :]
        far[at, :width] = dot(rows, right[...]).astype(BF)
        return carry

    lax.fori_loop(0, half // block, first, 0)
    lax.fori_loop(0, half // block, second, 0)


def lower_units(plan, activated, down):
    tall, width = activated.shape[0], down.shape[1]
    if not plan.cube:
        return halves(dot(activated, down))
    return call(
        functools.partial(lower_kernel, 2 * (tall // plan.group)),
        [sds((tall // 2, width), F32), sds((tall // 2, lanes(width)), BF)],
        [],
        2 * activated.size * width,
        [activated, down],
    )


def hidden_units(plan, pieces, up, bias, down):
    rows, width = pieces[0].shape[0], up.shape[0]
    if not plan.cube:
        full = jnp.concatenate(pieces)[:, :width]
        value, pull = gelu_both(dot(full, up) + bias)
        value = value.astype(BF)
        return (full, pull.astype(BF), value) + halves(dot(value, down))
    tall, units = plan.group * rows, up.shape[1]
    return call(
        functools.partial(hidden_kernel, plan.group),
        [
            sds((tall, width), BF),
            sds((tall, units), BF),
            sds((tall, units), BF),
            sds((tall // 2, width), F32),
            sds((tall // 2, lanes(width)), BF),
        ],
        [],
        4 * tall * width * units,
        [*pieces, up, bias[None], down],
    )


def hidden_back_kernel(count, *refs):
    pieces = refs[:count]
    slope, down, up, g_lift, g_bias, near, far, full = refs[count:]
    rows = pieces[0].shape[0]
    for i, piece in enumerate(pieces):
        full[i * rows : (i + 1) * rows, :] = piece[:, : full.shape[1]]
    block = 2 * rows

    def pull(i, carry):
        at = pl.ds(pl.multiple_of(i * block, block), block)
        g_lift[at, :] = (dot(full[at, :], down[...], 1, 1) * slope[at, :].astype(F32)).astype(BF)
        return carry

    lax.fori_loop(0, count // 2, pull, 0)
    spread_out(g_lift, up, near, far, block)
    g_bias[...] = jnp.sum(g_lift[...].astype(F32), axis=0, keepdims=True)


def hidden_back(plan, pieces, slope, down, up):
    rows, width = pieces[0].shape[0], up.shape[0]
    if not plan.cube:
        full = jnp.concatenate(pieces)[:, :width]
        g_lift = (dot(full, down, 1, 1) * slope.astype(F32)).astype(BF)
        return (g_lift, jnp.sum(g_lift.astype(F32), axis=0)) + halves(dot(g_lift, up, 1, 1))
    tall, units = plan.group * rows, up.shape[1]
    g_lift, g_bias, near, far = call(
        functools.partial(hidden_back_kernel, plan.group),
        [
            sds((tall, units), BF),
            sds((1, units), F32),
            sds((tall // 2, width), F32),
            sds((tall // 2, lanes(width)), BF),
        ],
        [pltpu.VMEM((tall, width), BF)],
        4 * tall * width * units,
        [*pieces, slope, down, up],
    )
    return g_lift, g_bias[0], near, far


def down_grad_kernel(count, *refs):
    left, out, full = refs[count:]
    rows = refs[0].shape[0]
    for i, piece in enumerate(refs[:count]):
        full[i * rows : (i + 1) * rows, :] = piece[:, : full.shape[1]]
    wgrad_kernel(left, full, out)


def down_grad(plan, left, pieces, width):
    if not plan.cube:
        return dot(left, jnp.concatenate(pieces)[:, :width], 0, 0).astype(BF)
    tall, units = left.shape
    return call(
        functools.partial(down_grad_kernel, plan.group),
        [sds((units, width), BF)],
        [pltpu.VMEM((tall, width), BF)],
        2 * left.size * width,
        [*pieces, left],
    )[0]


def head_columns_kernel(nf, ranks, span, x_ref, w_ref, out, wide):
    width = w_ref.shape[2] // 3
    padded = wide.shape[1] // 3
    w = w_ref[0].astype(F32)
    for i in range(3):
        wide[:, i * padded : i * padded + width] = w[:, i * width : (i + 1) * width]
        if padded > width:
            wide[:, i * padded + width : (i + 1) * padded] = jnp.zeros(
                (wide.shape[0], padded - width), F32
            )
    for x, row in enumerate(ranks):

        @pl.when(x_ref[0] == x)
        def _():
            for f in range(nf):
                for i in range(3):
                    start = i * padded + row[f] * span
                    out[0, f, :, i * span : (i + 1) * span] = wide[:, start : start + span].astype(
                        BF
                    )


def unit_columns_kernel(nz, nf, nr, piece, piece_rows, x_ref, w_ref, out):
    w = w_ref[0].astype(F32)
    for x in range(nr):

        @pl.when(x_ref[0] == x)
        def _():
            for f in range(nf):
                part = []
                for z in range(nz):
                    start = ((z * nf + f) * nr + x) * piece
                    part.append(w[:, start : start + piece])
                    if piece_rows > piece:
                        part.append(jnp.zeros((w.shape[0], piece_rows - piece), F32))
                out[0, f] = jnp.concatenate(part, axis=1).astype(BF)


def layered(kernel, x, w, columns, nf, scratch):
    layers, rows, full = w.shape
    return pl.pallas_call(
        kernel,
        grid_spec=pltpu.PrefetchScalarGridSpec(
            num_scalar_prefetch=1,
            grid=(layers,),
            in_specs=[pl.BlockSpec((1, rows, full), lambda i, s: (i, 0, 0))],
            out_specs=pl.BlockSpec((1, nf, rows, columns), lambda i, s: (i, 0, 0, 0)),
            scratch_shapes=scratch,
        ),
        out_shape=sds((layers, nf, rows, columns), BF),
        compiler_params=pltpu.CompilerParams(vmem_limit_bytes=44 * 1024 * 1024),
        cost_estimate=pl.CostEstimate(flops=0, bytes_accessed=4 * w.size, transcendentals=0),
    )(x, w)


def head_columns(plan, w):
    layers, rows, triple = w.shape
    nf, nr, span, group = plan.nf, plan.nr, plan.span, plan.group
    ranks = [[plan.rank_of(f, r) for f in range(nf)] for r in range(nr)]
    x = lax.axis_index("replica")
    if not plan.cube:
        width = triple // 3
        v = w.reshape(layers, rows, 3, width)
        v = jnp.pad(v, ((0, 0), (0, 0), (0, 0), (0, group * span - width)))
        v = jnp.take(v.reshape(layers, rows, 3, group, span), jnp.array(ranks)[x], axis=3)
        return v.transpose(0, 3, 1, 2, 4).reshape(layers, nf, rows, 3 * span)
    return layered(
        functools.partial(head_columns_kernel, nf, ranks, span),
        x.astype(jnp.int32).reshape(1),
        w,
        3 * span,
        nf,
        [pltpu.VMEM((rows, 3 * group * span), F32)],
    )


def unit_columns(plan, w, piece, piece_rows):
    layers, rows, _ = w.shape
    nz, nf, nr = plan.nz, plan.nf, plan.nr
    x = lax.axis_index("replica")
    if not plan.cube:
        v = w.reshape(layers, rows, nz, nf, nr, piece)
        v = lax.dynamic_index_in_dim(v, x, 4, keepdims=False)
        v = jnp.pad(v, ((0, 0),) * 4 + ((0, piece_rows - piece),))
        return v.transpose(0, 3, 1, 2, 4).reshape(layers, nf, rows, nz * piece_rows)
    return layered(
        functools.partial(unit_columns_kernel, nz, nf, nr, piece, piece_rows),
        x.astype(jnp.int32).reshape(1),
        w,
        nz * piece_rows,
        nf,
        [],
    )


def stacked(pairs, block):
    for i, pair in enumerate(pairs):
        for core in range(2):
            block[4 * core + i] = pair[core]


def heads_back_kernel(group, span, src_ref, *refs):
    out, wide, v_ref = refs[-3:]
    stacked(refs[:4], v_ref)
    width = out.shape[2] // 3
    padded = group * span
    for rank in range(group):
        block = v_ref[src_ref[rank]].astype(F32)
        for i in range(3):
            wide[:, i * padded + rank * span : i * padded + (rank + 1) * span] = block[
                :, i * span : (i + 1) * span
            ]
    for i in range(3):
        out[0, :, i * width : (i + 1) * width] = wide[:, i * padded : i * padded + width]


def units_back_kernel(nz, nf, nr, piece, piece_rows, ranks, src_ref, *refs):
    out, v_ref = refs[-2:]
    stacked(refs[:4], v_ref)
    for f in range(nf):
        blocks = [v_ref[src_ref[ranks[f][r]]].astype(F32) for r in range(nr)]
        for z in range(nz):
            part = [block[:, z * piece_rows : z * piece_rows + piece] for block in blocks]
            start = (z * nf + f) * nr * piece
            out[0, :, start : start + nr * piece] = jnp.concatenate(part, axis=1)


def into_layer(kernel, plan, pairs, shape, layer, previous, scratch):
    operands = [plan.source().astype(jnp.int32), *pairs]
    in_specs = [pl.BlockSpec(v.shape, lambda i, s: (0, 0, 0)) for v in pairs]
    scratch = scratch + [pltpu.VMEM((8,) + pairs[0].shape[1:], BF)]
    aliases = {}
    if previous is not None:
        operands.append(previous)
        in_specs.append(pl.BlockSpec(memory_space=pl.ANY))
        aliases = {5: 0}
    return pl.pallas_call(
        kernel,
        grid_spec=pltpu.PrefetchScalarGridSpec(
            num_scalar_prefetch=1,
            grid=(1,),
            in_specs=in_specs,
            out_specs=pl.BlockSpec((1,) + shape[1:], lambda i, s: (layer, 0, 0)),
            scratch_shapes=scratch,
        ),
        out_shape=sds(shape, F32),
        input_output_aliases=aliases,
        compiler_params=pltpu.CompilerParams(vmem_limit_bytes=44 * 1024 * 1024),
        cost_estimate=pl.CostEstimate(flops=0, bytes_accessed=48 * pairs[0].size, transcendentals=0),
    )(*operands)


def rows_back_kernel(kept, x_ref, own, other, *refs):
    out = refs[-1]
    for x in range(2):

        @pl.when(x_ref[0] == x)
        def _():
            first, second = (own, other) if x == 0 else (other, own)
            first, second = (v[...].astype(F32)[:kept] for v in (first, second))
            if kept % 8:
                out[0] = jnp.concatenate([first, second])
            else:
                out[0, :kept, :] = first
                out[0, kept:, :] = second


def shards(
    plan,
    tokens,
    cotangent,
    segments,
    norm1_gain,
    norm1_shift,
    w_qkv,
    b_query,
    b_value,
    w_out,
    b_out,
    norm2_gain,
    norm2_shift,
    w_up,
    b_up,
    w_down,
    b_down,
):
    nz, nf, nr, group, span = plan.nz, plan.nf, plan.nr, plan.group, plan.span
    layers, own_rows, triple = w_qkv.shape
    width = triple // 3
    own_hidden = w_down.shape[1]
    piece = own_hidden // nr
    part = -(-own_rows // nr)
    part_rows = -(-part // 16) * 16
    piece_rows = -(-piece // 16) * 16
    units = nz * piece_rows
    length = tokens.shape[1]
    total = length * nz
    scale = 1.0 / math.sqrt(HD)
    fsdp = lax.axis_index("fsdp")
    replica = lax.axis_index("replica")
    seq = lax.axis_index("seq")
    rank = plan.rank()

    def down_of(down):
        down = lax.dynamic_slice_in_dim(down, replica * piece, piece, 0)
        return jnp.pad(down, ((0, piece_rows - piece), (0, 0)))

    def out_of(out):
        out = jnp.pad(out, ((0, nr * part + part_rows - own_rows), (0, 0)))
        out = lax.dynamic_slice_in_dim(out, replica * part, part_rows, 0)
        valid = lax.broadcasted_iota(jnp.int32, out.shape, 0)
        valid = (valid < part) & (valid + replica * part < own_rows)
        return jnp.where(valid, out, jnp.zeros_like(out))

    qkv_send = head_columns(plan, w_qkv)
    first = plan.exchange_fsdp(qkv_send[0]).reshape(nf * own_rows, 3 * span)
    both = plan.regroup(jnp.concatenate([tokens[0], cotangent[0]]))
    small = jnp.concatenate(
        [norm1_gain, norm1_shift, b_query, b_value, b_out, norm2_gain, norm2_shift, b_down, b_up],
        axis=1,
    )
    each_small = small.shape[1]
    small = small.reshape(-1)
    flat_rows = -(-small.shape[0] // 2048) * 16
    small = jnp.pad(small, (0, flat_rows * 128 - small.shape[0])).reshape(flat_rows, 128)
    small = plan.gather_owners(small)
    small = small.reshape(nz * nf, flat_rows * 128)[:, : layers * each_small]
    small = small.reshape(nz * nf, layers, each_small)

    codes = segments[0] * CODE + seq * length + jnp.arange(length, dtype=jnp.int32)
    codes = plan.gather_doubling(plan.regroup(codes[None]))

    outs = jnp.concatenate([out_of(w_out[layer]) for layer in range(layers)])
    first, both, qkv_send, w_up, w_down, outs, small, codes = lax.optimization_barrier(
        (first, both, qkv_send, w_up, w_down, outs, small, codes)
    )
    hidden = both[:length].astype(F32)
    grad = both[length:].astype(F32)
    up_send = unit_columns(plan, w_up, piece, piece_rows)
    prepared = []
    for layer in range(layers):
        qkv = first
        if layer:
            qkv = plan.exchange_fsdp(qkv_send[layer]).reshape(nf * own_rows, 3 * span)
        up = plan.exchange_fsdp(up_send[layer]).reshape(nf * own_rows, units)
        prepared.append((qkv, up, down_of(w_down[layer])))
    early = [prepared[0][1:], prepared[1:]]
    codes, early = lax.optimization_barrier((codes, early))
    prepared = [(first, *early[0])] + early[1]

    weights = []
    for layer, (qkv, up, down) in enumerate(prepared):
        qkv = gather_seq(qkv)
        if layer == 0:
            outs = gather_seq(outs).reshape(nz, layers, part_rows, width)
        up = gather_seq(up)
        down = gather_seq(down, lead=layer % 2 == 0)
        weights.append((qkv, up, down))

    source = plan.source()
    feature_heads = (source[:, None] * span + jnp.arange(span, dtype=jnp.int32)).reshape(-1)
    fs = jnp.array(plan.place, dtype=jnp.int32)[source]
    inner = jnp.arange(part_rows, dtype=jnp.int32)
    within = (fs % nr)[:, None, None] * part + inner
    feature_rows = (
        jnp.arange(nz, dtype=jnp.int32)[None, :, None] * (nf * own_rows)
        + (fs // nr)[:, None, None] * own_rows
        + within
    )
    feature_rows = jnp.where((inner < part) & (within < own_rows), feature_rows, -1).reshape(-1)
    select = (feature_heads[:, None] == feature_rows[None, :]).astype(BF)

    def vectors(layer):
        each = [
            small[:, layer, i * own_rows : (i + 1) * own_rows].reshape(width).astype(F32)
            for i in range(8)
        ]
        bias_up = small[:, layer, 8 * own_rows :].reshape(nz, nf, nr, piece)
        bias_up = lax.dynamic_index_in_dim(bias_up, fsdp, 1, keepdims=False)
        bias_up = lax.dynamic_index_in_dim(bias_up, replica, 1, keepdims=False)

        def mine(v):
            return lax.dynamic_slice_in_dim(
                jnp.pad(v, (0, group * span - width)), rank * span, span
            )

        bias_qkv = jnp.concatenate([mine(each[2]), jnp.zeros((span,), F32), mine(each[3])])
        bias_up = jnp.pad(bias_up, ((0, 0), (0, piece_rows - piece)))
        return each, bias_qkv, bias_up.reshape(units).astype(F32)

    vecs = [vectors(layer) for layer in range(layers)]

    def out_block(layer):
        return outs[:, layer].reshape(nz * part_rows, width)

    kept = []
    for layer in range(layers):
        qkv_w, up_w, down_w = weights[layer]
        (gain1, shift1, _, _, bias_out, gain2, shift2, bias_down), bias_qkv, bias_up = vecs[layer]
        unit1, inv1 = norm_parts(hidden)
        pieces = plan.gather_pieces(widen((unit1 * gain1 + shift1).astype(BF)))
        if layer == layers - 1:
            grad_pieces = plan.gather_pieces(widen(grad.astype(BF)))
            pieces, grad_pieces = lax.optimization_barrier((pieces, grad_pieces))
        normed, packed, lse, mixed = attend(
            plan, pieces, qkv_w, bias_qkv, codes, total, scale
        )
        if layer == 0:
            out_w = jnp.concatenate(plan.gather_pieces(out_block(0)))
        weights[layer] = qkv_w, out_w, up_w, down_w
        if layer < layers - 1:
            next_out = plan.gather_pieces(after(out_block(layer + 1), packed))
        mixed = jnp.concatenate(plan.exchange(mixed), axis=1)
        mixed = dot(mixed, select).astype(BF)
        block = nz * part_rows
        mixed_own = plan.exchange(
            jnp.concatenate([mixed[:, i * block : (i + 1) * block] for i in range(group)])
        )
        middle = hidden + (dot(mixed, out_w) + bias_out)
        unit2, inv2 = norm_parts(middle)
        pieces = plan.gather_pieces(widen((unit2 * gain2 + shift2).astype(BF)))
        if layer == layers - 1:
            normed_two, slope, activated = lift_units(plan, pieces, up_w, bias_up)
        else:
            normed_two, slope, activated, near, far = hidden_units(
                plan, pieces, up_w, bias_up, down_w
            )
        kept.append(
            (
                unit1,
                inv1,
                normed,
                packed,
                lse,
                jnp.concatenate(mixed_own),
                unit2,
                inv2,
                normed_two,
                slope,
                activated,
            )
        )
        if layer < layers - 1:
            hidden = middle + (plan.scatter_parts(near, far) + bias_down)
            out_w = jnp.concatenate(next_out)

    def late_up(up, layer):
        up = plan.to_owners(up)
        if plan.cube:
            ranks = [[plan.rank_of(f, r) for r in range(nr)] for f in range(nf)]
            return into_layer(
                functools.partial(units_back_kernel, nz, nf, nr, piece, piece_rows, ranks),
                plan,
                up,
                (layers, own_rows, nf * nz * nr * piece),
                layer,
                into_up,
                [],
            )
        up = jnp.stack([up[plan.back[m]] for m in range(group)])
        up = up.reshape(nf, nr, own_rows, nz, piece_rows)[..., :piece].transpose(2, 3, 0, 1, 4)
        up = up.reshape(1, own_rows, -1).astype(F32)
        return up if into_up is None else jnp.concatenate([up, into_up])

    def late_qkv(qkv, layer):
        qkv = plan.to_owners(qkv)
        if plan.cube:
            return into_layer(
                functools.partial(heads_back_kernel, group, span),
                plan,
                qkv,
                (layers, own_rows, triple),
                layer,
                into_qkv,
                [pltpu.VMEM((own_rows, 3 * group * span), F32)],
            )
        qkv = qkv.reshape(group, own_rows, 3, span).transpose(1, 2, 0, 3)
        qkv = qkv.reshape(own_rows, 3, group * span)[:, :, :width]
        qkv = qkv.reshape(1, own_rows, triple).astype(F32)
        return qkv if into_qkv is None else jnp.concatenate([qkv, into_qkv])

    def late_rows(v, rows, kept, layer, previous):
        if not plan.cube:
            v = lax.all_gather(v, "replica", axis=0, tiled=False)
            v = v[:, :kept].reshape(nr * kept, width)[None, :rows].astype(F32)
            return v if previous is None else jnp.concatenate([v, previous])
        operands = [v, plan.swap_x(v)]
        in_specs = [pl.BlockSpec(v.shape, lambda i, s: (0, 0))] * 2
        operands = [replica.astype(jnp.int32).reshape(1)] + operands
        aliases = {}
        if previous is not None:
            operands.append(previous)
            in_specs.append(pl.BlockSpec(memory_space=pl.ANY))
            aliases = {3: 0}
        return pl.pallas_call(
            functools.partial(rows_back_kernel, kept),
            grid_spec=pltpu.PrefetchScalarGridSpec(
                num_scalar_prefetch=1,
                grid=(1,),
                in_specs=in_specs,
                out_specs=pl.BlockSpec((1, rows, width), lambda i, s: (layer, 0, 0)),
            ),
            out_shape=sds((layers, rows, width), F32),
            input_output_aliases=aliases,
            compiler_params=pltpu.CompilerParams(vmem_limit_bytes=44 * 1024 * 1024),
            cost_estimate=pl.CostEstimate(
                flops=0, bytes_accessed=12 * v.size, transcendentals=0
            ),
        )(*operands)

    def late_down(down, layer):
        return late_rows(down, own_hidden, piece, layer, into_down)

    def late_out(out, layer):
        return late_rows(out, own_rows, part, layer, into_out)

    into_qkv = into_up = into_down = into_out = None
    smalls = [None] * layers
    late = None
    for layer in reversed(range(layers)):
        qkv_w, out_w, up_w, down_w = weights[layer]
        (gain1, _, _, _, _, gain2, _, _), _, _ = vecs[layer]
        unit1, inv1, normed, packed, lse, mixed, unit2, inv2, normed_two, slope, activated = kept[
            layer
        ]
        g_low = grad.astype(BF)
        grad_down = down_grad(plan, activated, grad_pieces, width)
        if late is not None:
            above = layer + 1
            out = scatter_seq(down_grad(plan, *late[2], width))
            into_up = late_up(late[0], above)
            into_down = late_down(late[1], above)
            into_out = late_out(out, above)
        if late is None:
            grad_pieces, grad_down = lax.optimization_barrier((grad_pieces, grad_down))
        down = scatter_seq(grad_down, lead=True)
        g_lift, grad_b_up, near, far = hidden_back(
            plan, grad_pieces, slope, down_w, up_w
        )
        grad_up = wgrad(plan, normed_two, g_lift)
        g_n2 = plan.scatter_parts(near, far)
        up = scatter_seq(grad_up).reshape(nf, own_rows, units)
        g_mid = grad + norm_pull(g_n2, unit2, inv2, gain2)
        g_att = g_mid.astype(BF)
        g_mixed = dot(g_att, out_w, 1, 1).astype(BF)
        g_mixed = dot(g_mixed, select, 1, 1).astype(BF)
        g_mixed = jnp.concatenate(
            [g_mixed[:, i * span : (i + 1) * span] for i in range(group)]
        )
        g_mixed = plan.exchange(g_mixed)
        att_pieces = plan.gather_pieces(widen(g_att))
        if late is None:
            near, far = lower_units(plan, after(activated, g_mixed), down_w)
            hidden = middle + (plan.scatter_parts(near, far) + bias_down)
            output = plan.regroup(hidden.astype(BF), back=True)
        g_packed, g_b, near, far = attend_back(
            plan, g_mixed, packed, lse, codes, qkv_w, total, scale
        )
        grad_qkv = wgrad(plan, normed, g_packed)
        g_n1 = plan.scatter_parts(near, far)
        qkv = scatter_seq(grad_qkv)
        qkv = qkv.reshape(nf, own_rows, 3 * span)
        if late is not None:
            into_qkv = late_qkv(after(late[3], g_n1), above)
        if layer == 0:
            into_up = late_up(up, layer)
            into_down = late_down(down, layer)
        late = (up, down, (after(mixed, g_n1), att_pieces), qkv)
        smalls[layer] = (
            jnp.sum(g_n1 * unit1, axis=0),
            jnp.sum(g_n1, axis=0),
            g_b,
            jnp.sum(g_att.astype(F32), axis=0),
            jnp.sum(g_n2 * unit2, axis=0),
            jnp.sum(g_n2, axis=0),
            jnp.sum(g_low.astype(F32), axis=0),
            grad_b_up,
        )
        grad = g_mid + norm_pull(g_n1, unit1, inv1, gain1)
        if layer:
            grad_pieces = plan.gather_pieces(widen(grad.astype(BF)))
    out = scatter_seq(down_grad(plan, *late[2], width))
    grad_tokens = plan.regroup(grad.astype(BF), back=True).astype(F32)
    output = after(output, grad).astype(F32)
    into_qkv = late_qkv(after(late[3], (into_up, into_down)), 0)
    into_out = late_out(out, 0)

    def scattered(layer):
        n1g, n1s, g_b, b_o, n2g, n2s, b_d, b_u = smalls[layer]

        def place(v):
            full = lax.dynamic_update_slice_in_dim(
                jnp.zeros((group * span,), F32), v, rank * span, 0
            )
            return full[:width]

        b_u = lax.dynamic_update_slice(
            jnp.zeros((nz, nf, nr, piece), F32),
            b_u.reshape(nz, 1, 1, piece_rows)[..., :piece],
            (0, fsdp, replica, 0),
        )
        rows = [n1g, n1s, place(g_b[:span]), place(g_b[2 * span :]), b_o, n2g, n2s, b_d]
        return jnp.concatenate(
            [v.reshape(nz * nf, own_rows) for v in rows] + [b_u.reshape(nz * nf, own_hidden)],
            axis=1,
        )

    flat = jnp.concatenate([scattered(layer) for layer in range(layers)], axis=1)
    wide = lanes(-(-flat.shape[1] // 2))
    flat = jnp.pad(flat, ((0, 0), (0, 2 * wide - flat.shape[1])))
    flat = plan.scatter_small(flat.reshape(nz, nf, 2, wide))
    flat = jnp.sum(plan.to_owners_small(flat), axis=0).reshape(-1)
    flat = flat[: layers * each_small].reshape(layers, each_small)
    vec = [flat[:, i * own_rows : (i + 1) * own_rows] for i in range(8)]
    return (
        output[None],
        grad_tokens[None],
        vec[0],
        vec[1],
        into_qkv,
        vec[2],
        vec[3],
        into_out,
        vec[4],
        vec[5],
        vec[6],
        into_up,
        flat[:, 8 * own_rows :],
        into_down,
        vec[7],
    )


def solution(mesh):
    plan = Plan(mesh)
    data = P(("fsdp", "replica"), "seq", None)
    vector = P(None, ("seq", "fsdp"))
    matrix = P(None, ("seq", "fsdp"), None)
    weights = (
        vector,
        vector,
        matrix,
        vector,
        vector,
        matrix,
        vector,
        vector,
        vector,
        matrix,
        vector,
        matrix,
        vector,
    )
    in_specs = (data, data, P(("fsdp", "replica"), "seq")) + weights
    out_specs = (data, data) + weights
    return jax.shard_map(
        functools.partial(shards, plan),
        mesh=mesh,
        in_specs=in_specs,
        out_specs=out_specs,
        check_vma=False,
    )
```

```python
import functools
import math

import jax
import jax.numpy as jnp
from jax import lax
from jax.experimental import pallas as pl
from jax.experimental.pallas import tpu as pltpu
from jax.sharding import PartitionSpec as P


HEADS = 25
HD = 64
BF = jnp.bfloat16
F32 = jnp.float32
ALL = ("seq", "fsdp", "replica")
GROUP = ("fsdp", "replica")
OWNERS = ("seq", "fsdp")
CODE = 65536
LOW = -1e30


def dot(a, b, ca=1, cb=0):
    return lax.dot_general(a, b, (((ca,), (cb,)), ((), ())), preferred_element_type=F32)


def norm_parts(v):
    mean = jnp.mean(v, axis=-1, keepdims=True)
    centred = v - mean
    spread = jnp.mean(centred * centred, axis=-1, keepdims=True)
    inv = lax.rsqrt(spread + 1e-05)
    return centred * inv, inv


def norm_pull(grad, unit, inv, gain):
    scaled = grad * gain
    first = jnp.mean(scaled, axis=-1, keepdims=True)
    second = jnp.mean(scaled * unit, axis=-1, keepdims=True)
    return inv * (scaled - first - unit * second)


def gelu_both(value):
    tanh = jnp.tanh(0.7978845608028654 * (value + 0.044715 * value * value * value))
    inner = 0.7978845608028654 * (1.0 + 3.0 * 0.044715 * value * value)
    half = 0.5 * (1.0 + tanh)
    return value * half, half + 0.5 * value * (1.0 - tanh * tanh) * inner


class Plan:
    def __init__(self, mesh):
        self.nz = mesh.shape["seq"]
        self.nf = mesh.shape["fsdp"]
        self.nr = mesh.shape["replica"]
        self.group = self.nf * self.nr
        self.cube = self.nf == 4 and self.nr == 2
        self.heads = 2 * -(-HEADS // (2 * self.group))
        self.span = self.heads * HD
        order = sorted(
            (self.rank_of(f, r), f * self.nr + r) for f in range(self.nf) for r in range(self.nr)
        )
        self.place = [member for _, member in order]
        self.back = [0] * self.group
        for rank, member in order:
            self.back[member] = rank

    def rank_of(self, f, r):
        half = self.group // 2
        if self.nf % 2:
            return f * self.nr + r
        return (f % 2) * half + (f // 2) * self.nr + r

    def rank(self):
        return self.rank_of(lax.axis_index("fsdp"), lax.axis_index("replica"))

    def regroup(self, v, back=False):
        nz = self.nz
        pairs = []
        for z in range(nz):
            for g in range(self.group):
                goal = g % nz
                slot = (g // nz) * nz + (z ^ goal if nz & (nz - 1) == 0 else z)
                pairs.append((z * self.group + self.place[g], goal * self.group + self.place[slot]))
        if back:
            pairs = [(there, here) for here, there in pairs]
        return lax.ppermute(v, ALL, pairs)

    def swap_core(self, v):
        return lax.ppermute(v, "fsdp", [(f, f ^ 1) for f in range(self.nf)])

    def swap_y(self, v):
        return lax.ppermute(v, "fsdp", [(f, f ^ 2) for f in range(self.nf)])

    def swap_x(self, v):
        return lax.ppermute(v, "replica", [(r, r ^ 1) for r in range(self.nr)])

    def swap_xy(self, v):
        pairs = [
            (f * self.nr + r, (f ^ 2) * self.nr + (r ^ 1))
            for f in range(self.nf)
            for r in range(self.nr)
        ]
        return lax.ppermute(v, GROUP, pairs)

    def source(self):
        base = jnp.arange(self.group, dtype=jnp.int32)
        return base ^ self.rank() if self.cube else base

    def gather_pieces(self, v):
        if not self.cube:
            full = lax.all_gather(v, GROUP, axis=0, tiled=False)
            return [full[member] for member in self.place]
        near = [v, self.swap_x(v), self.swap_y(v), self.swap_xy(v)]
        return near + [self.swap_core(piece) for piece in near]

    def gather_doubling(self, v):
        if not self.cube:
            return jnp.concatenate(self.gather_pieces(v))
        for swap in (self.swap_x, self.swap_y, self.swap_core):
            v = jnp.concatenate([v, swap(v)])
        return v

    def scatter_parts(self, near, far):
        if not self.cube:
            blocks = jnp.concatenate([near.astype(BF), far])
            rows = blocks.shape[0] // self.group
            blocks = blocks.reshape(self.group, rows, -1)[jnp.array(self.back)]
            blocks = blocks.reshape(self.group * rows, -1)
            return lax.psum_scatter(blocks, GROUP, scatter_dimension=0, tiled=True).astype(F32)
        rows, columns = near.shape[0] // 4, near.shape[1]
        own, to_x, to_y, to_xy = call(
            fold_kernel,
            [sds((rows, columns), F32)] + [sds((rows, lanes(columns)), BF)] * 3,
            [],
            0,
            [near, self.swap_core(far)],
        )
        parts = self.swap_xy(to_xy), self.swap_x(to_x), self.swap_y(to_y)
        parts = [part[:, :columns].astype(F32) for part in parts]
        return own + parts[0] + parts[1] + parts[2]

    def exchange(self, v):
        if not self.cube:
            v = v.reshape(self.group, -1, v.shape[1])[jnp.array(self.back)]
            v = lax.all_to_all(v, GROUP, split_axis=0, concat_axis=0, tiled=True)
            return [v[member] for member in self.place]
        rows = v.shape[0] // 8
        half = 4 * rows
        far = self.swap_core(v[half:])
        out = [[v[:rows], far[:rows]]]
        for i, swap in ((1, self.swap_x), (2, self.swap_y), (3, self.swap_xy)):
            both = swap(
                jnp.concatenate([v[i * rows : (i + 1) * rows], far[i * rows : (i + 1) * rows]])
            )
            out.append([both[:rows], both[rows:]])
        return [pair[0] for pair in out] + [pair[1] for pair in out]

    def flips(self, v):
        f = lax.axis_index("fsdp")
        v = v.reshape((2, 2) + v.shape[1:])
        v = jnp.where(f // 2 == 1, jnp.flip(v, 0), v)
        return jnp.where(f % 2 == 1, jnp.flip(v, 1), v)

    def gather_owners(self, v):
        if not self.cube or self.nz != 4:
            return lax.all_gather(v, OWNERS, axis=0, tiled=False)
        z, f = lax.axis_index("seq"), lax.axis_index("fsdp")
        far = [
            lax.ppermute(v, "seq", [(i, i ^ d) for i in range(4)]) if d else v for d in range(4)
        ]
        v = jnp.stack(far).reshape((2, 2) + v.shape)
        v = jnp.where(z // 2 == 1, jnp.flip(v, 0), v)
        v = jnp.where(z % 2 == 1, jnp.flip(v, 1), v)
        other = self.swap_core(v)
        v = jnp.stack([jnp.where(f % 2 == 0, v, other), jnp.where(f % 2 == 0, other, v)], axis=2)
        other = self.swap_y(v)
        v = jnp.stack([jnp.where(f // 2 == 0, v, other), jnp.where(f // 2 == 0, other, v)], axis=2)
        return v.reshape((16,) + v.shape[4:])

    def exchange_fsdp(self, v):
        if not self.cube:
            return lax.all_to_all(v, "fsdp", split_axis=0, concat_axis=0, tiled=True)
        shape = v.shape
        v = self.flips(v)
        both = jnp.stack([v[:, 0], self.swap_core(v[:, 1])], axis=1)
        return self.flips(jnp.stack([both[0], self.swap_y(both[1])]).reshape(shape)).reshape(shape)

    def scatter_small(self, v):
        if not self.cube or self.nz != 4:
            return lax.psum_scatter(v, "seq", scatter_dimension=0, tiled=False)
        z = lax.axis_index("seq")
        total = lax.dynamic_index_in_dim(v, z, 0, keepdims=False)
        for d in range(1, 4):
            other = lax.dynamic_index_in_dim(v, z ^ d, 0, keepdims=False)
            total = total + lax.ppermute(other, "seq", [(i, i ^ d) for i in range(4)])
        return total

    def to_owners_small(self, v):
        if not self.cube:
            v = lax.all_to_all(v, "fsdp", split_axis=0, concat_axis=0, tiled=True)
            v = lax.all_gather(v, "replica", axis=1, tiled=False)
            return jnp.stack([v[m // self.nr, m % self.nr] for m in self.place])
        v = self.flips(v)
        far = self.swap_core(v[:, 1])
        here = jnp.stack([v[0, 0], far[0]])
        there = jnp.stack([v[1, 0], far[1]])
        return jnp.stack(
            [here, self.swap_x(here), self.swap_y(there), self.swap_xy(there)], axis=1
        ).reshape((8,) + v.shape[2:])

    def to_owners(self, v):
        if not self.cube:
            return self.to_owners_small(v)
        nf, rows, columns = v.shape
        f = lax.axis_index("fsdp")
        pick = (f ^ jnp.arange(nf, dtype=jnp.int32)).astype(jnp.int32)
        pair = sds((2, rows, columns), BF)
        near, far = pl.pallas_call(
            pick_kernel,
            grid_spec=pltpu.PrefetchScalarGridSpec(
                num_scalar_prefetch=1,
                grid=(1,),
                in_specs=[pl.BlockSpec(v.shape, lambda i, s: (0, 0, 0))],
                out_specs=[pl.BlockSpec(pair.shape, lambda i, s: (0, 0, 0))] * 2,
            ),
            out_shape=[pair] * 2,
            compiler_params=pltpu.CompilerParams(vmem_limit_bytes=44 * 1024 * 1024),
        )(pick, v)
        here, there = call(pair_kernel, [pair] * 2, [], 0, [near, self.swap_core(far)])
        return [here, self.swap_x(here), self.swap_y(there), self.swap_xy(there)]


def pick_kernel(order, v, near, far):
    for y in range(2):
        near[y] = v[order[2 * y]]
        far[y] = v[order[2 * y + 1]]


def pair_kernel(near, far, here, there):
    for y, out in enumerate((here, there)):
        out[0] = near[y]
        out[1] = far[y]


def gather_seq(v, lead=False):
    if lead:
        return lax.all_gather(v[None], "seq", axis=1, tiled=True)[0]
    return lax.all_gather(v, "seq", axis=0, tiled=True)


def scatter_seq(v, lead=False):
    if lead:
        return lax.psum_scatter(v[None], "seq", scatter_dimension=1, tiled=True)[0]
    return lax.psum_scatter(v, "seq", scatter_dimension=0, tiled=True)


def call(kernel, outs, scratch, flops, operands, **more):
    params = pltpu.CompilerParams(vmem_limit_bytes=44 * 1024 * 1024)
    size = sum(math.prod(o.shape) * o.dtype.itemsize for o in list(outs) + list(operands))
    return pl.pallas_call(
        kernel,
        out_shape=tuple(outs),
        scratch_shapes=scratch,
        compiler_params=params,
        cost_estimate=pl.CostEstimate(
            flops=int(flops), bytes_accessed=int(size), transcendentals=0
        ),
        **more,
    )(*operands)


def lanes(columns):
    return -(-columns // 128) * 128


def widen(v):
    return jnp.pad(v, ((0, 0), (0, lanes(v.shape[1]) - v.shape[1])))


def sds(shape, dtype):
    return jax.ShapeDtypeStruct(shape, dtype)


def fold_kernel(near, far, own, to_x, to_y, to_xy):
    rows, columns = own.shape
    own[...] = near[:rows, :] + far[:rows, :columns].astype(F32)
    for i, out in ((1, to_x), (2, to_y), (3, to_xy)):
        at = slice(i * rows, (i + 1) * rows)
        out[:, :columns] = (near[at, :] + far[at, :columns].astype(F32)).astype(BF)


def wgrad_kernel(left, right, out):
    tall = out.shape[0]
    block = 256

    def body(i, carry):
        at = pl.ds(pl.multiple_of(i * block, block), block)
        out[at, :] = dot(left[:, at], right[...], 0, 0).astype(BF)
        return carry

    whole = tall // block
    lax.fori_loop(0, whole, body, 0)
    if tall % block:
        out[whole * block :, :] = dot(left[:, whole * block :], right[...], 0, 0).astype(BF)


def wgrad(plan, left, right):
    if not plan.cube:
        return dot(left, right, 0, 0).astype(BF)
    tall, width = left.shape[1], right.shape[1]
    return call(
        wgrad_kernel, [sds((tall, width), BF)], [], 2 * left.size * width, [left, right]
    )[0]


def after(v, other):
    return lax.optimization_barrier((v, other))[0]


def first_half(shape):
    return lax.broadcasted_iota(jnp.int32, shape, 1) < HD


def attend_kernel(count, total, span, scale, *refs):
    pieces = refs[:count]
    w, bias, code_col, code_row, full, packed, lse, mixed = refs[count:]
    rows = pieces[0].shape[0]
    for i, piece in enumerate(pieces):
        full[i * rows : (i + 1) * rows, :] = piece[:, : full.shape[1]]
    block = 2 * rows

    def project(i, carry):
        at = pl.ds(pl.multiple_of(i * block, block), block)
        packed[at, :] = (dot(full[at, :], w[...]) + bias[...]).astype(BF)
        return carry

    lax.fori_loop(0, count // 2, project, 0)
    blocks = total // rows
    left = first_half((rows, 2 * HD))
    lane = lax.broadcasted_iota(jnp.int32, (rows, 128), 1)

    def queries(i, carry):
        at = pl.ds(pl.multiple_of(i * rows, rows), rows)
        seq = i // blocks
        keys_at = pl.ds(pl.multiple_of(seq * total, total), total)
        code_q = code_col[at, :]
        code_k = code_row[pl.ds(seq, 1), :]
        allowed = (code_k <= code_q) & (code_k >= (code_q // CODE) * CODE)
        stats = jnp.zeros((rows, 128), F32)
        for pair in range(span // 128):
            q = packed[at, pair * 128 : pair * 128 + 128]
            k = packed[keys_at, span + pair * 128 : span + pair * 128 + 128]
            v = packed[keys_at, 2 * span + pair * 128 : 2 * span + pair * 128 + 128]
            both = []
            for side in range(2):
                own = left if side == 0 else ~left
                scores = dot(jnp.where(own, q, jnp.zeros_like(q)), k, 1, 1) * scale
                scores = jnp.where(allowed, scores, LOW)
                top = jnp.max(scores, axis=1, keepdims=True)
                expo = jnp.exp(scores - top)
                denom = jnp.sum(expo, axis=1, keepdims=True)
                probs = (expo * (1.0 / denom)).astype(BF)
                both.append(dot(probs, v))
                stats = jnp.where(lane == 2 * pair + side, top + jnp.log(denom), stats)
            mixed[at, pair * 128 : pair * 128 + 128] = jnp.where(left, both[0], both[1]).astype(BF)
        lse[:, at] = stats.T[: lse.shape[0], :]
        return carry

    lax.fori_loop(0, count, queries, 0)


def attend(plan, pieces, w, bias, codes, total, scale):
    rows, width = pieces[0].shape[0], w.shape[0]
    count, span = plan.group, plan.span
    if not plan.cube:
        full = jnp.concatenate(pieces)[:, :width]
        packed = (dot(full, w) + bias).astype(BF)
        q, k, v = (
            packed[:, i * span : (i + 1) * span].reshape(-1, total, plan.heads, HD)
            for i in range(3)
        )
        allowed = mask_of(codes, total)
        scores = jnp.einsum("sqhd,skhd->shqk", q, k, preferred_element_type=F32) * scale
        scores = jnp.where(allowed[:, None], scores, LOW)
        top = jnp.max(scores, axis=-1, keepdims=True)
        expo = jnp.exp(scores - top)
        denom = jnp.sum(expo, axis=-1, keepdims=True)
        probs = (expo / denom).astype(BF)
        mixed = jnp.einsum("shqk,skhd->sqhd", probs, v, preferred_element_type=F32)
        return full, packed, top + jnp.log(denom), mixed.reshape(-1, span).astype(BF)
    tall = count * rows
    return call(
        functools.partial(attend_kernel, count, total, span, scale),
        [
            sds((tall, width), BF),
            sds((tall, 3 * span), BF),
            sds((8, tall), F32),
            sds((tall, span), BF),
        ],
        [],
        2 * tall * width * 3 * span + 8 * tall * total * span,
        [*pieces, w, bias[None], codes.reshape(-1, 1), codes.reshape(-1, total)],
    )


def mask_of(codes, total):
    code = codes.reshape(-1, total)
    low = (code // CODE) * CODE
    return (code[:, None, :] <= code[:, :, None]) & (code[:, None, :] >= low[:, :, None])


def attend_back_kernel(count, total, span, scale, *refs):
    pieces = refs[:count]
    packed, lse, code_col, code_row, w, g_packed, g_bias, near, far, gm, g_k, g_v = refs[count:]
    rows = pieces[0].shape[0]
    for i, piece in enumerate(pieces):
        gm[i * rows : (i + 1) * rows, :] = piece[...]
    blocks = total // rows
    left = first_half((rows, 2 * HD))

    def sequence(seq, carry):
        keys_at = pl.ds(pl.multiple_of(seq * total, total), total)
        code_k = code_col[keys_at, :]
        for pair in range(span // 128):
            lanes = slice(pair * 128, pair * 128 + 128)
            k_lanes = slice(span + pair * 128, span + pair * 128 + 128)
            v_lanes = slice(2 * span + pair * 128, 2 * span + pair * 128 + 128)
            k = packed[keys_at, k_lanes]
            v = packed[keys_at, v_lanes]
            g_k[...] = jnp.zeros_like(g_k)
            g_v[...] = jnp.zeros_like(g_v)

            def queries(i, inner):
                at = pl.ds(pl.multiple_of(seq * total + i * rows, rows), rows)
                code_q = code_row[pl.ds(seq * blocks + i, 1), :]
                allowed = (code_k <= code_q) & (code_k >= (code_q // CODE) * CODE)
                q = packed[at, lanes]
                g = gm[at, lanes]
                both = []
                for side in range(2):
                    own = left if side == 0 else ~left
                    q_own = jnp.where(own, q, jnp.zeros_like(q))
                    g_own = jnp.where(own, g, jnp.zeros_like(g))
                    scores = dot(k, q_own, 1, 1) * scale
                    row = 2 * pair + side
                    probs = jnp.exp(jnp.where(allowed, scores, LOW) - lse[row : row + 1, at])
                    g_probs = dot(v, g_own, 1, 1)
                    each = jnp.sum(g_probs * probs, axis=0, keepdims=True)
                    g_scores = (probs * (g_probs - each)).astype(BF)
                    g_v[...] += dot(probs.astype(BF), g_own)
                    g_k[...] += dot(g_scores, q_own)
                    both.append(dot(g_scores, k, 0, 0))
                g_packed[at, lanes] = (jnp.where(left, both[0], both[1]) * scale).astype(BF)
                return inner

            lax.fori_loop(0, blocks, queries, 0)
            g_packed[keys_at, k_lanes] = (g_k[...] * scale).astype(BF)
            g_packed[keys_at, v_lanes] = g_v[...].astype(BF)
        return carry

    lax.fori_loop(0, count // blocks, sequence, 0)
    g_bias[...] = jnp.sum(g_packed[...].astype(F32), axis=0, keepdims=True)
    spread_out(g_packed, w, near, far, 2 * rows)


def spread_out(left, right, near, far, block):
    half = near.shape[0]

    def first(i, carry):
        at = pl.ds(pl.multiple_of(i * block, block), block)
        near[at, :] = dot(left[at, :], right[...], 1, 1)
        return carry

    def second(i, carry):
        at = pl.ds(pl.multiple_of(i * block, block), block)
        far[at, : near.shape[1]] = dot(
            left[pl.ds(pl.multiple_of(half + i * block, block), block), :], right[...], 1, 1
        ).astype(BF)
        return carry

    lax.fori_loop(0, half // block, first, 0)
    lax.fori_loop(0, half // block, second, 0)


def halves(v):
    half = v.shape[0] // 2
    return v[:half], v[half:].astype(BF)


def attend_back(plan, pieces, packed, lse, codes, w, total, scale):
    count, span = plan.group, plan.span
    rows = pieces[0].shape[0]
    width = w.shape[0]
    if not plan.cube:
        q, k, v = (
            packed[:, i * span : (i + 1) * span].reshape(-1, total, plan.heads, HD)
            for i in range(3)
        )
        gm = jnp.concatenate(pieces).reshape(-1, total, plan.heads, HD)
        allowed = mask_of(codes, total)
        scores = jnp.einsum("sqhd,skhd->shqk", q, k, preferred_element_type=F32) * scale
        probs = jnp.exp(jnp.where(allowed[:, None], scores, LOW) - lse)
        g_probs = jnp.einsum("sqhd,skhd->shqk", gm, v, preferred_element_type=F32)
        g_v = jnp.einsum("shqk,sqhd->skhd", probs.astype(BF), gm, preferred_element_type=F32)
        row = jnp.sum(g_probs * probs, axis=-1, keepdims=True)
        g_s = (probs * (g_probs - row)).astype(BF)
        g_q = jnp.einsum("shqk,skhd->sqhd", g_s, k, preferred_element_type=F32) * scale
        g_k = jnp.einsum("shqk,sqhd->skhd", g_s, q, preferred_element_type=F32) * scale
        g_packed = jnp.concatenate(
            [u.reshape(-1, span).astype(BF) for u in (g_q, g_k, g_v)], axis=1
        )
        near, far = halves(dot(g_packed, w, 1, 1))
        return g_packed, jnp.sum(g_packed.astype(F32), axis=0), near, far
    tall = count * rows
    g_packed, g_bias, near, far = call(
        functools.partial(attend_back_kernel, count, total, span, scale),
        [
            sds((tall, 3 * span), BF),
            sds((1, 3 * span), F32),
            sds((tall // 2, width), F32),
            sds((tall // 2, lanes(width)), BF),
        ],
        [pltpu.VMEM((tall, span), BF)] + [pltpu.VMEM((total, 128), F32)] * 2,
        2 * tall * width * 3 * span + 20 * tall * total * span,
        [*pieces, packed, lse, codes.reshape(-1, 1), codes.reshape(-1, rows), w],
    )
    return g_packed, g_bias[0], near, far


def hidden_kernel(count, *refs):
    pieces = refs[:count]
    up, bias, down, full, slope, activated, near, far = refs[count:]
    rows = pieces[0].shape[0]
    for i, piece in enumerate(pieces):
        full[i * rows : (i + 1) * rows, :] = piece[:, : full.shape[1]]
    block = 2 * rows
    half = near.shape[0]

    def lift(at):
        value, pull = gelu_both(dot(full[at, :], up[...]) + bias[...])
        value = value.astype(BF)
        activated[at, :] = value
        slope[at, :] = pull.astype(BF)
        return dot(value, down[...])

    def first(i, carry):
        at = pl.ds(pl.multiple_of(i * block, block), block)
        near[at, :] = lift(at)
        return carry

    def second(i, carry):
        at = pl.ds(pl.multiple_of(i * block, block), block)
        out = lift(pl.ds(pl.multiple_of(half + i * block, block), block))
        far[at, : near.shape[1]] = out.astype(BF)
        return carry

    lax.fori_loop(0, half // block, first, 0)
    lax.fori_loop(0, half // block, second, 0)


def lift_kernel(count, *refs):
    pieces = refs[:count]
    up, bias, full, slope, activated = refs[count:]
    rows = pieces[0].shape[0]
    for i, piece in enumerate(pieces):
        full[i * rows : (i + 1) * rows, :] = piece[:, : full.shape[1]]
    block = 2 * rows

    def lift(i, carry):
        at = pl.ds(pl.multiple_of(i * block, block), block)
        value, pull = gelu_both(dot(full[at, :], up[...]) + bias[...])
        activated[at, :] = value.astype(BF)
        slope[at, :] = pull.astype(BF)
        return carry

    lax.fori_loop(0, count // 2, lift, 0)


def lift_units(plan, pieces, up, bias):
    rows, width = pieces[0].shape[0], up.shape[0]
    if not plan.cube:
        full = jnp.concatenate(pieces)[:, :width]
        value, pull = gelu_both(dot(full, up) + bias)
        return full, pull.astype(BF), value.astype(BF)
    tall, units = plan.group * rows, up.shape[1]
    return call(
        functools.partial(lift_kernel, plan.group),
        [sds((tall, width), BF), sds((tall, units), BF), sds((tall, units), BF)],
        [],
        2 * tall * width * units,
        [*pieces, up, bias[None]],
    )


def lower_kernel(block, left, right, near, far):
    half, width = near.shape

    def first(i, carry):
        at = pl.ds(pl.multiple_of(i * block, block), block)
        near[at, :] = dot(left[at, :], right[...])
        return carry

    def second(i, carry):
        at = pl.ds(pl.multiple_of(i * block, block), block)
        rows = left[pl.ds(pl.multiple_of(half + i * block, block), block), :]
        far[at, :width] = dot(rows, right[...]).astype(BF)
        return carry

    lax.fori_loop(0, half // block, first, 0)
    lax.fori_loop(0, half // block, second, 0)


def lower_units(plan, activated, down):
    tall, width = activated.shape[0], down.shape[1]
    if not plan.cube:
        return halves(dot(activated, down))
    return call(
        functools.partial(lower_kernel, 2 * (tall // plan.group)),
        [sds((tall // 2, width), F32), sds((tall // 2, lanes(width)), BF)],
        [],
        2 * activated.size * width,
        [activated, down],
    )


def hidden_units(plan, pieces, up, bias, down):
    rows, width = pieces[0].shape[0], up.shape[0]
    if not plan.cube:
        full = jnp.concatenate(pieces)[:, :width]
        value, pull = gelu_both(dot(full, up) + bias)
        value = value.astype(BF)
        return (full, pull.astype(BF), value) + halves(dot(value, down))
    tall, units = plan.group * rows, up.shape[1]
    return call(
        functools.partial(hidden_kernel, plan.group),
        [
            sds((tall, width), BF),
            sds((tall, units), BF),
            sds((tall, units), BF),
            sds((tall // 2, width), F32),
            sds((tall // 2, lanes(width)), BF),
        ],
        [],
        4 * tall * width * units,
        [*pieces, up, bias[None], down],
    )


def hidden_back_kernel(count, *refs):
    pieces = refs[:count]
    slope, down, up, g_lift, g_bias, near, far, full = refs[count:]
    rows = pieces[0].shape[0]
    for i, piece in enumerate(pieces):
        full[i * rows : (i + 1) * rows, :] = piece[:, : full.shape[1]]
    block = 2 * rows

    def pull(i, carry):
        at = pl.ds(pl.multiple_of(i * block, block), block)
        g_lift[at, :] = (dot(full[at, :], down[...], 1, 1) * slope[at, :].astype(F32)).astype(BF)
        return carry

    lax.fori_loop(0, count // 2, pull, 0)
    spread_out(g_lift, up, near, far, block)
    g_bias[...] = jnp.sum(g_lift[...].astype(F32), axis=0, keepdims=True)


def hidden_back(plan, pieces, slope, down, up):
    rows, width = pieces[0].shape[0], up.shape[0]
    if not plan.cube:
        full = jnp.concatenate(pieces)[:, :width]
        g_lift = (dot(full, down, 1, 1) * slope.astype(F32)).astype(BF)
        return (g_lift, jnp.sum(g_lift.astype(F32), axis=0)) + halves(dot(g_lift, up, 1, 1))
    tall, units = plan.group * rows, up.shape[1]
    g_lift, g_bias, near, far = call(
        functools.partial(hidden_back_kernel, plan.group),
        [
            sds((tall, units), BF),
            sds((1, units), F32),
            sds((tall // 2, width), F32),
            sds((tall // 2, lanes(width)), BF),
        ],
        [pltpu.VMEM((tall, width), BF)],
        4 * tall * width * units,
        [*pieces, slope, down, up],
    )
    return g_lift, g_bias[0], near, far


def down_grad_kernel(count, *refs):
    left, out, full = refs[count:]
    rows = refs[0].shape[0]
    for i, piece in enumerate(refs[:count]):
        full[i * rows : (i + 1) * rows, :] = piece[:, : full.shape[1]]
    wgrad_kernel(left, full, out)


def down_grad(plan, left, pieces, width):
    if not plan.cube:
        return dot(left, jnp.concatenate(pieces)[:, :width], 0, 0).astype(BF)
    tall, units = left.shape
    return call(
        functools.partial(down_grad_kernel, plan.group),
        [sds((units, width), BF)],
        [pltpu.VMEM((tall, width), BF)],
        2 * left.size * width,
        [*pieces, left],
    )[0]


def head_columns_kernel(nf, ranks, span, x_ref, w_ref, out, wide):
    width = w_ref.shape[2] // 3
    padded = wide.shape[1] // 3
    w = w_ref[0].astype(F32)
    for i in range(3):
        wide[:, i * padded : i * padded + width] = w[:, i * width : (i + 1) * width]
        if padded > width:
            wide[:, i * padded + width : (i + 1) * padded] = jnp.zeros(
                (wide.shape[0], padded - width), F32
            )
    for x, row in enumerate(ranks):

        @pl.when(x_ref[0] == x)
        def _():
            for f in range(nf):
                for i in range(3):
                    start = i * padded + row[f] * span
                    out[0, f, :, i * span : (i + 1) * span] = wide[:, start : start + span].astype(
                        BF
                    )


def unit_columns_kernel(nz, nf, nr, piece, piece_rows, x_ref, w_ref, out):
    w = w_ref[0].astype(F32)
    for x in range(nr):

        @pl.when(x_ref[0] == x)
        def _():
            for f in range(nf):
                part = []
                for z in range(nz):
                    start = ((z * nf + f) * nr + x) * piece
                    part.append(w[:, start : start + piece])
                    if piece_rows > piece:
                        part.append(jnp.zeros((w.shape[0], piece_rows - piece), F32))
                out[0, f] = jnp.concatenate(part, axis=1).astype(BF)


def layered(kernel, x, w, columns, nf, scratch):
    layers, rows, full = w.shape
    return pl.pallas_call(
        kernel,
        grid_spec=pltpu.PrefetchScalarGridSpec(
            num_scalar_prefetch=1,
            grid=(layers,),
            in_specs=[pl.BlockSpec((1, rows, full), lambda i, s: (i, 0, 0))],
            out_specs=pl.BlockSpec((1, nf, rows, columns), lambda i, s: (i, 0, 0, 0)),
            scratch_shapes=scratch,
        ),
        out_shape=sds((layers, nf, rows, columns), BF),
        compiler_params=pltpu.CompilerParams(vmem_limit_bytes=44 * 1024 * 1024),
        cost_estimate=pl.CostEstimate(flops=0, bytes_accessed=4 * w.size, transcendentals=0),
    )(x, w)


def head_columns(plan, w):
    layers, rows, triple = w.shape
    nf, nr, span, group = plan.nf, plan.nr, plan.span, plan.group
    ranks = [[plan.rank_of(f, r) for f in range(nf)] for r in range(nr)]
    x = lax.axis_index("replica")
    if not plan.cube:
        width = triple // 3
        v = w.reshape(layers, rows, 3, width)
        v = jnp.pad(v, ((0, 0), (0, 0), (0, 0), (0, group * span - width)))
        v = jnp.take(v.reshape(layers, rows, 3, group, span), jnp.array(ranks)[x], axis=3)
        return v.transpose(0, 3, 1, 2, 4).reshape(layers, nf, rows, 3 * span)
    return layered(
        functools.partial(head_columns_kernel, nf, ranks, span),
        x.astype(jnp.int32).reshape(1),
        w,
        3 * span,
        nf,
        [pltpu.VMEM((rows, 3 * group * span), F32)],
    )


def unit_columns(plan, w, piece, piece_rows):
    layers, rows, _ = w.shape
    nz, nf, nr = plan.nz, plan.nf, plan.nr
    x = lax.axis_index("replica")
    if not plan.cube:
        v = w.reshape(layers, rows, nz, nf, nr, piece)
        v = lax.dynamic_index_in_dim(v, x, 4, keepdims=False)
        v = jnp.pad(v, ((0, 0),) * 4 + ((0, piece_rows - piece),))
        return v.transpose(0, 3, 1, 2, 4).reshape(layers, nf, rows, nz * piece_rows)
    return layered(
        functools.partial(unit_columns_kernel, nz, nf, nr, piece, piece_rows),
        x.astype(jnp.int32).reshape(1),
        w,
        nz * piece_rows,
        nf,
        [],
    )


def stacked(pairs, block):
    for i, pair in enumerate(pairs):
        for core in range(2):
            block[4 * core + i] = pair[core]


def heads_back_kernel(group, span, src_ref, *refs):
    out, wide, v_ref = refs[-3:]
    stacked(refs[:4], v_ref)
    width = out.shape[2] // 3
    padded = group * span
    for rank in range(group):
        block = v_ref[src_ref[rank]].astype(F32)
        for i in range(3):
            wide[:, i * padded + rank * span : i * padded + (rank + 1) * span] = block[
                :, i * span : (i + 1) * span
            ]
    for i in range(3):
        out[0, :, i * width : (i + 1) * width] = wide[:, i * padded : i * padded + width]


def units_back_kernel(nz, nf, nr, piece, piece_rows, ranks, src_ref, *refs):
    out, v_ref = refs[-2:]
    stacked(refs[:4], v_ref)
    for f in range(nf):
        blocks = [v_ref[src_ref[ranks[f][r]]].astype(F32) for r in range(nr)]
        for z in range(nz):
            part = [block[:, z * piece_rows : z * piece_rows + piece] for block in blocks]
            start = (z * nf + f) * nr * piece
            out[0, :, start : start + nr * piece] = jnp.concatenate(part, axis=1)


def into_layer(kernel, plan, pairs, shape, layer, previous, scratch):
    operands = [plan.source().astype(jnp.int32), *pairs]
    in_specs = [pl.BlockSpec(v.shape, lambda i, s: (0, 0, 0)) for v in pairs]
    scratch = scratch + [pltpu.VMEM((8,) + pairs[0].shape[1:], BF)]
    aliases = {}
    if previous is not None:
        operands.append(previous)
        in_specs.append(pl.BlockSpec(memory_space=pl.ANY))
        aliases = {5: 0}
    return pl.pallas_call(
        kernel,
        grid_spec=pltpu.PrefetchScalarGridSpec(
            num_scalar_prefetch=1,
            grid=(1,),
            in_specs=in_specs,
            out_specs=pl.BlockSpec((1,) + shape[1:], lambda i, s: (layer, 0, 0)),
            scratch_shapes=scratch,
        ),
        out_shape=sds(shape, F32),
        input_output_aliases=aliases,
        compiler_params=pltpu.CompilerParams(vmem_limit_bytes=44 * 1024 * 1024),
        cost_estimate=pl.CostEstimate(flops=0, bytes_accessed=48 * pairs[0].size, transcendentals=0),
    )(*operands)


def rows_back_kernel(kept, x_ref, own, other, *refs):
    out = refs[-1]
    for x in range(2):

        @pl.when(x_ref[0] == x)
        def _():
            first, second = (own, other) if x == 0 else (other, own)
            first, second = (v[...].astype(F32)[:kept] for v in (first, second))
            if kept % 8:
                out[0] = jnp.concatenate([first, second])
            else:
                out[0, :kept, :] = first
                out[0, kept:, :] = second


def shards(
    plan,
    tokens,
    cotangent,
    segments,
    norm1_gain,
    norm1_shift,
    w_qkv,
    b_query,
    b_value,
    w_out,
    b_out,
    norm2_gain,
    norm2_shift,
    w_up,
    b_up,
    w_down,
    b_down,
):
    nz, nf, nr, group, span = plan.nz, plan.nf, plan.nr, plan.group, plan.span
    layers, own_rows, triple = w_qkv.shape
    width = triple // 3
    own_hidden = w_down.shape[1]
    piece = own_hidden // nr
    part = -(-own_rows // nr)
    part_rows = -(-part // 16) * 16
    piece_rows = -(-piece // 16) * 16
    units = nz * piece_rows
    length = tokens.shape[1]
    total = length * nz
    scale = 1.0 / math.sqrt(HD)
    fsdp = lax.axis_index("fsdp")
    replica = lax.axis_index("replica")
    seq = lax.axis_index("seq")
    rank = plan.rank()

    def down_of(down):
        down = lax.dynamic_slice_in_dim(down, replica * piece, piece, 0)
        return jnp.pad(down, ((0, piece_rows - piece), (0, 0)))

    def out_of(out):
        out = jnp.pad(out, ((0, nr * part + part_rows - own_rows), (0, 0)))
        out = lax.dynamic_slice_in_dim(out, replica * part, part_rows, 0)
        valid = lax.broadcasted_iota(jnp.int32, out.shape, 0)
        valid = (valid < part) & (valid + replica * part < own_rows)
        return jnp.where(valid, out, jnp.zeros_like(out))

    qkv_send = head_columns(plan, w_qkv)
    first = plan.exchange_fsdp(qkv_send[0]).reshape(nf * own_rows, 3 * span)
    both = plan.regroup(jnp.concatenate([tokens[0], cotangent[0]]))
    small = jnp.concatenate(
        [norm1_gain, norm1_shift, b_query, b_value, b_out, norm2_gain, norm2_shift, b_down, b_up],
        axis=1,
    )
    each_small = small.shape[1]
    small = small.reshape(-1)
    flat_rows = -(-small.shape[0] // 2048) * 16
    small = jnp.pad(small, (0, flat_rows * 128 - small.shape[0])).reshape(flat_rows, 128)
    small = plan.gather_owners(small)
    small = small.reshape(nz * nf, flat_rows * 128)[:, : layers * each_small]
    small = small.reshape(nz * nf, layers, each_small)

    codes = segments[0] * CODE + seq * length + jnp.arange(length, dtype=jnp.int32)
    codes = plan.gather_doubling(plan.regroup(codes[None]))

    outs = jnp.concatenate([out_of(w_out[layer]) for layer in range(layers)])
    first, both, qkv_send, w_up, w_down, outs, small, codes = lax.optimization_barrier(
        (first, both, qkv_send, w_up, w_down, outs, small, codes)
    )
    hidden = both[:length].astype(F32)
    grad = both[length:].astype(F32)
    up_send = unit_columns(plan, w_up, piece, piece_rows)
    prepared = []
    for layer in range(layers):
        qkv = first
        if layer:
            qkv = plan.exchange_fsdp(qkv_send[layer]).reshape(nf * own_rows, 3 * span)
        up = plan.exchange_fsdp(up_send[layer]).reshape(nf * own_rows, units)
        prepared.append((qkv, up, down_of(w_down[layer])))
    early = [prepared[0][1:], prepared[1:]]
    codes, early = lax.optimization_barrier((codes, early))
    prepared = [(first, *early[0])] + early[1]

    weights = []
    for layer, (qkv, up, down) in enumerate(prepared):
        qkv = gather_seq(qkv)
        if layer == 0:
            outs = gather_seq(outs).reshape(nz, layers, part_rows, width)
        up = gather_seq(up)
        down = gather_seq(down, lead=layer % 2 == 0)
        weights.append((qkv, up, down))

    source = plan.source()
    feature_heads = (source[:, None] * span + jnp.arange(span, dtype=jnp.int32)).reshape(-1)
    fs = jnp.array(plan.place, dtype=jnp.int32)[source]
    inner = jnp.arange(part_rows, dtype=jnp.int32)
    within = (fs % nr)[:, None, None] * part + inner
    feature_rows = (
        jnp.arange(nz, dtype=jnp.int32)[None, :, None] * (nf * own_rows)
        + (fs // nr)[:, None, None] * own_rows
        + within
    )
    feature_rows = jnp.where((inner < part) & (within < own_rows), feature_rows, -1).reshape(-1)
    select = (feature_heads[:, None] == feature_rows[None, :]).astype(BF)

    def vectors(layer):
        each = [
            small[:, layer, i * own_rows : (i + 1) * own_rows].reshape(width).astype(F32)
            for i in range(8)
        ]
        bias_up = small[:, layer, 8 * own_rows :].reshape(nz, nf, nr, piece)
        bias_up = lax.dynamic_index_in_dim(bias_up, fsdp, 1, keepdims=False)
        bias_up = lax.dynamic_index_in_dim(bias_up, replica, 1, keepdims=False)

        def mine(v):
            return lax.dynamic_slice_in_dim(
                jnp.pad(v, (0, group * span - width)), rank * span, span
            )

        bias_qkv = jnp.concatenate([mine(each[2]), jnp.zeros((span,), F32), mine(each[3])])
        bias_up = jnp.pad(bias_up, ((0, 0), (0, piece_rows - piece)))
        return each, bias_qkv, bias_up.reshape(units).astype(F32)

    vecs = [vectors(layer) for layer in range(layers)]

    def out_block(layer):
        return outs[:, layer].reshape(nz * part_rows, width)

    kept = []
    for layer in range(layers):
        qkv_w, up_w, down_w = weights[layer]
        (gain1, shift1, _, _, bias_out, gain2, shift2, bias_down), bias_qkv, bias_up = vecs[layer]
        unit1, inv1 = norm_parts(hidden)
        pieces = plan.gather_pieces(widen((unit1 * gain1 + shift1).astype(BF)))
        if layer == 0:
            grad_pieces = plan.gather_pieces(widen(after(grad.astype(BF), pieces)))
        normed, packed, lse, mixed = attend(plan, pieces, qkv_w, bias_qkv, codes, total, scale)
        out_w = out_block(layer)
        out_w = jnp.concatenate(plan.gather_pieces(after(out_w, pieces) if layer else out_w))
        weights[layer] = qkv_w, out_w, up_w, down_w
        mixed = jnp.concatenate(plan.exchange(mixed), axis=1)
        mixed = dot(mixed, select).astype(BF)
        block = nz * part_rows
        mixed_own = plan.exchange(
            jnp.concatenate([mixed[:, i * block : (i + 1) * block] for i in range(group)])
        )
        middle = hidden + (dot(mixed, out_w) + bias_out)
        unit2, inv2 = norm_parts(middle)
        pieces = plan.gather_pieces(widen((unit2 * gain2 + shift2).astype(BF)))
        if layer == layers - 1:
            normed_two, slope, activated = lift_units(plan, pieces, up_w, bias_up)
        else:
            normed_two, slope, activated, near, far = hidden_units(
                plan, pieces, up_w, bias_up, down_w
            )
        kept.append(
            (
                unit1,
                inv1,
                normed,
                packed,
                lse,
                jnp.concatenate(mixed_own),
                unit2,
                inv2,
                normed_two,
                slope,
                activated,
            )
        )
        if layer < layers - 1:
            hidden = middle + (plan.scatter_parts(near, far) + bias_down)

    def late_up(up, layer):
        up = plan.to_owners(up)
        if plan.cube:
            ranks = [[plan.rank_of(f, r) for r in range(nr)] for f in range(nf)]
            return into_layer(
                functools.partial(units_back_kernel, nz, nf, nr, piece, piece_rows, ranks),
                plan,
                up,
                (layers, own_rows, nf * nz * nr * piece),
                layer,
                into_up,
                [],
            )
        up = jnp.stack([up[plan.back[m]] for m in range(group)])
        up = up.reshape(nf, nr, own_rows, nz, piece_rows)[..., :piece].transpose(2, 3, 0, 1, 4)
        up = up.reshape(1, own_rows, -1).astype(F32)
        return up if into_up is None else jnp.concatenate([up, into_up])

    def late_qkv(qkv, layer):
        qkv = plan.to_owners(qkv)
        if plan.cube:
            return into_layer(
                functools.partial(heads_back_kernel, group, span),
                plan,
                qkv,
                (layers, own_rows, triple),
                layer,
                into_qkv,
                [pltpu.VMEM((own_rows, 3 * group * span), F32)],
            )
        qkv = qkv.reshape(group, own_rows, 3, span).transpose(1, 2, 0, 3)
        qkv = qkv.reshape(own_rows, 3, group * span)[:, :, :width]
        qkv = qkv.reshape(1, own_rows, triple).astype(F32)
        return qkv if into_qkv is None else jnp.concatenate([qkv, into_qkv])

    def late_rows(v, rows, kept, layer, previous):
        if not plan.cube:
            v = lax.all_gather(v, "replica", axis=0, tiled=False)
            v = v[:, :kept].reshape(nr * kept, width)[None, :rows].astype(F32)
            return v if previous is None else jnp.concatenate([v, previous])
        operands = [v, plan.swap_x(v)]
        in_specs = [pl.BlockSpec(v.shape, lambda i, s: (0, 0))] * 2
        operands = [replica.astype(jnp.int32).reshape(1)] + operands
        aliases = {}
        if previous is not None:
            operands.append(previous)
            in_specs.append(pl.BlockSpec(memory_space=pl.ANY))
            aliases = {3: 0}
        return pl.pallas_call(
            functools.partial(rows_back_kernel, kept),
            grid_spec=pltpu.PrefetchScalarGridSpec(
                num_scalar_prefetch=1,
                grid=(1,),
                in_specs=in_specs,
                out_specs=pl.BlockSpec((1, rows, width), lambda i, s: (layer, 0, 0)),
            ),
            out_shape=sds((layers, rows, width), F32),
            input_output_aliases=aliases,
            compiler_params=pltpu.CompilerParams(vmem_limit_bytes=44 * 1024 * 1024),
            cost_estimate=pl.CostEstimate(
                flops=0, bytes_accessed=12 * v.size, transcendentals=0
            ),
        )(*operands)

    def late_down(down, layer):
        return late_rows(down, own_hidden, piece, layer, into_down)

    def late_out(out, layer):
        return late_rows(out, own_rows, part, layer, into_out)

    into_qkv = into_up = into_down = into_out = None
    smalls = [None] * layers
    late = None
    for layer in reversed(range(layers)):
        qkv_w, out_w, up_w, down_w = weights[layer]
        (gain1, _, _, _, _, gain2, _, _), _, _ = vecs[layer]
        unit1, inv1, normed, packed, lse, mixed, unit2, inv2, normed_two, slope, activated = kept[
            layer
        ]
        g_low = grad.astype(BF)
        grad_down = down_grad(plan, activated, grad_pieces, width)
        if late is not None:
            above = layer + 1
            out = scatter_seq(down_grad(plan, *late[2], width))
            if above == layers - 1:
                last_down = weights[above][3]
                parts = lower_units(plan, after(kept[above][-1], late[2][0]), last_down)
                hidden = middle + (plan.scatter_parts(*parts) + bias_down)
                output = plan.regroup(hidden.astype(BF), back=True)
            into_up = late_up(late[0], above)
            into_down = late_down(late[1], above)
            into_out = late_out(out, above)
        if late is None:
            grad_pieces, grad_down = lax.optimization_barrier((grad_pieces, grad_down))
        down = scatter_seq(grad_down, lead=True)
        g_lift, grad_b_up, near, far = hidden_back(
            plan, grad_pieces, slope, down_w, up_w
        )
        grad_up = wgrad(plan, normed_two, g_lift)
        g_n2 = plan.scatter_parts(near, far)
        up = scatter_seq(grad_up).reshape(nf, own_rows, units)
        g_mid = grad + norm_pull(g_n2, unit2, inv2, gain2)
        g_att = g_mid.astype(BF)
        g_mixed = dot(g_att, out_w, 1, 1).astype(BF)
        g_mixed = dot(g_mixed, select, 1, 1).astype(BF)
        g_mixed = jnp.concatenate(
            [g_mixed[:, i * span : (i + 1) * span] for i in range(group)]
        )
        g_mixed = plan.exchange(g_mixed)
        att_pieces = plan.gather_pieces(widen(g_att))
        g_packed, g_b, near, far = attend_back(
            plan, g_mixed, packed, lse, codes, qkv_w, total, scale
        )
        grad_qkv = wgrad(plan, normed, g_packed)
        g_n1 = plan.scatter_parts(near, far)
        qkv = scatter_seq(grad_qkv)
        qkv = qkv.reshape(nf, own_rows, 3 * span)
        if late is not None:
            into_qkv = late_qkv(after(late[3], g_n1), above)
        if layer == 0:
            into_up = late_up(up, layer)
            into_down = late_down(down, layer)
        late = (up, down, (after(mixed, g_n1 if layer else grad_qkv), att_pieces), qkv)
        smalls[layer] = (
            jnp.sum(g_n1 * unit1, axis=0),
            jnp.sum(g_n1, axis=0),
            g_b,
            jnp.sum(g_att.astype(F32), axis=0),
            jnp.sum(g_n2 * unit2, axis=0),
            jnp.sum(g_n2, axis=0),
            jnp.sum(g_low.astype(F32), axis=0),
            grad_b_up,
        )
        grad = g_mid + norm_pull(g_n1, unit1, inv1, gain1)
        if layer:
            grad_pieces = plan.gather_pieces(widen(grad.astype(BF)))
    out = scatter_seq(down_grad(plan, *late[2], width))
    grad_tokens = plan.regroup(grad.astype(BF), back=True).astype(F32)
    output = after(output, grad).astype(F32)
    into_qkv = late_qkv(after(late[3], (into_up, into_down)), 0)
    into_out = late_out(out, 0)

    def scattered(layer):
        n1g, n1s, g_b, b_o, n2g, n2s, b_d, b_u = smalls[layer]

        def place(v):
            full = lax.dynamic_update_slice_in_dim(
                jnp.zeros((group * span,), F32), v, rank * span, 0
            )
            return full[:width]

        b_u = lax.dynamic_update_slice(
            jnp.zeros((nz, nf, nr, piece), F32),
            b_u.reshape(nz, 1, 1, piece_rows)[..., :piece],
            (0, fsdp, replica, 0),
        )
        rows = [n1g, n1s, place(g_b[:span]), place(g_b[2 * span :]), b_o, n2g, n2s, b_d]
        return jnp.concatenate(
            [v.reshape(nz * nf, own_rows) for v in rows] + [b_u.reshape(nz * nf, own_hidden)],
            axis=1,
        )

    flat = jnp.concatenate([scattered(layer) for layer in range(layers)], axis=1)
    wide = lanes(-(-flat.shape[1] // 2))
    flat = jnp.pad(flat, ((0, 0), (0, 2 * wide - flat.shape[1])))
    flat = plan.scatter_small(flat.reshape(nz, nf, 2, wide))
    flat = jnp.sum(plan.to_owners_small(flat), axis=0).reshape(-1)
    flat = flat[: layers * each_small].reshape(layers, each_small)
    vec = [flat[:, i * own_rows : (i + 1) * own_rows] for i in range(8)]
    return (
        output[None],
        grad_tokens[None],
        vec[0],
        vec[1],
        into_qkv,
        vec[2],
        vec[3],
        into_out,
        vec[4],
        vec[5],
        vec[6],
        into_up,
        flat[:, 8 * own_rows :],
        into_down,
        vec[7],
    )


def solution(mesh):
    plan = Plan(mesh)
    data = P(("fsdp", "replica"), "seq", None)
    vector = P(None, ("seq", "fsdp"))
    matrix = P(None, ("seq", "fsdp"), None)
    weights = (
        vector,
        vector,
        matrix,
        vector,
        vector,
        matrix,
        vector,
        vector,
        vector,
        matrix,
        vector,
        matrix,
        vector,
    )
    in_specs = (data, data, P(("fsdp", "replica"), "seq")) + weights
    out_specs = (data, data) + weights
    return jax.shard_map(
        functools.partial(shards, plan),
        mesh=mesh,
        in_specs=in_specs,
        out_specs=out_specs,
        check_vma=False,
    )
```

```python
import functools
import math

import jax
import jax.numpy as jnp
from jax import lax
from jax.experimental import pallas as pl
from jax.experimental.pallas import tpu as pltpu
from jax.sharding import PartitionSpec as P


HEADS = 25
HD = 64
BF = jnp.bfloat16
F32 = jnp.float32
CODE = 65536
LOW = -1e30
SEQ, FSDP, REPLICA = "seq", "fsdp", "replica"
QK, PV, PK = "sqhd,skhd->shqk", "shqk,skhd->sqhd", "shqk,sqhd->skhd"
ALL = (SEQ, FSDP, REPLICA)
GROUP = (FSDP, REPLICA)
OWNERS = (SEQ, FSDP)


def dot(a, b, ca=1, cb=0):
    return lax.dot_general(a, b, (((ca,), (cb,)), ((), ())), preferred_element_type=F32)


def norm_parts(v):
    mean = jnp.mean(v, axis=-1, keepdims=True)
    centred = v - mean
    spread = jnp.mean(centred * centred, axis=-1, keepdims=True)
    inv = lax.rsqrt(spread + 1e-05)
    return centred * inv, inv


def norm_pull(grad, unit, inv, gain):
    scaled = grad * gain
    first = jnp.mean(scaled, axis=-1, keepdims=True)
    second = jnp.mean(scaled * unit, axis=-1, keepdims=True)
    return inv * (scaled - first - unit * second)


def gelu_both(value):
    tanh = jnp.tanh(0.7978845608028654 * (value + 0.044715 * value * value * value))
    inner = 0.7978845608028654 * (1.0 + 3.0 * 0.044715 * value * value)
    half = 0.5 * (1.0 + tanh)
    return value * half, half + 0.5 * value * (1.0 - tanh * tanh) * inner


class Plan:
    def __init__(self, mesh):
        self.nz = mesh.shape[SEQ]
        self.nf = mesh.shape[FSDP]
        self.nr = mesh.shape[REPLICA]
        self.group = self.nf * self.nr
        self.cube = self.nf == 4 and self.nr == 2
        self.heads = 2 * -(-HEADS // (2 * self.group))
        self.span = self.heads * HD
        order = sorted(
            (self.rank_of(f, r), f * self.nr + r) for f in range(self.nf) for r in range(self.nr)
        )
        self.place = [member for _, member in order]
        self.back = [0] * self.group
        for rank, member in order:
            self.back[member] = rank

    def rank_of(self, f, r):
        half = self.group // 2
        if self.nf % 2:
            return f * self.nr + r
        return (f % 2) * half + (f // 2) * self.nr + r

    def rank(self):
        return self.rank_of(lax.axis_index(FSDP), lax.axis_index(REPLICA))

    def regroup(self, v, back=False):
        nz = self.nz
        pairs = []
        for z in range(nz):
            for g in range(self.group):
                goal = g % nz
                slot = (g // nz) * nz + (z ^ goal if nz & (nz - 1) == 0 else z)
                pairs.append((z * self.group + self.place[g], goal * self.group + self.place[slot]))
        if back:
            pairs = [(there, here) for here, there in pairs]
        return lax.ppermute(v, ALL, pairs)

    def swap_core(self, v):
        return lax.ppermute(v, FSDP, [(f, f ^ 1) for f in range(self.nf)])

    def swap_y(self, v):
        return lax.ppermute(v, FSDP, [(f, f ^ 2) for f in range(self.nf)])

    def swap_x(self, v):
        return lax.ppermute(v, REPLICA, [(r, r ^ 1) for r in range(self.nr)])

    def swap_xy(self, v):
        pairs = [
            (f * self.nr + r, (f ^ 2) * self.nr + (r ^ 1))
            for f in range(self.nf)
            for r in range(self.nr)
        ]
        return lax.ppermute(v, GROUP, pairs)

    def source(self):
        base = jnp.arange(self.group, dtype=jnp.int32)
        return base ^ self.rank() if self.cube else base

    def gather_pieces(self, v):
        if not self.cube:
            full = lax.all_gather(v, GROUP, axis=0, tiled=False)
            return [full[member] for member in self.place]
        near = [v, self.swap_x(v), self.swap_y(v), self.swap_xy(v)]
        return near + [self.swap_core(piece) for piece in near]

    def gather_doubling(self, v):
        if not self.cube:
            return jnp.concatenate(self.gather_pieces(v))
        for swap in (self.swap_x, self.swap_y, self.swap_core):
            v = jnp.concatenate([v, swap(v)])
        return v

    def scatter_parts(self, near, far):
        if not self.cube:
            blocks = jnp.concatenate([near.astype(BF), far])
            rows = blocks.shape[0] // self.group
            blocks = blocks.reshape(self.group, rows, -1)[jnp.array(self.back)]
            blocks = blocks.reshape(self.group * rows, -1)
            return lax.psum_scatter(blocks, GROUP, scatter_dimension=0, tiled=True).astype(F32)
        rows, columns = near.shape[0] // 4, near.shape[1]
        own, to_x, to_y, to_xy = call(
            fold_kernel,
            [sds((rows, columns), F32)] + [sds((rows, lanes(columns)), BF)] * 3,
            [],
            0,
            [near, self.swap_core(far)],
        )
        parts = self.swap_xy(to_xy), self.swap_x(to_x), self.swap_y(to_y)
        parts = [part[:, :columns].astype(F32) for part in parts]
        return own + parts[0] + parts[1] + parts[2]

    def exchange(self, v):
        if not self.cube:
            v = v.reshape(self.group, -1, v.shape[1])[jnp.array(self.back)]
            v = lax.all_to_all(v, GROUP, split_axis=0, concat_axis=0, tiled=True)
            return [v[member] for member in self.place]
        rows = v.shape[0] // 8
        half = 4 * rows
        far = self.swap_core(v[half:])
        out = [[v[:rows], far[:rows]]]
        for i, swap in ((1, self.swap_x), (2, self.swap_y), (3, self.swap_xy)):
            both = swap(
                jnp.concatenate([v[i * rows : (i + 1) * rows], far[i * rows : (i + 1) * rows]])
            )
            out.append([both[:rows], both[rows:]])
        return [pair[0] for pair in out] + [pair[1] for pair in out]

    def flips(self, v):
        f = lax.axis_index(FSDP)
        v = v.reshape((2, 2) + v.shape[1:])
        v = jnp.where(f // 2 == 1, jnp.flip(v, 0), v)
        return jnp.where(f % 2 == 1, jnp.flip(v, 1), v)

    def gather_owners(self, v):
        if not self.cube or self.nz != 4:
            return lax.all_gather(v, OWNERS, axis=0, tiled=False)
        z, f = lax.axis_index(SEQ), lax.axis_index(FSDP)
        far = [
            lax.ppermute(v, SEQ, [(i, i ^ d) for i in range(4)]) if d else v for d in range(4)
        ]
        v = jnp.stack(far).reshape((2, 2) + v.shape)
        v = jnp.where(z // 2 == 1, jnp.flip(v, 0), v)
        v = jnp.where(z % 2 == 1, jnp.flip(v, 1), v)
        other = self.swap_core(v)
        v = jnp.stack([jnp.where(f % 2 == 0, v, other), jnp.where(f % 2 == 0, other, v)], axis=2)
        other = self.swap_y(v)
        v = jnp.stack([jnp.where(f // 2 == 0, v, other), jnp.where(f // 2 == 0, other, v)], axis=2)
        return v.reshape((16,) + v.shape[4:])

    def exchange_fsdp(self, v):
        if not self.cube:
            return lax.all_to_all(v, FSDP, split_axis=0, concat_axis=0, tiled=True)
        shape = v.shape
        v = self.flips(v)
        both = jnp.stack([v[:, 0], self.swap_core(v[:, 1])], axis=1)
        return self.flips(jnp.stack([both[0], self.swap_y(both[1])]).reshape(shape)).reshape(shape)

    def scatter_small(self, v):
        if not self.cube or self.nz != 4:
            return lax.psum_scatter(v, SEQ, scatter_dimension=0, tiled=False)
        z = lax.axis_index(SEQ)
        total = lax.dynamic_index_in_dim(v, z, 0, keepdims=False)
        for d in range(1, 4):
            other = lax.dynamic_index_in_dim(v, z ^ d, 0, keepdims=False)
            total = total + lax.ppermute(other, SEQ, [(i, i ^ d) for i in range(4)])
        return total

    def to_owners_small(self, v):
        if not self.cube:
            v = lax.all_to_all(v, FSDP, split_axis=0, concat_axis=0, tiled=True)
            v = lax.all_gather(v, REPLICA, axis=1, tiled=False)
            return jnp.stack([v[m // self.nr, m % self.nr] for m in self.place])
        v = self.flips(v)
        far = self.swap_core(v[:, 1])
        here = jnp.stack([v[0, 0], far[0]])
        there = jnp.stack([v[1, 0], far[1]])
        return jnp.stack(
            [here, self.swap_x(here), self.swap_y(there), self.swap_xy(there)], axis=1
        ).reshape((8,) + v.shape[2:])

    def to_owners(self, v):
        if not self.cube:
            return self.to_owners_small(v)
        nf, rows, columns = v.shape
        f = lax.axis_index(FSDP)
        pick = (f ^ jnp.arange(nf, dtype=jnp.int32)).astype(jnp.int32)
        pair = sds((2, rows, columns), BF)
        near, far = pl.pallas_call(
            pick_kernel,
            grid_spec=pltpu.PrefetchScalarGridSpec(
                num_scalar_prefetch=1,
                grid=(1,),
                in_specs=[pl.BlockSpec(v.shape, lambda i, s: (0, 0, 0))],
                out_specs=[pl.BlockSpec(pair.shape, lambda i, s: (0, 0, 0))] * 2,
            ),
            out_shape=[pair] * 2,
            compiler_params=pltpu.CompilerParams(vmem_limit_bytes=44 * 1024 * 1024),
        )(pick, v)
        here, there = call(pair_kernel, [pair] * 2, [], 0, [near, self.swap_core(far)])
        return [here, self.swap_x(here), self.swap_y(there), self.swap_xy(there)]


def pick_kernel(order, v, near, far):
    for y in range(2):
        near[y] = v[order[2 * y]]
        far[y] = v[order[2 * y + 1]]


def pair_kernel(near, far, here, there):
    for y, out in enumerate((here, there)):
        out[0] = near[y]
        out[1] = far[y]


def gather_seq(v, lead=False):
    if lead:
        return lax.all_gather(v[None], SEQ, axis=1, tiled=True)[0]
    return lax.all_gather(v, SEQ, axis=0, tiled=True)


def scatter_seq(v, lead=False):
    if lead:
        return lax.psum_scatter(v[None], SEQ, scatter_dimension=1, tiled=True)[0]
    return lax.psum_scatter(v, SEQ, scatter_dimension=0, tiled=True)


def call(kernel, outs, scratch, flops, operands, **more):
    params = pltpu.CompilerParams(vmem_limit_bytes=44 * 1024 * 1024)
    size = sum(math.prod(o.shape) * o.dtype.itemsize for o in list(outs) + list(operands))
    return pl.pallas_call(
        kernel,
        out_shape=tuple(outs),
        scratch_shapes=scratch,
        compiler_params=params,
        cost_estimate=pl.CostEstimate(
            flops=int(flops), bytes_accessed=int(size), transcendentals=0
        ),
        **more,
    )(*operands)


def lanes(columns):
    return -(-columns // 128) * 128


def widen(v):
    return jnp.pad(v, ((0, 0), (0, lanes(v.shape[1]) - v.shape[1])))


def sds(shape, dtype):
    return jax.ShapeDtypeStruct(shape, dtype)


def fold_kernel(near, far, own, to_x, to_y, to_xy):
    rows, columns = own.shape
    own[...] = near[:rows, :] + far[:rows, :columns].astype(F32)
    for i, out in ((1, to_x), (2, to_y), (3, to_xy)):
        at = slice(i * rows, (i + 1) * rows)
        out[:, :columns] = (near[at, :] + far[at, :columns].astype(F32)).astype(BF)


def wgrad_kernel(left, right, out):
    tall = out.shape[0]
    block = 256

    def body(i, carry):
        at = pl.ds(pl.multiple_of(i * block, block), block)
        out[at, :] = dot(left[:, at], right[...], 0, 0).astype(BF)
        return carry

    whole = tall // block
    lax.fori_loop(0, whole, body, 0)
    if tall % block:
        out[whole * block :, :] = dot(left[:, whole * block :], right[...], 0, 0).astype(BF)


def wgrad(plan, left, right):
    if not plan.cube:
        return dot(left, right, 0, 0).astype(BF)
    tall, width = left.shape[1], right.shape[1]
    return call(
        wgrad_kernel, [sds((tall, width), BF)], [], 2 * left.size * width, [left, right]
    )[0]


def after(v, other):
    return lax.optimization_barrier((v, other))[0]


def project_kernel(count, left, *refs):
    block = refs[0].shape[0]
    total = dot(left[:, :block], refs[0][...])
    for i in range(1, count):
        total = total + dot(left[:, i * block : (i + 1) * block], refs[i][...])
    refs[-1][...] = total


def project(plan, left, pieces):
    if not plan.cube:
        return dot(left, jnp.concatenate(pieces))
    shape = sds((left.shape[0], pieces[0].shape[1]), F32)
    kernel = functools.partial(project_kernel, len(pieces))
    return call(kernel, [shape], [], 2 * left.size * shape.shape[1], [left, *pieces])[0]


def project_back_kernel(count, left, *refs):
    block = refs[0].shape[0]
    for i in range(count):
        refs[-1][:, i * block : (i + 1) * block] = dot(left[...], refs[i][...], 1, 1).astype(BF)


def project_back(plan, left, pieces):
    if not plan.cube:
        return dot(left, jnp.concatenate(pieces), 1, 1).astype(BF)
    shape = sds((left.shape[0], len(pieces) * pieces[0].shape[0]), BF)
    kernel = functools.partial(project_back_kernel, len(pieces))
    return call(kernel, [shape], [], 2 * left.size * shape.shape[1], [left, *pieces])[0]


def first_half(shape):
    return lax.broadcasted_iota(jnp.int32, shape, 1) < HD


def attend_kernel(count, total, span, scale, *refs):
    pieces = refs[:count]
    w, bias, code_col, code_row, full, packed, lse, mixed = refs[count:]
    rows = pieces[0].shape[0]
    for i, piece in enumerate(pieces):
        full[i * rows : (i + 1) * rows, :] = piece[:, : full.shape[1]]
    block = 2 * rows

    def project(i, carry):
        at = pl.ds(pl.multiple_of(i * block, block), block)
        packed[at, :] = (dot(full[at, :], w[...]) + bias[...]).astype(BF)
        return carry

    lax.fori_loop(0, count // 2, project, 0)
    blocks = total // rows
    left = first_half((rows, 2 * HD))
    lane = lax.broadcasted_iota(jnp.int32, (rows, 128), 1)

    def queries(i, carry):
        at = pl.ds(pl.multiple_of(i * rows, rows), rows)
        seq = i // blocks
        keys_at = pl.ds(pl.multiple_of(seq * total, total), total)
        code_q = code_col[at, :]
        code_k = code_row[pl.ds(seq, 1), :]
        allowed = (code_k <= code_q) & (code_k >= (code_q // CODE) * CODE)
        stats = jnp.zeros((rows, 128), F32)
        for pair in range(span // 128):
            q = packed[at, pair * 128 : pair * 128 + 128]
            k = packed[keys_at, span + pair * 128 : span + pair * 128 + 128]
            v = packed[keys_at, 2 * span + pair * 128 : 2 * span + pair * 128 + 128]
            both = []
            for side in range(2):
                own = left if side == 0 else ~left
                scores = dot(jnp.where(own, q, jnp.zeros_like(q)), k, 1, 1) * scale
                scores = jnp.where(allowed, scores, LOW)
                top = jnp.max(scores, axis=1, keepdims=True)
                expo = jnp.exp(scores - top)
                denom = jnp.sum(expo, axis=1, keepdims=True)
                probs = (expo * (1.0 / denom)).astype(BF)
                both.append(dot(probs, v))
                stats = jnp.where(lane == 2 * pair + side, top + jnp.log(denom), stats)
            mixed[at, pair * 128 : pair * 128 + 128] = jnp.where(left, both[0], both[1]).astype(BF)
        lse[:, at] = stats.T[: lse.shape[0], :]
        return carry

    lax.fori_loop(0, count, queries, 0)


def attend(plan, pieces, w, bias, codes, total, scale):
    rows, width = pieces[0].shape[0], w.shape[0]
    count, span = plan.group, plan.span
    if not plan.cube:
        full = jnp.concatenate(pieces)[:, :width]
        packed = (dot(full, w) + bias).astype(BF)
        q, k, v = (
            packed[:, i * span : (i + 1) * span].reshape(-1, total, plan.heads, HD)
            for i in range(3)
        )
        allowed = mask_of(codes, total)
        scores = jnp.einsum(QK, q, k, preferred_element_type=F32) * scale
        scores = jnp.where(allowed[:, None], scores, LOW)
        top = jnp.max(scores, axis=-1, keepdims=True)
        expo = jnp.exp(scores - top)
        denom = jnp.sum(expo, axis=-1, keepdims=True)
        probs = (expo / denom).astype(BF)
        mixed = jnp.einsum(PV, probs, v, preferred_element_type=F32)
        return full, packed, top + jnp.log(denom), mixed.reshape(-1, span).astype(BF)
    tall = count * rows
    return call(
        functools.partial(attend_kernel, count, total, span, scale),
        [
            sds((tall, width), BF),
            sds((tall, 3 * span), BF),
            sds((8, tall), F32),
            sds((tall, span), BF),
        ],
        [],
        2 * tall * width * 3 * span + 8 * tall * total * span,
        [*pieces, w, bias[None], codes.reshape(-1, 1), codes.reshape(-1, total)],
    )


def mask_of(codes, total):
    code = codes.reshape(-1, total)
    low = (code // CODE) * CODE
    return (code[:, None, :] <= code[:, :, None]) & (code[:, None, :] >= low[:, :, None])


def attend_back_kernel(count, total, span, scale, *refs):
    pieces = refs[:count]
    packed, lse, code_col, code_row, w, g_packed, g_bias, near, far, gm, g_k, g_v = refs[count:]
    rows = pieces[0].shape[0]
    for i, piece in enumerate(pieces):
        gm[i * rows : (i + 1) * rows, :] = piece[...]
    blocks = total // rows
    left = first_half((rows, 2 * HD))

    def sequence(seq, carry):
        keys_at = pl.ds(pl.multiple_of(seq * total, total), total)
        code_k = code_col[keys_at, :]
        for pair in range(span // 128):
            lanes = slice(pair * 128, pair * 128 + 128)
            k_lanes = slice(span + pair * 128, span + pair * 128 + 128)
            v_lanes = slice(2 * span + pair * 128, 2 * span + pair * 128 + 128)
            k = packed[keys_at, k_lanes]
            v = packed[keys_at, v_lanes]
            g_k[...] = jnp.zeros_like(g_k)
            g_v[...] = jnp.zeros_like(g_v)

            def queries(i, inner):
                at = pl.ds(pl.multiple_of(seq * total + i * rows, rows), rows)
                code_q = code_row[pl.ds(seq * blocks + i, 1), :]
                allowed = (code_k <= code_q) & (code_k >= (code_q // CODE) * CODE)
                q = packed[at, lanes]
                g = gm[at, lanes]
                both = []
                for side in range(2):
                    own = left if side == 0 else ~left
                    q_own = jnp.where(own, q, jnp.zeros_like(q))
                    g_own = jnp.where(own, g, jnp.zeros_like(g))
                    scores = dot(k, q_own, 1, 1) * scale
                    row = 2 * pair + side
                    probs = jnp.exp(jnp.where(allowed, scores, LOW) - lse[row : row + 1, at])
                    g_probs = dot(v, g_own, 1, 1)
                    each = jnp.sum(g_probs * probs, axis=0, keepdims=True)
                    g_scores = (probs * (g_probs - each)).astype(BF)
                    g_v[...] += dot(probs.astype(BF), g_own)
                    g_k[...] += dot(g_scores, q_own)
                    both.append(dot(g_scores, k, 0, 0))
                g_packed[at, lanes] = (jnp.where(left, both[0], both[1]) * scale).astype(BF)
                return inner

            lax.fori_loop(0, blocks, queries, 0)
            g_packed[keys_at, k_lanes] = (g_k[...] * scale).astype(BF)
            g_packed[keys_at, v_lanes] = g_v[...].astype(BF)
        return carry

    lax.fori_loop(0, count // blocks, sequence, 0)
    g_bias[...] = jnp.sum(g_packed[...].astype(F32), axis=0, keepdims=True)
    spread_out(g_packed, w, near, far, 2 * rows)


def spread_out(left, right, near, far, block):
    half = near.shape[0]

    def first(i, carry):
        at = pl.ds(pl.multiple_of(i * block, block), block)
        near[at, :] = dot(left[at, :], right[...], 1, 1)
        return carry

    def second(i, carry):
        at = pl.ds(pl.multiple_of(i * block, block), block)
        far[at, : near.shape[1]] = dot(
            left[pl.ds(pl.multiple_of(half + i * block, block), block), :], right[...], 1, 1
        ).astype(BF)
        return carry

    lax.fori_loop(0, half // block, first, 0)
    lax.fori_loop(0, half // block, second, 0)


def halves(v):
    half = v.shape[0] // 2
    return v[:half], v[half:].astype(BF)


def attend_back(plan, pieces, packed, lse, codes, w, total, scale):
    count, span = plan.group, plan.span
    rows = pieces[0].shape[0]
    width = w.shape[0]
    if not plan.cube:
        q, k, v = (
            packed[:, i * span : (i + 1) * span].reshape(-1, total, plan.heads, HD)
            for i in range(3)
        )
        gm = jnp.concatenate(pieces).reshape(-1, total, plan.heads, HD)
        allowed = mask_of(codes, total)
        scores = jnp.einsum(QK, q, k, preferred_element_type=F32) * scale
        probs = jnp.exp(jnp.where(allowed[:, None], scores, LOW) - lse)
        g_probs = jnp.einsum(QK, gm, v, preferred_element_type=F32)
        g_v = jnp.einsum(PK, probs.astype(BF), gm, preferred_element_type=F32)
        row = jnp.sum(g_probs * probs, axis=-1, keepdims=True)
        g_s = (probs * (g_probs - row)).astype(BF)
        g_q = jnp.einsum(PV, g_s, k, preferred_element_type=F32) * scale
        g_k = jnp.einsum(PK, g_s, q, preferred_element_type=F32) * scale
        g_packed = jnp.concatenate(
            [u.reshape(-1, span).astype(BF) for u in (g_q, g_k, g_v)], axis=1
        )
        near, far = halves(dot(g_packed, w, 1, 1))
        return g_packed, jnp.sum(g_packed.astype(F32), axis=0), near, far
    tall = count * rows
    g_packed, g_bias, near, far = call(
        functools.partial(attend_back_kernel, count, total, span, scale),
        [
            sds((tall, 3 * span), BF),
            sds((1, 3 * span), F32),
            sds((tall // 2, width), F32),
            sds((tall // 2, lanes(width)), BF),
        ],
        [pltpu.VMEM((tall, span), BF)] + [pltpu.VMEM((total, 128), F32)] * 2,
        2 * tall * width * 3 * span + 20 * tall * total * span,
        [*pieces, packed, lse, codes.reshape(-1, 1), codes.reshape(-1, rows), w],
    )
    return g_packed, g_bias[0], near, far


def hidden_kernel(count, *refs):
    pieces = refs[:count]
    up, bias, down, full, slope, activated, near, far = refs[count:]
    rows = pieces[0].shape[0]
    for i, piece in enumerate(pieces):
        full[i * rows : (i + 1) * rows, :] = piece[:, : full.shape[1]]
    block = 2 * rows
    half = near.shape[0]

    def lift(at):
        value, pull = gelu_both(dot(full[at, :], up[...]) + bias[...])
        value = value.astype(BF)
        activated[at, :] = value
        slope[at, :] = pull.astype(BF)
        return dot(value, down[...])

    def first(i, carry):
        at = pl.ds(pl.multiple_of(i * block, block), block)
        near[at, :] = lift(at)
        return carry

    def second(i, carry):
        at = pl.ds(pl.multiple_of(i * block, block), block)
        out = lift(pl.ds(pl.multiple_of(half + i * block, block), block))
        far[at, : near.shape[1]] = out.astype(BF)
        return carry

    lax.fori_loop(0, half // block, first, 0)
    lax.fori_loop(0, half // block, second, 0)


def lift_kernel(count, *refs):
    pieces = refs[:count]
    up, bias, full, slope, activated = refs[count:]
    rows = pieces[0].shape[0]
    for i, piece in enumerate(pieces):
        full[i * rows : (i + 1) * rows, :] = piece[:, : full.shape[1]]
    block = 2 * rows

    def lift(i, carry):
        at = pl.ds(pl.multiple_of(i * block, block), block)
        value, pull = gelu_both(dot(full[at, :], up[...]) + bias[...])
        activated[at, :] = value.astype(BF)
        slope[at, :] = pull.astype(BF)
        return carry

    lax.fori_loop(0, count // 2, lift, 0)


def lift_units(plan, pieces, up, bias):
    rows, width = pieces[0].shape[0], up.shape[0]
    if not plan.cube:
        full = jnp.concatenate(pieces)[:, :width]
        value, pull = gelu_both(dot(full, up) + bias)
        return full, pull.astype(BF), value.astype(BF)
    tall, units = plan.group * rows, up.shape[1]
    return call(
        functools.partial(lift_kernel, plan.group),
        [sds((tall, width), BF), sds((tall, units), BF), sds((tall, units), BF)],
        [],
        2 * tall * width * units,
        [*pieces, up, bias[None]],
    )


def lower_kernel(block, left, right, near, far):
    half, width = near.shape

    def first(i, carry):
        at = pl.ds(pl.multiple_of(i * block, block), block)
        near[at, :] = dot(left[at, :], right[...])
        return carry

    def second(i, carry):
        at = pl.ds(pl.multiple_of(i * block, block), block)
        rows = left[pl.ds(pl.multiple_of(half + i * block, block), block), :]
        far[at, :width] = dot(rows, right[...]).astype(BF)
        return carry

    lax.fori_loop(0, half // block, first, 0)
    lax.fori_loop(0, half // block, second, 0)


def lower_units(plan, activated, down):
    tall, width = activated.shape[0], down.shape[1]
    if not plan.cube:
        return halves(dot(activated, down))
    return call(
        functools.partial(lower_kernel, 2 * (tall // plan.group)),
        [sds((tall // 2, width), F32), sds((tall // 2, lanes(width)), BF)],
        [],
        2 * activated.size * width,
        [activated, down],
    )


def hidden_units(plan, pieces, up, bias, down):
    rows, width = pieces[0].shape[0], up.shape[0]
    if not plan.cube:
        full = jnp.concatenate(pieces)[:, :width]
        value, pull = gelu_both(dot(full, up) + bias)
        value = value.astype(BF)
        return (full, pull.astype(BF), value) + halves(dot(value, down))
    tall, units = plan.group * rows, up.shape[1]
    return call(
        functools.partial(hidden_kernel, plan.group),
        [
            sds((tall, width), BF),
            sds((tall, units), BF),
            sds((tall, units), BF),
            sds((tall // 2, width), F32),
            sds((tall // 2, lanes(width)), BF),
        ],
        [],
        4 * tall * width * units,
        [*pieces, up, bias[None], down],
    )


def hidden_back_kernel(count, *refs):
    pieces = refs[:count]
    slope, down, up, g_lift, g_bias, near, far, full = refs[count:]
    rows = pieces[0].shape[0]
    for i, piece in enumerate(pieces):
        full[i * rows : (i + 1) * rows, :] = piece[:, : full.shape[1]]
    block = 2 * rows

    def pull(i, carry):
        at = pl.ds(pl.multiple_of(i * block, block), block)
        g_lift[at, :] = (dot(full[at, :], down[...], 1, 1) * slope[at, :].astype(F32)).astype(BF)
        return carry

    lax.fori_loop(0, count // 2, pull, 0)
    spread_out(g_lift, up, near, far, block)
    g_bias[...] = jnp.sum(g_lift[...].astype(F32), axis=0, keepdims=True)


def hidden_back(plan, pieces, slope, down, up):
    rows, width = pieces[0].shape[0], up.shape[0]
    if not plan.cube:
        full = jnp.concatenate(pieces)[:, :width]
        g_lift = (dot(full, down, 1, 1) * slope.astype(F32)).astype(BF)
        return (g_lift, jnp.sum(g_lift.astype(F32), axis=0)) + halves(dot(g_lift, up, 1, 1))
    tall, units = plan.group * rows, up.shape[1]
    g_lift, g_bias, near, far = call(
        functools.partial(hidden_back_kernel, plan.group),
        [
            sds((tall, units), BF),
            sds((1, units), F32),
            sds((tall // 2, width), F32),
            sds((tall // 2, lanes(width)), BF),
        ],
        [pltpu.VMEM((tall, width), BF)],
        4 * tall * width * units,
        [*pieces, slope, down, up],
    )
    return g_lift, g_bias[0], near, far


def down_grad_kernel(count, *refs):
    left, out, full = refs[count:]
    rows = refs[0].shape[0]
    for i, piece in enumerate(refs[:count]):
        full[i * rows : (i + 1) * rows, :] = piece[:, : full.shape[1]]
    wgrad_kernel(left, full, out)


def down_grad(plan, left, pieces, width):
    if not plan.cube:
        return dot(left, jnp.concatenate(pieces)[:, :width], 0, 0).astype(BF)
    tall, units = left.shape
    return call(
        functools.partial(down_grad_kernel, plan.group),
        [sds((units, width), BF)],
        [pltpu.VMEM((tall, width), BF)],
        2 * left.size * width,
        [*pieces, left],
    )[0]


def head_columns_kernel(nf, ranks, span, x_ref, w_ref, out, wide):
    width = w_ref.shape[2] // 3
    padded = wide.shape[1] // 3
    w = w_ref[0].astype(F32)
    for i in range(3):
        wide[:, i * padded : i * padded + width] = w[:, i * width : (i + 1) * width]
        if padded > width:
            wide[:, i * padded + width : (i + 1) * padded] = jnp.zeros(
                (wide.shape[0], padded - width), F32
            )
    for x, row in enumerate(ranks):

        @pl.when(x_ref[0] == x)
        def _():
            for f in range(nf):
                for i in range(3):
                    start = i * padded + row[f] * span
                    out[0, f, :, i * span : (i + 1) * span] = wide[:, start : start + span].astype(
                        BF
                    )


def unit_columns_kernel(nz, nf, nr, piece, piece_rows, x_ref, w_ref, out):
    w = w_ref[0].astype(F32)
    for x in range(nr):

        @pl.when(x_ref[0] == x)
        def _():
            for f in range(nf):
                part = []
                for z in range(nz):
                    start = ((z * nf + f) * nr + x) * piece
                    part.append(w[:, start : start + piece])
                    if piece_rows > piece:
                        part.append(jnp.zeros((w.shape[0], piece_rows - piece), F32))
                out[0, f] = jnp.concatenate(part, axis=1).astype(BF)


def layered(kernel, x, w, columns, nf, scratch):
    layers, rows, full = w.shape
    return pl.pallas_call(
        kernel,
        grid_spec=pltpu.PrefetchScalarGridSpec(
            num_scalar_prefetch=1,
            grid=(layers,),
            in_specs=[pl.BlockSpec((1, rows, full), lambda i, s: (i, 0, 0))],
            out_specs=pl.BlockSpec((1, nf, rows, columns), lambda i, s: (i, 0, 0, 0)),
            scratch_shapes=scratch,
        ),
        out_shape=sds((layers, nf, rows, columns), BF),
        compiler_params=pltpu.CompilerParams(vmem_limit_bytes=44 * 1024 * 1024),
        cost_estimate=pl.CostEstimate(flops=0, bytes_accessed=4 * w.size, transcendentals=0),
    )(x, w)


def head_columns(plan, w):
    layers, rows, triple = w.shape
    nf, nr, span, group = plan.nf, plan.nr, plan.span, plan.group
    ranks = [[plan.rank_of(f, r) for f in range(nf)] for r in range(nr)]
    x = lax.axis_index(REPLICA)
    if not plan.cube:
        width = triple // 3
        v = w.reshape(layers, rows, 3, width)
        v = jnp.pad(v, ((0, 0), (0, 0), (0, 0), (0, group * span - width)))
        v = jnp.take(v.reshape(layers, rows, 3, group, span), jnp.array(ranks)[x], axis=3)
        return v.transpose(0, 3, 1, 2, 4).reshape(layers, nf, rows, 3 * span)
    return layered(
        functools.partial(head_columns_kernel, nf, ranks, span),
        x.astype(jnp.int32).reshape(1),
        w,
        3 * span,
        nf,
        [pltpu.VMEM((rows, 3 * group * span), F32)],
    )


def unit_columns(plan, w, piece, piece_rows):
    layers, rows, _ = w.shape
    nz, nf, nr = plan.nz, plan.nf, plan.nr
    x = lax.axis_index(REPLICA)
    if not plan.cube:
        v = w.reshape(layers, rows, nz, nf, nr, piece)
        v = lax.dynamic_index_in_dim(v, x, 4, keepdims=False)
        v = jnp.pad(v, ((0, 0),) * 4 + ((0, piece_rows - piece),))
        return v.transpose(0, 3, 1, 2, 4).reshape(layers, nf, rows, nz * piece_rows)
    return layered(
        functools.partial(unit_columns_kernel, nz, nf, nr, piece, piece_rows),
        x.astype(jnp.int32).reshape(1),
        w,
        nz * piece_rows,
        nf,
        [],
    )


def stacked(pairs, block):
    for i, pair in enumerate(pairs):
        for core in range(2):
            block[4 * core + i] = pair[core]


def heads_back_kernel(group, span, src_ref, *refs):
    out, wide, v_ref = refs[-3:]
    stacked(refs[:4], v_ref)
    width = out.shape[2] // 3
    padded = group * span
    for rank in range(group):
        block = v_ref[src_ref[rank]].astype(F32)
        for i in range(3):
            wide[:, i * padded + rank * span : i * padded + (rank + 1) * span] = block[
                :, i * span : (i + 1) * span
            ]
    for i in range(3):
        out[0, :, i * width : (i + 1) * width] = wide[:, i * padded : i * padded + width]


def units_back_kernel(nz, nf, nr, piece, piece_rows, ranks, src_ref, *refs):
    out, v_ref = refs[-2:]
    stacked(refs[:4], v_ref)
    for f in range(nf):
        blocks = [v_ref[src_ref[ranks[f][r]]].astype(F32) for r in range(nr)]
        for z in range(nz):
            part = [block[:, z * piece_rows : z * piece_rows + piece] for block in blocks]
            start = (z * nf + f) * nr * piece
            out[0, :, start : start + nr * piece] = jnp.concatenate(part, axis=1)


def into_layer(kernel, plan, pairs, shape, layer, previous, scratch):
    operands = [plan.source().astype(jnp.int32), *pairs]
    in_specs = [pl.BlockSpec(v.shape, lambda i, s: (0, 0, 0)) for v in pairs]
    scratch = scratch + [pltpu.VMEM((8,) + pairs[0].shape[1:], BF)]
    aliases = {}
    if previous is not None:
        operands.append(previous)
        in_specs.append(pl.BlockSpec(memory_space=pl.ANY))
        aliases = {5: 0}
    return pl.pallas_call(
        kernel,
        grid_spec=pltpu.PrefetchScalarGridSpec(
            num_scalar_prefetch=1,
            grid=(1,),
            in_specs=in_specs,
            out_specs=pl.BlockSpec((1,) + shape[1:], lambda i, s: (layer, 0, 0)),
            scratch_shapes=scratch,
        ),
        out_shape=sds(shape, F32),
        input_output_aliases=aliases,
        compiler_params=pltpu.CompilerParams(vmem_limit_bytes=44 * 1024 * 1024),
        cost_estimate=pl.CostEstimate(flops=0, bytes_accessed=48 * pairs[0].size, transcendentals=0),
    )(*operands)


def rows_back_kernel(kept, x_ref, own, other, *refs):
    out = refs[-1]
    for x in range(2):

        @pl.when(x_ref[0] == x)
        def _():
            first, second = (own, other) if x == 0 else (other, own)
            first, second = (v[...].astype(F32)[:kept] for v in (first, second))
            if kept % 8:
                out[0] = jnp.concatenate([first, second])
            else:
                out[0, :kept, :] = first
                out[0, kept:, :] = second


def shards(
    plan,
    tokens,
    cotangent,
    segments,
    norm1_gain,
    norm1_shift,
    w_qkv,
    b_query,
    b_value,
    w_out,
    b_out,
    norm2_gain,
    norm2_shift,
    w_up,
    b_up,
    w_down,
    b_down,
):
    nz, nf, nr, group, span = plan.nz, plan.nf, plan.nr, plan.group, plan.span
    layers, own_rows, triple = w_qkv.shape
    width = triple // 3
    own_hidden = w_down.shape[1]
    piece = own_hidden // nr
    part = -(-own_rows // nr)
    part_rows = -(-part // 16) * 16
    piece_rows = -(-piece // 16) * 16
    units = nz * piece_rows
    length = tokens.shape[1]
    total = length * nz
    scale = 1.0 / math.sqrt(HD)
    fsdp = lax.axis_index(FSDP)
    replica = lax.axis_index(REPLICA)
    seq = lax.axis_index(SEQ)
    rank = plan.rank()

    def down_of(down):
        down = lax.dynamic_slice_in_dim(down, replica * piece, piece, 0)
        return jnp.pad(down, ((0, piece_rows - piece), (0, 0)))

    def out_of(out):
        out = jnp.pad(out, ((0, nr * part + part_rows - own_rows), (0, 0)))
        out = lax.dynamic_slice_in_dim(out, replica * part, part_rows, 0)
        valid = lax.broadcasted_iota(jnp.int32, out.shape, 0)
        valid = (valid < part) & (valid + replica * part < own_rows)
        return jnp.where(valid, out, jnp.zeros_like(out))

    qkv_send = head_columns(plan, w_qkv)
    first = plan.exchange_fsdp(qkv_send[0]).reshape(nf * own_rows, 3 * span)
    hidden = plan.regroup(tokens[0]).astype(F32)
    small = jnp.concatenate(
        [norm1_gain, norm1_shift, b_query, b_value, b_out, norm2_gain, norm2_shift, b_down, b_up],
        axis=1,
    )
    each_small = small.shape[1]
    small = small.reshape(-1)
    flat_rows = -(-small.shape[0] // 2048) * 16
    small = jnp.pad(small, (0, flat_rows * 128 - small.shape[0])).reshape(flat_rows, 128)
    small = plan.gather_owners(small)
    small = small.reshape(nz * nf, flat_rows * 128)[:, : layers * each_small]
    small = small.reshape(nz * nf, layers, each_small)

    codes = segments[0] * CODE + seq * length + jnp.arange(length, dtype=jnp.int32)
    codes = plan.gather_doubling(plan.regroup(codes[None]))

    outs = jnp.concatenate([out_of(w_out[layer]) for layer in range(layers)])
    first, qkv_send, w_up, w_down, outs, small, codes = lax.optimization_barrier(
        (first, qkv_send, w_up, w_down, outs, small, codes)
    )
    grad = plan.regroup(after(cotangent[0], hidden)).astype(F32)
    up_send = unit_columns(plan, w_up, piece, piece_rows)
    prepared = []
    for layer in range(layers):
        qkv = first
        if layer:
            qkv = plan.exchange_fsdp(qkv_send[layer]).reshape(nf * own_rows, 3 * span)
        up = plan.exchange_fsdp(up_send[layer]).reshape(nf * own_rows, units)
        prepared.append((qkv, up, down_of(w_down[layer])))
    early = [prepared[0][1:], prepared[1:]]
    codes, early = lax.optimization_barrier((codes, early))
    prepared = [(first, *early[0])] + early[1]

    weights = []
    for layer, (qkv, up, down) in enumerate(prepared):
        qkv = gather_seq(qkv)
        if layer == 0:
            outs = gather_seq(outs).reshape(nz, layers, part_rows, width)
        up = gather_seq(up)
        down = gather_seq(down, lead=layer % 2 == 0)
        weights.append((qkv, up, down))

    source = plan.source()
    feature_heads = (source[:, None] * span + jnp.arange(span, dtype=jnp.int32)).reshape(-1)
    fs = jnp.array(plan.place, dtype=jnp.int32)[source]
    inner = jnp.arange(part_rows, dtype=jnp.int32)
    within = (fs % nr)[:, None, None] * part + inner
    feature_rows = (
        jnp.arange(nz, dtype=jnp.int32)[None, :, None] * (nf * own_rows)
        + (fs // nr)[:, None, None] * own_rows
        + within
    )
    feature_rows = jnp.where((inner < part) & (within < own_rows), feature_rows, -1).reshape(-1)
    select = (feature_heads[:, None] == feature_rows[None, :]).astype(BF)

    def vectors(layer):
        each = [
            small[:, layer, i * own_rows : (i + 1) * own_rows].reshape(width).astype(F32)
            for i in range(8)
        ]
        bias_up = small[:, layer, 8 * own_rows :].reshape(nz, nf, nr, piece)
        bias_up = lax.dynamic_index_in_dim(bias_up, fsdp, 1, keepdims=False)
        bias_up = lax.dynamic_index_in_dim(bias_up, replica, 1, keepdims=False)

        def mine(v):
            return lax.dynamic_slice_in_dim(
                jnp.pad(v, (0, group * span - width)), rank * span, span
            )

        bias_qkv = jnp.concatenate([mine(each[2]), jnp.zeros((span,), F32), mine(each[3])])
        bias_up = jnp.pad(bias_up, ((0, 0), (0, piece_rows - piece)))
        return each, bias_qkv, bias_up.reshape(units).astype(F32)

    vecs = [vectors(layer) for layer in range(layers)]

    def out_block(layer):
        return outs[:, layer].reshape(nz * part_rows, width)

    kept = []
    for layer in range(layers):
        qkv_w, up_w, down_w = weights[layer]
        (gain1, shift1, _, _, bias_out, gain2, shift2, bias_down), bias_qkv, bias_up = vecs[layer]
        unit1, inv1 = norm_parts(hidden)
        pieces = plan.gather_pieces(widen((unit1 * gain1 + shift1).astype(BF)))
        if layer == 0:
            grad_pieces = plan.gather_pieces(widen(after(grad.astype(BF), pieces)))
        normed, packed, lse, mixed = attend(plan, pieces, qkv_w, bias_qkv, codes, total, scale)
        out_w = out_block(layer)
        out_w = plan.gather_pieces(after(out_w, pieces) if layer else out_w)
        weights[layer] = qkv_w, out_w, up_w, down_w
        mixed = jnp.concatenate(plan.exchange(mixed), axis=1)
        mixed = dot(mixed, select).astype(BF)
        block = nz * part_rows
        mixed_own = plan.exchange(
            jnp.concatenate([mixed[:, i * block : (i + 1) * block] for i in range(group)])
        )
        middle = hidden + (project(plan, mixed, out_w) + bias_out)
        unit2, inv2 = norm_parts(middle)
        pieces = plan.gather_pieces(widen((unit2 * gain2 + shift2).astype(BF)))
        if layer == layers - 1:
            normed_two, slope, activated = lift_units(plan, pieces, up_w, bias_up)
        else:
            normed_two, slope, activated, near, far = hidden_units(
                plan, pieces, up_w, bias_up, down_w
            )
        kept.append(
            (
                unit1,
                inv1,
                normed,
                packed,
                lse,
                jnp.concatenate(mixed_own),
                unit2,
                inv2,
                normed_two,
                slope,
                activated,
            )
        )
        if layer < layers - 1:
            hidden = middle + (plan.scatter_parts(near, far) + bias_down)

    def late_up(up, layer):
        up = plan.to_owners(up)
        if plan.cube:
            ranks = [[plan.rank_of(f, r) for r in range(nr)] for f in range(nf)]
            return into_layer(
                functools.partial(units_back_kernel, nz, nf, nr, piece, piece_rows, ranks),
                plan,
                up,
                (layers, own_rows, nf * nz * nr * piece),
                layer,
                into_up,
                [],
            )
        up = jnp.stack([up[plan.back[m]] for m in range(group)])
        up = up.reshape(nf, nr, own_rows, nz, piece_rows)[..., :piece].transpose(2, 3, 0, 1, 4)
        up = up.reshape(1, own_rows, -1).astype(F32)
        return up if into_up is None else jnp.concatenate([up, into_up])

    def late_qkv(qkv, layer):
        qkv = plan.to_owners(qkv)
        if plan.cube:
            return into_layer(
                functools.partial(heads_back_kernel, group, span),
                plan,
                qkv,
                (layers, own_rows, triple),
                layer,
                into_qkv,
                [pltpu.VMEM((own_rows, 3 * group * span), F32)],
            )
        qkv = qkv.reshape(group, own_rows, 3, span).transpose(1, 2, 0, 3)
        qkv = qkv.reshape(own_rows, 3, group * span)[:, :, :width]
        qkv = qkv.reshape(1, own_rows, triple).astype(F32)
        return qkv if into_qkv is None else jnp.concatenate([qkv, into_qkv])

    def late_rows(v, rows, kept, layer, previous):
        if not plan.cube:
            v = lax.all_gather(v, REPLICA, axis=0, tiled=False)
            v = v[:, :kept].reshape(nr * kept, width)[None, :rows].astype(F32)
            return v if previous is None else jnp.concatenate([v, previous])
        operands = [v, plan.swap_x(v)]
        in_specs = [pl.BlockSpec(v.shape, lambda i, s: (0, 0))] * 2
        operands = [replica.astype(jnp.int32).reshape(1)] + operands
        aliases = {}
        if previous is not None:
            operands.append(previous)
            in_specs.append(pl.BlockSpec(memory_space=pl.ANY))
            aliases = {3: 0}
        return pl.pallas_call(
            functools.partial(rows_back_kernel, kept),
            grid_spec=pltpu.PrefetchScalarGridSpec(
                num_scalar_prefetch=1,
                grid=(1,),
                in_specs=in_specs,
                out_specs=pl.BlockSpec((1, rows, width), lambda i, s: (layer, 0, 0)),
            ),
            out_shape=sds((layers, rows, width), F32),
            input_output_aliases=aliases,
            compiler_params=pltpu.CompilerParams(vmem_limit_bytes=44 * 1024 * 1024),
            cost_estimate=pl.CostEstimate(
                flops=0, bytes_accessed=12 * v.size, transcendentals=0
            ),
        )(*operands)

    def late_down(down, layer):
        return late_rows(down, own_hidden, piece, layer, into_down)

    def late_out(out, layer):
        return late_rows(out, own_rows, part, layer, into_out)

    into_qkv = into_up = into_down = into_out = None
    smalls = [None] * layers
    late = None
    for layer in reversed(range(layers)):
        qkv_w, out_w, up_w, down_w = weights[layer]
        (gain1, _, _, _, _, gain2, _, _), _, _ = vecs[layer]
        unit1, inv1, normed, packed, lse, mixed, unit2, inv2, normed_two, slope, activated = kept[
            layer
        ]
        g_low = grad.astype(BF)
        grad_down = down_grad(plan, activated, grad_pieces, width)
        if late is not None:
            above = layer + 1
            out = scatter_seq(down_grad(plan, *late[2], width))
            if above == layers - 1:
                output = plan.regroup(hidden.astype(BF), back=True)
            into_up = late_up(late[0], above)
            into_down = late_down(late[1], above)
            into_out = late_out(out, above)
            into_qkv = late_qkv(late[3], above)
        if late is None:
            grad_pieces, grad_down = lax.optimization_barrier((grad_pieces, grad_down))
        down = scatter_seq(grad_down, lead=True)
        g_lift, grad_b_up, near, far = hidden_back(
            plan, grad_pieces, slope, down_w, up_w
        )
        grad_up = wgrad(plan, normed_two, g_lift)
        g_n2 = plan.scatter_parts(near, far)
        up = scatter_seq(grad_up).reshape(nf, own_rows, units)
        g_mid = grad + norm_pull(g_n2, unit2, inv2, gain2)
        g_att = g_mid.astype(BF)
        g_mixed = project_back(plan, g_att, out_w)
        g_mixed = dot(g_mixed, select, 1, 1).astype(BF)
        g_mixed = jnp.concatenate(
            [g_mixed[:, i * span : (i + 1) * span] for i in range(group)]
        )
        g_mixed = plan.exchange(g_mixed)
        if late is None:
            parts = lower_units(plan, after(activated, g_lift), down_w)
            hidden = middle + (plan.scatter_parts(*parts) + bias_down)
        att_pieces = plan.gather_pieces(widen(g_att))
        g_packed, g_b, near, far = attend_back(
            plan, g_mixed, packed, lse, codes, qkv_w, total, scale
        )
        grad_qkv = wgrad(plan, normed, g_packed)
        g_n1 = plan.scatter_parts(near, far)
        qkv = scatter_seq(grad_qkv)
        qkv = qkv.reshape(nf, own_rows, 3 * span)
        if layer == 0:
            into_up = late_up(up, layer)
            into_down = late_down(down, layer)
        late = (up, down, (after(mixed, g_n1 if layer else grad_qkv), att_pieces), qkv)
        smalls[layer] = (
            jnp.sum(g_n1 * unit1, axis=0),
            jnp.sum(g_n1, axis=0),
            g_b,
            jnp.sum(g_att.astype(F32), axis=0),
            jnp.sum(g_n2 * unit2, axis=0),
            jnp.sum(g_n2, axis=0),
            jnp.sum(g_low.astype(F32), axis=0),
            grad_b_up,
        )
        grad = g_mid + norm_pull(g_n1, unit1, inv1, gain1)
        if layer:
            grad_pieces = plan.gather_pieces(widen(grad.astype(BF)))
    out = scatter_seq(down_grad(plan, *late[2], width))
    grad_tokens = plan.regroup(grad.astype(BF), back=True).astype(F32)
    into_qkv = late_qkv(after(late[3], (into_up, into_down)), 0)
    output = after(output, grad).astype(F32)
    into_out = late_out(out, 0)

    def scattered(layer):
        n1g, n1s, g_b, b_o, n2g, n2s, b_d, b_u = smalls[layer]

        def place(v):
            full = lax.dynamic_update_slice_in_dim(
                jnp.zeros((group * span,), F32), v, rank * span, 0
            )
            return full[:width]

        b_u = lax.dynamic_update_slice(
            jnp.zeros((nz, nf, nr, piece), F32),
            b_u.reshape(nz, 1, 1, piece_rows)[..., :piece],
            (0, fsdp, replica, 0),
        )
        rows = [n1g, n1s, place(g_b[:span]), place(g_b[2 * span :]), b_o, n2g, n2s, b_d]
        return jnp.concatenate(
            [v.reshape(nz * nf, own_rows) for v in rows] + [b_u.reshape(nz * nf, own_hidden)],
            axis=1,
        )

    flat = jnp.concatenate([scattered(layer) for layer in range(layers)], axis=1)
    wide = lanes(-(-flat.shape[1] // 2))
    flat = jnp.pad(flat, ((0, 0), (0, 2 * wide - flat.shape[1])))
    flat = plan.scatter_small(flat.reshape(nz, nf, 2, wide))
    flat = jnp.sum(plan.to_owners_small(flat), axis=0).reshape(-1)
    flat = flat[: layers * each_small].reshape(layers, each_small)
    vec = [flat[:, i * own_rows : (i + 1) * own_rows] for i in range(8)]
    return (
        output[None],
        grad_tokens[None],
        vec[0],
        vec[1],
        into_qkv,
        vec[2],
        vec[3],
        into_out,
        vec[4],
        vec[5],
        vec[6],
        into_up,
        flat[:, 8 * own_rows :],
        into_down,
        vec[7],
    )


def solution(mesh):
    plan = Plan(mesh)
    data = P((FSDP, REPLICA), SEQ, None)
    vector = P(None, (SEQ, FSDP))
    matrix = P(None, (SEQ, FSDP), None)
    weights = (
        vector,
        vector,
        matrix,
        vector,
        vector,
        matrix,
        vector,
        vector,
        vector,
        matrix,
        vector,
        matrix,
        vector,
    )
    in_specs = (data, data, P((FSDP, REPLICA), SEQ)) + weights
    out_specs = (data, data) + weights
    return jax.shard_map(
        functools.partial(shards, plan),
        mesh=mesh,
        in_specs=in_specs,
        out_specs=out_specs,
        check_vma=False,
    )
```

```python
import functools
import math

import jax
import jax.numpy as jnp
from jax import lax
from jax.experimental import pallas as pl
from jax.experimental.pallas import tpu as pltpu
from jax.sharding import PartitionSpec as P


HEADS = 25
HD = 64
BF = jnp.bfloat16
F32 = jnp.float32
CODE = 65536
LOW = -1e30
SEQ, FSDP, REPLICA = "seq", "fsdp", "replica"
QK, PV, PK = "sqhd,skhd->shqk", "shqk,skhd->sqhd", "shqk,sqhd->skhd"
ALL = (SEQ, FSDP, REPLICA)
GROUP = (FSDP, REPLICA)
OWNERS = (SEQ, FSDP)


def dot(a, b, ca=1, cb=0):
    return lax.dot_general(a, b, (((ca,), (cb,)), ((), ())), preferred_element_type=F32)


def norm_parts(v):
    mean = jnp.mean(v, axis=-1, keepdims=True)
    centred = v - mean
    spread = jnp.mean(centred * centred, axis=-1, keepdims=True)
    inv = lax.rsqrt(spread + 1e-05)
    return centred * inv, inv


def norm_pull(grad, unit, inv, gain):
    scaled = grad * gain
    first = jnp.mean(scaled, axis=-1, keepdims=True)
    second = jnp.mean(scaled * unit, axis=-1, keepdims=True)
    return inv * (scaled - first - unit * second)


def gelu_both(value):
    tanh = jnp.tanh(0.7978845608028654 * (value + 0.044715 * value * value * value))
    inner = 0.7978845608028654 * (1.0 + 3.0 * 0.044715 * value * value)
    half = 0.5 * (1.0 + tanh)
    return value * half, half + 0.5 * value * (1.0 - tanh * tanh) * inner


class Plan:
    def __init__(self, mesh):
        self.nz = mesh.shape[SEQ]
        self.nf = mesh.shape[FSDP]
        self.nr = mesh.shape[REPLICA]
        self.group = self.nf * self.nr
        self.cube = self.nf == 4 and self.nr == 2
        self.heads = 2 * -(-HEADS // (2 * self.group))
        self.span = self.heads * HD
        order = sorted(
            (self.rank_of(f, r), f * self.nr + r) for f in range(self.nf) for r in range(self.nr)
        )
        self.place = [member for _, member in order]
        self.back = [0] * self.group
        for rank, member in order:
            self.back[member] = rank

    def rank_of(self, f, r):
        half = self.group // 2
        if self.nf % 2:
            return f * self.nr + r
        return (f % 2) * half + (f // 2) * self.nr + r

    def rank(self):
        return self.rank_of(lax.axis_index(FSDP), lax.axis_index(REPLICA))

    def regroup(self, v, back=False):
        nz = self.nz
        pairs = []
        for z in range(nz):
            for g in range(self.group):
                goal = g % nz
                slot = (g // nz) * nz + (z ^ goal if nz & (nz - 1) == 0 else z)
                pairs.append((z * self.group + self.place[g], goal * self.group + self.place[slot]))
        if back:
            pairs = [(there, here) for here, there in pairs]
        return lax.ppermute(v, ALL, pairs)

    def swap_core(self, v):
        return lax.ppermute(v, FSDP, [(f, f ^ 1) for f in range(self.nf)])

    def swap_y(self, v):
        return lax.ppermute(v, FSDP, [(f, f ^ 2) for f in range(self.nf)])

    def swap_x(self, v):
        return lax.ppermute(v, REPLICA, [(r, r ^ 1) for r in range(self.nr)])

    def swap_xy(self, v):
        pairs = [
            (f * self.nr + r, (f ^ 2) * self.nr + (r ^ 1))
            for f in range(self.nf)
            for r in range(self.nr)
        ]
        return lax.ppermute(v, GROUP, pairs)

    def source(self):
        base = jnp.arange(self.group, dtype=jnp.int32)
        return base ^ self.rank() if self.cube else base

    def gather_pieces(self, v):
        if not self.cube:
            full = lax.all_gather(v, GROUP, axis=0, tiled=False)
            return [full[member] for member in self.place]
        near = [v, self.swap_x(v), self.swap_y(v), self.swap_xy(v)]
        return near + [self.swap_core(piece) for piece in near]

    def gather_doubling(self, v):
        if not self.cube:
            return jnp.concatenate(self.gather_pieces(v))
        for swap in (self.swap_x, self.swap_y, self.swap_core):
            v = jnp.concatenate([v, swap(v)])
        return v

    def scatter_parts(self, near, far, gate=None):
        if not self.cube:
            blocks = jnp.concatenate([near.astype(BF), far])
            rows = blocks.shape[0] // self.group
            blocks = blocks.reshape(self.group, rows, -1)[jnp.array(self.back)]
            blocks = blocks.reshape(self.group * rows, -1)
            return lax.psum_scatter(blocks, GROUP, scatter_dimension=0, tiled=True).astype(F32)
        rows, columns = near.shape[0] // 4, near.shape[1]
        own, to_x, to_y, to_xy = call(
            fold_kernel,
            [sds((rows, columns), F32)] + [sds((rows, lanes(columns)), BF)] * 3,
            [],
            0,
            [near, self.swap_core(far)],
        )
        parts = self.swap_xy(to_xy), self.swap_x(to_x), self.swap_y(to_y)
        if gate is not None:
            own = after(own, gate)
        parts = [part[:, :columns].astype(F32) for part in parts]
        return own + parts[0] + parts[1] + parts[2]

    def exchange(self, v):
        if not self.cube:
            v = v.reshape(self.group, -1, v.shape[1])[jnp.array(self.back)]
            v = lax.all_to_all(v, GROUP, split_axis=0, concat_axis=0, tiled=True)
            return [v[member] for member in self.place]
        rows = v.shape[0] // 8
        half = 4 * rows
        far = self.swap_core(v[half:])
        out = [[v[:rows], far[:rows]]]
        for i, swap in ((1, self.swap_x), (2, self.swap_y), (3, self.swap_xy)):
            both = swap(
                jnp.concatenate([v[i * rows : (i + 1) * rows], far[i * rows : (i + 1) * rows]])
            )
            out.append([both[:rows], both[rows:]])
        return [pair[0] for pair in out] + [pair[1] for pair in out]

    def flips(self, v):
        f = lax.axis_index(FSDP)
        v = v.reshape((2, 2) + v.shape[1:])
        v = jnp.where(f // 2 == 1, jnp.flip(v, 0), v)
        return jnp.where(f % 2 == 1, jnp.flip(v, 1), v)

    def gather_owners(self, v):
        if not self.cube or self.nz != 4:
            return lax.all_gather(v, OWNERS, axis=0, tiled=False)
        z, f = lax.axis_index(SEQ), lax.axis_index(FSDP)
        far = [
            lax.ppermute(v, SEQ, [(i, i ^ d) for i in range(4)]) if d else v for d in range(4)
        ]
        v = jnp.stack(far).reshape((2, 2) + v.shape)
        v = jnp.where(z // 2 == 1, jnp.flip(v, 0), v)
        v = jnp.where(z % 2 == 1, jnp.flip(v, 1), v)
        other = self.swap_core(v)
        v = jnp.stack([jnp.where(f % 2 == 0, v, other), jnp.where(f % 2 == 0, other, v)], axis=2)
        other = self.swap_y(v)
        v = jnp.stack([jnp.where(f // 2 == 0, v, other), jnp.where(f // 2 == 0, other, v)], axis=2)
        return v.reshape((16,) + v.shape[4:])

    def exchange_fsdp(self, v):
        if not self.cube:
            return lax.all_to_all(v, FSDP, split_axis=0, concat_axis=0, tiled=True)
        shape = v.shape
        v = self.flips(v)
        both = jnp.stack([v[:, 0], self.swap_core(v[:, 1])], axis=1)
        return self.flips(jnp.stack([both[0], self.swap_y(both[1])]).reshape(shape)).reshape(shape)

    def scatter_small(self, v):
        if not self.cube or self.nz != 4:
            return lax.psum_scatter(v, SEQ, scatter_dimension=0, tiled=False)
        z = lax.axis_index(SEQ)
        total = lax.dynamic_index_in_dim(v, z, 0, keepdims=False)
        for d in range(1, 4):
            other = lax.dynamic_index_in_dim(v, z ^ d, 0, keepdims=False)
            total = total + lax.ppermute(other, SEQ, [(i, i ^ d) for i in range(4)])
        return total

    def to_owners_small(self, v):
        if not self.cube:
            v = lax.all_to_all(v, FSDP, split_axis=0, concat_axis=0, tiled=True)
            v = lax.all_gather(v, REPLICA, axis=1, tiled=False)
            return jnp.stack([v[m // self.nr, m % self.nr] for m in self.place])
        v = self.flips(v)
        far = self.swap_core(v[:, 1])
        here = jnp.stack([v[0, 0], far[0]])
        there = jnp.stack([v[1, 0], far[1]])
        return jnp.stack(
            [here, self.swap_x(here), self.swap_y(there), self.swap_xy(there)], axis=1
        ).reshape((8,) + v.shape[2:])

    def to_owners(self, v):
        if not self.cube:
            return self.to_owners_small(v)
        nf, rows, columns = v.shape
        f = lax.axis_index(FSDP)
        pick = (f ^ jnp.arange(nf, dtype=jnp.int32)).astype(jnp.int32)
        pair = sds((2, rows, columns), BF)
        near, far = pl.pallas_call(
            pick_kernel,
            grid_spec=pltpu.PrefetchScalarGridSpec(
                num_scalar_prefetch=1,
                grid=(1,),
                in_specs=[pl.BlockSpec(v.shape, lambda i, s: (0, 0, 0))],
                out_specs=[pl.BlockSpec(pair.shape, lambda i, s: (0, 0, 0))] * 2,
            ),
            out_shape=[pair] * 2,
            compiler_params=pltpu.CompilerParams(vmem_limit_bytes=44 * 1024 * 1024),
        )(pick, v)
        here, there = call(pair_kernel, [pair] * 2, [], 0, [near, self.swap_core(far)])
        return [here, self.swap_x(here), self.swap_y(there), self.swap_xy(there)]


def pick_kernel(order, v, near, far):
    for y in range(2):
        near[y] = v[order[2 * y]]
        far[y] = v[order[2 * y + 1]]


def pair_kernel(near, far, here, there):
    for y, out in enumerate((here, there)):
        out[0] = near[y]
        out[1] = far[y]


def gather_seq(v, lead=False):
    if lead:
        return lax.all_gather(v[None], SEQ, axis=1, tiled=True)[0]
    return lax.all_gather(v, SEQ, axis=0, tiled=True)


def scatter_seq(v, lead=False):
    if lead:
        return lax.psum_scatter(v[None], SEQ, scatter_dimension=1, tiled=True)[0]
    return lax.psum_scatter(v, SEQ, scatter_dimension=0, tiled=True)


def call(kernel, outs, scratch, flops, operands, **more):
    params = pltpu.CompilerParams(vmem_limit_bytes=44 * 1024 * 1024)
    size = sum(math.prod(o.shape) * o.dtype.itemsize for o in list(outs) + list(operands))
    return pl.pallas_call(
        kernel,
        out_shape=tuple(outs),
        scratch_shapes=scratch,
        compiler_params=params,
        cost_estimate=pl.CostEstimate(
            flops=int(flops), bytes_accessed=int(size), transcendentals=0
        ),
        **more,
    )(*operands)


def lanes(columns):
    return -(-columns // 128) * 128


def widen(v):
    return jnp.pad(v, ((0, 0), (0, lanes(v.shape[1]) - v.shape[1])))


def sds(shape, dtype):
    return jax.ShapeDtypeStruct(shape, dtype)


def fold_kernel(near, far, own, to_x, to_y, to_xy):
    rows, columns = own.shape
    own[...] = near[:rows, :] + far[:rows, :columns].astype(F32)
    for i, out in ((1, to_x), (2, to_y), (3, to_xy)):
        at = slice(i * rows, (i + 1) * rows)
        out[:, :columns] = (near[at, :] + far[at, :columns].astype(F32)).astype(BF)


def wgrad_kernel(left, right, out):
    tall = out.shape[0]
    block = 256

    def body(i, carry):
        at = pl.ds(pl.multiple_of(i * block, block), block)
        out[at, :] = dot(left[:, at], right[...], 0, 0).astype(BF)
        return carry

    whole = tall // block
    lax.fori_loop(0, whole, body, 0)
    if tall % block:
        out[whole * block :, :] = dot(left[:, whole * block :], right[...], 0, 0).astype(BF)


def wgrad(plan, left, right):
    if not plan.cube:
        return dot(left, right, 0, 0).astype(BF)
    tall, width = left.shape[1], right.shape[1]
    return call(
        wgrad_kernel, [sds((tall, width), BF)], [], 2 * left.size * width, [left, right]
    )[0]


def after(v, other):
    return lax.optimization_barrier((v, other))[0]


def project_kernel(count, left, *refs):
    block, width = refs[0].shape[0], refs[-1].shape[1]
    total = dot(left[:, :block], refs[0][:, :width])
    for i in range(1, count):
        total = total + dot(left[:, i * block : (i + 1) * block], refs[i][:, :width])
    refs[-1][...] = total


def project(plan, left, pieces, width):
    if not plan.cube:
        return dot(left, jnp.concatenate(pieces)[:, :width])
    shape = sds((left.shape[0], width), F32)
    kernel = functools.partial(project_kernel, len(pieces))
    return call(kernel, [shape], [], 2 * left.size * shape.shape[1], [left, *pieces])[0]


def project_back_kernel(count, left, *refs):
    block, width = refs[0].shape[0], left.shape[1]
    for i in range(count):
        part = dot(left[...], refs[i][:, :width], 1, 1)
        refs[-1][:, i * block : (i + 1) * block] = part.astype(BF)


def project_back(plan, left, pieces):
    if not plan.cube:
        return dot(left, jnp.concatenate(pieces)[:, : left.shape[1]], 1, 1).astype(BF)
    shape = sds((left.shape[0], len(pieces) * pieces[0].shape[0]), BF)
    kernel = functools.partial(project_back_kernel, len(pieces))
    return call(kernel, [shape], [], 2 * left.size * shape.shape[1], [left, *pieces])[0]


def first_half(shape):
    return lax.broadcasted_iota(jnp.int32, shape, 1) < HD


def attend_kernel(count, total, span, scale, *refs):
    pieces = refs[:count]
    w, bias, code_col, code_row, full, packed, lse, mixed = refs[count:]
    rows = pieces[0].shape[0]
    for i, piece in enumerate(pieces):
        full[i * rows : (i + 1) * rows, :] = piece[:, : full.shape[1]]
    block = 2 * rows

    def project(i, carry):
        at = pl.ds(pl.multiple_of(i * block, block), block)
        packed[at, :] = (dot(full[at, :], w[...]) + bias[...]).astype(BF)
        return carry

    lax.fori_loop(0, count // 2, project, 0)
    blocks = total // rows
    left = first_half((rows, 2 * HD))
    lane = lax.broadcasted_iota(jnp.int32, (rows, 128), 1)

    def queries(i, carry):
        at = pl.ds(pl.multiple_of(i * rows, rows), rows)
        seq = i // blocks
        keys_at = pl.ds(pl.multiple_of(seq * total, total), total)
        code_q = code_col[at, :]
        code_k = code_row[pl.ds(seq, 1), :]
        allowed = (code_k <= code_q) & (code_k >= (code_q // CODE) * CODE)
        stats = jnp.zeros((rows, 128), F32)
        for pair in range(span // 128):
            q = packed[at, pair * 128 : pair * 128 + 128]
            k = packed[keys_at, span + pair * 128 : span + pair * 128 + 128]
            v = packed[keys_at, 2 * span + pair * 128 : 2 * span + pair * 128 + 128]
            both = []
            for side in range(2):
                own = left if side == 0 else ~left
                scores = dot(jnp.where(own, q, jnp.zeros_like(q)), k, 1, 1) * scale
                scores = jnp.where(allowed, scores, LOW)
                top = jnp.max(scores, axis=1, keepdims=True)
                expo = jnp.exp(scores - top)
                denom = jnp.sum(expo, axis=1, keepdims=True)
                probs = (expo * (1.0 / denom)).astype(BF)
                both.append(dot(probs, v))
                stats = jnp.where(lane == 2 * pair + side, top + jnp.log(denom), stats)
            mixed[at, pair * 128 : pair * 128 + 128] = jnp.where(left, both[0], both[1]).astype(BF)
        lse[:, at] = stats.T[: lse.shape[0], :]
        return carry

    lax.fori_loop(0, count, queries, 0)


def attend(plan, pieces, w, bias, codes, total, scale):
    rows, width = pieces[0].shape[0], w.shape[0]
    count, span = plan.group, plan.span
    if not plan.cube:
        full = jnp.concatenate(pieces)[:, :width]
        packed = (dot(full, w) + bias).astype(BF)
        q, k, v = (
            packed[:, i * span : (i + 1) * span].reshape(-1, total, plan.heads, HD)
            for i in range(3)
        )
        allowed = mask_of(codes, total)
        scores = jnp.einsum(QK, q, k, preferred_element_type=F32) * scale
        scores = jnp.where(allowed[:, None], scores, LOW)
        top = jnp.max(scores, axis=-1, keepdims=True)
        expo = jnp.exp(scores - top)
        denom = jnp.sum(expo, axis=-1, keepdims=True)
        probs = (expo / denom).astype(BF)
        mixed = jnp.einsum(PV, probs, v, preferred_element_type=F32)
        return full, packed, top + jnp.log(denom), mixed.reshape(-1, span).astype(BF)
    tall = count * rows
    return call(
        functools.partial(attend_kernel, count, total, span, scale),
        [
            sds((tall, width), BF),
            sds((tall, 3 * span), BF),
            sds((8, tall), F32),
            sds((tall, span), BF),
        ],
        [],
        2 * tall * width * 3 * span + 8 * tall * total * span,
        [*pieces, w, bias[None], codes.reshape(-1, 1), codes.reshape(-1, total)],
    )


def mask_of(codes, total):
    code = codes.reshape(-1, total)
    low = (code // CODE) * CODE
    return (code[:, None, :] <= code[:, :, None]) & (code[:, None, :] >= low[:, :, None])


def attend_back_kernel(count, total, span, scale, *refs):
    pieces = refs[:count]
    packed, lse, code_col, code_row, w, g_packed, g_bias, near, far, gm, g_k, g_v = refs[count:]
    rows = pieces[0].shape[0]
    for i, piece in enumerate(pieces):
        gm[i * rows : (i + 1) * rows, :] = piece[...]
    blocks = total // rows
    left = first_half((rows, 2 * HD))

    def sequence(seq, carry):
        keys_at = pl.ds(pl.multiple_of(seq * total, total), total)
        code_k = code_col[keys_at, :]
        for pair in range(span // 128):
            lanes = slice(pair * 128, pair * 128 + 128)
            k_lanes = slice(span + pair * 128, span + pair * 128 + 128)
            v_lanes = slice(2 * span + pair * 128, 2 * span + pair * 128 + 128)
            k = packed[keys_at, k_lanes]
            v = packed[keys_at, v_lanes]
            g_k[...] = jnp.zeros_like(g_k)
            g_v[...] = jnp.zeros_like(g_v)

            def queries(i, inner):
                at = pl.ds(pl.multiple_of(seq * total + i * rows, rows), rows)
                code_q = code_row[pl.ds(seq * blocks + i, 1), :]
                allowed = (code_k <= code_q) & (code_k >= (code_q // CODE) * CODE)
                q = packed[at, lanes]
                g = gm[at, lanes]
                both = []
                for side in range(2):
                    own = left if side == 0 else ~left
                    q_own = jnp.where(own, q, jnp.zeros_like(q))
                    g_own = jnp.where(own, g, jnp.zeros_like(g))
                    scores = dot(k, q_own, 1, 1) * scale
                    row = 2 * pair + side
                    probs = jnp.exp(jnp.where(allowed, scores, LOW) - lse[row : row + 1, at])
                    g_probs = dot(v, g_own, 1, 1)
                    each = jnp.sum(g_probs * probs, axis=0, keepdims=True)
                    g_scores = (probs * (g_probs - each)).astype(BF)
                    g_v[...] += dot(probs.astype(BF), g_own)
                    g_k[...] += dot(g_scores, q_own)
                    both.append(dot(g_scores, k, 0, 0))
                g_packed[at, lanes] = (jnp.where(left, both[0], both[1]) * scale).astype(BF)
                return inner

            lax.fori_loop(0, blocks, queries, 0)
            g_packed[keys_at, k_lanes] = (g_k[...] * scale).astype(BF)
            g_packed[keys_at, v_lanes] = g_v[...].astype(BF)
        return carry

    lax.fori_loop(0, count // blocks, sequence, 0)
    g_bias[...] = jnp.sum(g_packed[...].astype(F32), axis=0, keepdims=True)
    spread_out(g_packed, w, near, far, 2 * rows)


def spread_out(left, right, near, far, block):
    half = near.shape[0]

    def first(i, carry):
        at = pl.ds(pl.multiple_of(i * block, block), block)
        near[at, :] = dot(left[at, :], right[...], 1, 1)
        return carry

    def second(i, carry):
        at = pl.ds(pl.multiple_of(i * block, block), block)
        far[at, : near.shape[1]] = dot(
            left[pl.ds(pl.multiple_of(half + i * block, block), block), :], right[...], 1, 1
        ).astype(BF)
        return carry

    lax.fori_loop(0, half // block, first, 0)
    lax.fori_loop(0, half // block, second, 0)


def halves(v):
    half = v.shape[0] // 2
    return v[:half], v[half:].astype(BF)


def attend_back(plan, pieces, packed, lse, codes, w, total, scale):
    count, span = plan.group, plan.span
    rows = pieces[0].shape[0]
    width = w.shape[0]
    if not plan.cube:
        q, k, v = (
            packed[:, i * span : (i + 1) * span].reshape(-1, total, plan.heads, HD)
            for i in range(3)
        )
        gm = jnp.concatenate(pieces).reshape(-1, total, plan.heads, HD)
        allowed = mask_of(codes, total)
        scores = jnp.einsum(QK, q, k, preferred_element_type=F32) * scale
        probs = jnp.exp(jnp.where(allowed[:, None], scores, LOW) - lse)
        g_probs = jnp.einsum(QK, gm, v, preferred_element_type=F32)
        g_v = jnp.einsum(PK, probs.astype(BF), gm, preferred_element_type=F32)
        row = jnp.sum(g_probs * probs, axis=-1, keepdims=True)
        g_s = (probs * (g_probs - row)).astype(BF)
        g_q = jnp.einsum(PV, g_s, k, preferred_element_type=F32) * scale
        g_k = jnp.einsum(PK, g_s, q, preferred_element_type=F32) * scale
        g_packed = jnp.concatenate(
            [u.reshape(-1, span).astype(BF) for u in (g_q, g_k, g_v)], axis=1
        )
        near, far = halves(dot(g_packed, w, 1, 1))
        return g_packed, jnp.sum(g_packed.astype(F32), axis=0), near, far
    tall = count * rows
    g_packed, g_bias, near, far = call(
        functools.partial(attend_back_kernel, count, total, span, scale),
        [
            sds((tall, 3 * span), BF),
            sds((1, 3 * span), F32),
            sds((tall // 2, width), F32),
            sds((tall // 2, lanes(width)), BF),
        ],
        [pltpu.VMEM((tall, span), BF)] + [pltpu.VMEM((total, 128), F32)] * 2,
        2 * tall * width * 3 * span + 20 * tall * total * span,
        [*pieces, packed, lse, codes.reshape(-1, 1), codes.reshape(-1, rows), w],
    )
    return g_packed, g_bias[0], near, far


def hidden_kernel(count, *refs):
    pieces = refs[:count]
    up, bias, down, full, slope, activated, near, far = refs[count:]
    rows = pieces[0].shape[0]
    for i, piece in enumerate(pieces):
        full[i * rows : (i + 1) * rows, :] = piece[:, : full.shape[1]]
    block = 2 * rows
    half = near.shape[0]

    def lift(at):
        value, pull = gelu_both(dot(full[at, :], up[...]) + bias[...])
        value = value.astype(BF)
        activated[at, :] = value
        slope[at, :] = pull.astype(BF)
        return dot(value, down[...])

    def first(i, carry):
        at = pl.ds(pl.multiple_of(i * block, block), block)
        near[at, :] = lift(at)
        return carry

    def second(i, carry):
        at = pl.ds(pl.multiple_of(i * block, block), block)
        out = lift(pl.ds(pl.multiple_of(half + i * block, block), block))
        far[at, : near.shape[1]] = out.astype(BF)
        return carry

    lax.fori_loop(0, half // block, first, 0)
    lax.fori_loop(0, half // block, second, 0)


def lift_kernel(count, *refs):
    pieces = refs[:count]
    up, bias, full, slope, activated = refs[count:]
    rows = pieces[0].shape[0]
    for i, piece in enumerate(pieces):
        full[i * rows : (i + 1) * rows, :] = piece[:, : full.shape[1]]
    block = 2 * rows

    def lift(i, carry):
        at = pl.ds(pl.multiple_of(i * block, block), block)
        value, pull = gelu_both(dot(full[at, :], up[...]) + bias[...])
        activated[at, :] = value.astype(BF)
        slope[at, :] = pull.astype(BF)
        return carry

    lax.fori_loop(0, count // 2, lift, 0)


def lift_units(plan, pieces, up, bias):
    rows, width = pieces[0].shape[0], up.shape[0]
    if not plan.cube:
        full = jnp.concatenate(pieces)[:, :width]
        value, pull = gelu_both(dot(full, up) + bias)
        return full, pull.astype(BF), value.astype(BF)
    tall, units = plan.group * rows, up.shape[1]
    return call(
        functools.partial(lift_kernel, plan.group),
        [sds((tall, width), BF), sds((tall, units), BF), sds((tall, units), BF)],
        [],
        2 * tall * width * units,
        [*pieces, up, bias[None]],
    )


def lower_kernel(block, left, right, near, far):
    half, width = near.shape

    def first(i, carry):
        at = pl.ds(pl.multiple_of(i * block, block), block)
        near[at, :] = dot(left[at, :], right[...])
        return carry

    def second(i, carry):
        at = pl.ds(pl.multiple_of(i * block, block), block)
        rows = left[pl.ds(pl.multiple_of(half + i * block, block), block), :]
        far[at, :width] = dot(rows, right[...]).astype(BF)
        return carry

    lax.fori_loop(0, half // block, first, 0)
    lax.fori_loop(0, half // block, second, 0)


def lower_units(plan, activated, down):
    tall, width = activated.shape[0], down.shape[1]
    if not plan.cube:
        return halves(dot(activated, down))
    return call(
        functools.partial(lower_kernel, 2 * (tall // plan.group)),
        [sds((tall // 2, width), F32), sds((tall // 2, lanes(width)), BF)],
        [],
        2 * activated.size * width,
        [activated, down],
    )


def hidden_units(plan, pieces, up, bias, down):
    rows, width = pieces[0].shape[0], up.shape[0]
    if not plan.cube:
        full = jnp.concatenate(pieces)[:, :width]
        value, pull = gelu_both(dot(full, up) + bias)
        value = value.astype(BF)
        return (full, pull.astype(BF), value) + halves(dot(value, down))
    tall, units = plan.group * rows, up.shape[1]
    return call(
        functools.partial(hidden_kernel, plan.group),
        [
            sds((tall, width), BF),
            sds((tall, units), BF),
            sds((tall, units), BF),
            sds((tall // 2, width), F32),
            sds((tall // 2, lanes(width)), BF),
        ],
        [],
        4 * tall * width * units,
        [*pieces, up, bias[None], down],
    )


def hidden_back_kernel(count, *refs):
    pieces = refs[:count]
    slope, down, up, g_lift, g_bias, near, far, full = refs[count:]
    rows = pieces[0].shape[0]
    for i, piece in enumerate(pieces):
        full[i * rows : (i + 1) * rows, :] = piece[:, : full.shape[1]]
    block = 2 * rows

    def pull(i, carry):
        at = pl.ds(pl.multiple_of(i * block, block), block)
        g_lift[at, :] = (dot(full[at, :], down[...], 1, 1) * slope[at, :].astype(F32)).astype(BF)
        return carry

    lax.fori_loop(0, count // 2, pull, 0)
    spread_out(g_lift, up, near, far, block)
    g_bias[...] = jnp.sum(g_lift[...].astype(F32), axis=0, keepdims=True)


def hidden_back(plan, pieces, slope, down, up):
    rows, width = pieces[0].shape[0], up.shape[0]
    if not plan.cube:
        full = jnp.concatenate(pieces)[:, :width]
        g_lift = (dot(full, down, 1, 1) * slope.astype(F32)).astype(BF)
        return (g_lift, jnp.sum(g_lift.astype(F32), axis=0)) + halves(dot(g_lift, up, 1, 1))
    tall, units = plan.group * rows, up.shape[1]
    g_lift, g_bias, near, far = call(
        functools.partial(hidden_back_kernel, plan.group),
        [
            sds((tall, units), BF),
            sds((1, units), F32),
            sds((tall // 2, width), F32),
            sds((tall // 2, lanes(width)), BF),
        ],
        [pltpu.VMEM((tall, width), BF)],
        4 * tall * width * units,
        [*pieces, slope, down, up],
    )
    return g_lift, g_bias[0], near, far


def down_grad_kernel(count, *refs):
    left, out, full = refs[count:]
    rows = refs[0].shape[0]
    for i, piece in enumerate(refs[:count]):
        full[i * rows : (i + 1) * rows, :] = piece[:, : full.shape[1]]
    wgrad_kernel(left, full, out)


def down_grad(plan, left, pieces, width):
    if not plan.cube:
        return dot(left, jnp.concatenate(pieces)[:, :width], 0, 0).astype(BF)
    tall, units = left.shape
    return call(
        functools.partial(down_grad_kernel, plan.group),
        [sds((units, width), BF)],
        [pltpu.VMEM((tall, width), BF)],
        2 * left.size * width,
        [*pieces, left],
    )[0]


def head_columns_kernel(nf, ranks, span, x_ref, w_ref, out, wide):
    width = w_ref.shape[2] // 3
    padded = wide.shape[1] // 3
    w = w_ref[0].astype(F32)
    for i in range(3):
        wide[:, i * padded : i * padded + width] = w[:, i * width : (i + 1) * width]
        if padded > width:
            wide[:, i * padded + width : (i + 1) * padded] = jnp.zeros(
                (wide.shape[0], padded - width), F32
            )
    for x, row in enumerate(ranks):

        @pl.when(x_ref[0] == x)
        def _():
            for f in range(nf):
                for i in range(3):
                    start = i * padded + row[f] * span
                    out[0, f, :, i * span : (i + 1) * span] = wide[:, start : start + span].astype(
                        BF
                    )


def unit_columns_kernel(nz, nf, nr, piece, piece_rows, x_ref, w_ref, out):
    w = w_ref[0].astype(F32)
    for x in range(nr):

        @pl.when(x_ref[0] == x)
        def _():
            for f in range(nf):
                part = []
                for z in range(nz):
                    start = ((z * nf + f) * nr + x) * piece
                    part.append(w[:, start : start + piece])
                    if piece_rows > piece:
                        part.append(jnp.zeros((w.shape[0], piece_rows - piece), F32))
                out[0, f] = jnp.concatenate(part, axis=1).astype(BF)


def layered(kernel, x, w, columns, nf, scratch):
    layers, rows, full = w.shape
    return pl.pallas_call(
        kernel,
        grid_spec=pltpu.PrefetchScalarGridSpec(
            num_scalar_prefetch=1,
            grid=(layers,),
            in_specs=[pl.BlockSpec((1, rows, full), lambda i, s: (i, 0, 0))],
            out_specs=pl.BlockSpec((1, nf, rows, columns), lambda i, s: (i, 0, 0, 0)),
            scratch_shapes=scratch,
        ),
        out_shape=sds((layers, nf, rows, columns), BF),
        compiler_params=pltpu.CompilerParams(vmem_limit_bytes=44 * 1024 * 1024),
        cost_estimate=pl.CostEstimate(flops=0, bytes_accessed=4 * w.size, transcendentals=0),
    )(x, w)


def head_columns(plan, w):
    layers, rows, triple = w.shape
    nf, nr, span, group = plan.nf, plan.nr, plan.span, plan.group
    ranks = [[plan.rank_of(f, r) for f in range(nf)] for r in range(nr)]
    x = lax.axis_index(REPLICA)
    if not plan.cube:
        width = triple // 3
        v = w.reshape(layers, rows, 3, width)
        v = jnp.pad(v, ((0, 0), (0, 0), (0, 0), (0, group * span - width)))
        v = jnp.take(v.reshape(layers, rows, 3, group, span), jnp.array(ranks)[x], axis=3)
        return v.transpose(0, 3, 1, 2, 4).reshape(layers, nf, rows, 3 * span)
    return layered(
        functools.partial(head_columns_kernel, nf, ranks, span),
        x.astype(jnp.int32).reshape(1),
        w,
        3 * span,
        nf,
        [pltpu.VMEM((rows, 3 * group * span), F32)],
    )


def unit_columns(plan, w, piece, piece_rows):
    layers, rows, _ = w.shape
    nz, nf, nr = plan.nz, plan.nf, plan.nr
    x = lax.axis_index(REPLICA)
    if not plan.cube:
        v = w.reshape(layers, rows, nz, nf, nr, piece)
        v = lax.dynamic_index_in_dim(v, x, 4, keepdims=False)
        v = jnp.pad(v, ((0, 0),) * 4 + ((0, piece_rows - piece),))
        return v.transpose(0, 3, 1, 2, 4).reshape(layers, nf, rows, nz * piece_rows)
    return layered(
        functools.partial(unit_columns_kernel, nz, nf, nr, piece, piece_rows),
        x.astype(jnp.int32).reshape(1),
        w,
        nz * piece_rows,
        nf,
        [],
    )


def stacked(pairs, block):
    for i, pair in enumerate(pairs):
        for core in range(2):
            block[4 * core + i] = pair[core]


def heads_back_kernel(group, span, src_ref, *refs):
    out, wide, v_ref = refs[-3:]
    stacked(refs[:4], v_ref)
    width = out.shape[2] // 3
    padded = group * span
    for rank in range(group):
        block = v_ref[src_ref[rank]].astype(F32)
        for i in range(3):
            wide[:, i * padded + rank * span : i * padded + (rank + 1) * span] = block[
                :, i * span : (i + 1) * span
            ]
    for i in range(3):
        out[0, :, i * width : (i + 1) * width] = wide[:, i * padded : i * padded + width]


def units_back_kernel(nz, nf, nr, piece, piece_rows, ranks, src_ref, *refs):
    out, v_ref = refs[-2:]
    stacked(refs[:4], v_ref)
    for f in range(nf):
        blocks = [v_ref[src_ref[ranks[f][r]]].astype(F32) for r in range(nr)]
        for z in range(nz):
            part = [block[:, z * piece_rows : z * piece_rows + piece] for block in blocks]
            start = (z * nf + f) * nr * piece
            out[0, :, start : start + nr * piece] = jnp.concatenate(part, axis=1)


def into_layer(kernel, plan, pairs, shape, layer, previous, scratch):
    operands = [plan.source().astype(jnp.int32), *pairs]
    in_specs = [pl.BlockSpec(v.shape, lambda i, s: (0, 0, 0)) for v in pairs]
    scratch = scratch + [pltpu.VMEM((8,) + pairs[0].shape[1:], BF)]
    aliases = {}
    if previous is not None:
        operands.append(previous)
        in_specs.append(pl.BlockSpec(memory_space=pl.ANY))
        aliases = {5: 0}
    return pl.pallas_call(
        kernel,
        grid_spec=pltpu.PrefetchScalarGridSpec(
            num_scalar_prefetch=1,
            grid=(1,),
            in_specs=in_specs,
            out_specs=pl.BlockSpec((1,) + shape[1:], lambda i, s: (layer, 0, 0)),
            scratch_shapes=scratch,
        ),
        out_shape=sds(shape, F32),
        input_output_aliases=aliases,
        compiler_params=pltpu.CompilerParams(vmem_limit_bytes=44 * 1024 * 1024),
        cost_estimate=pl.CostEstimate(flops=0, bytes_accessed=48 * pairs[0].size, transcendentals=0),
    )(*operands)


def rows_back_kernel(kept, x_ref, own, other, *refs):
    out = refs[-1]
    for x in range(2):

        @pl.when(x_ref[0] == x)
        def _():
            first, second = (own, other) if x == 0 else (other, own)
            first, second = (v[...].astype(F32)[:kept] for v in (first, second))
            if kept % 8:
                out[0] = jnp.concatenate([first, second])
            else:
                out[0, :kept, :] = first
                out[0, kept:, :] = second


def shards(
    plan,
    tokens,
    cotangent,
    segments,
    norm1_gain,
    norm1_shift,
    w_qkv,
    b_query,
    b_value,
    w_out,
    b_out,
    norm2_gain,
    norm2_shift,
    w_up,
    b_up,
    w_down,
    b_down,
):
    nz, nf, nr, group, span = plan.nz, plan.nf, plan.nr, plan.group, plan.span
    layers, own_rows, triple = w_qkv.shape
    width = triple // 3
    own_hidden = w_down.shape[1]
    piece = own_hidden // nr
    part = -(-own_rows // nr)
    part_rows = -(-part // 16) * 16
    piece_rows = -(-piece // 16) * 16
    units = nz * piece_rows
    length = tokens.shape[1]
    total = length * nz
    scale = 1.0 / math.sqrt(HD)
    fsdp = lax.axis_index(FSDP)
    replica = lax.axis_index(REPLICA)
    seq = lax.axis_index(SEQ)
    rank = plan.rank()

    def down_of(down):
        down = lax.dynamic_slice_in_dim(down, replica * piece, piece, 0)
        return jnp.pad(down, ((0, piece_rows - piece), (0, 0)))

    def out_of(out):
        out = jnp.pad(out, ((0, nr * part + part_rows - own_rows), (0, 0)))
        out = lax.dynamic_slice_in_dim(out, replica * part, part_rows, 0)
        valid = lax.broadcasted_iota(jnp.int32, out.shape, 0)
        valid = (valid < part) & (valid + replica * part < own_rows)
        return jnp.where(valid, out, jnp.zeros_like(out))

    qkv_send = head_columns(plan, w_qkv)
    first = plan.exchange_fsdp(qkv_send[0]).reshape(nf * own_rows, 3 * span)
    hidden = plan.regroup(tokens[0]).astype(F32)
    small = jnp.concatenate(
        [norm1_gain, norm1_shift, b_query, b_value, b_out, norm2_gain, norm2_shift, b_down, b_up],
        axis=1,
    )
    each_small = small.shape[1]
    small = small.reshape(-1)
    flat_rows = -(-small.shape[0] // 2048) * 16
    small = jnp.pad(small, (0, flat_rows * 128 - small.shape[0])).reshape(flat_rows, 128)
    small = plan.gather_owners(small)
    small = small.reshape(nz * nf, flat_rows * 128)[:, : layers * each_small]
    small = small.reshape(nz * nf, layers, each_small)

    codes = segments[0] * CODE + seq * length + jnp.arange(length, dtype=jnp.int32)
    codes = plan.gather_doubling(plan.regroup(codes[None]))

    outs = jnp.concatenate([out_of(w_out[layer]) for layer in range(layers)])
    first, qkv_send, w_up, w_down, outs, small, codes = lax.optimization_barrier(
        (first, qkv_send, w_up, w_down, outs, small, codes)
    )
    grad = plan.regroup(after(cotangent[0], hidden)).astype(F32)
    up_send = unit_columns(plan, w_up, piece, piece_rows)
    prepared = []
    for layer in range(layers):
        qkv = first
        if layer:
            qkv = plan.exchange_fsdp(qkv_send[layer]).reshape(nf * own_rows, 3 * span)
        up = plan.exchange_fsdp(up_send[layer]).reshape(nf * own_rows, units)
        prepared.append((qkv, up, down_of(w_down[layer])))
    early = [prepared[0][1:], prepared[1:]]
    codes, early = lax.optimization_barrier((codes, early))
    prepared = [(first, *early[0])] + early[1]

    weights = []
    for layer, (qkv, up, down) in enumerate(prepared):
        qkv = gather_seq(qkv)
        if layer == 0:
            outs = gather_seq(outs).reshape(nz, layers, part_rows, width)
        up = gather_seq(up)
        down = gather_seq(down, lead=layer % 2 == 0)
        weights.append((qkv, up, down))

    source = plan.source()
    feature_heads = (source[:, None] * span + jnp.arange(span, dtype=jnp.int32)).reshape(-1)
    fs = jnp.array(plan.place, dtype=jnp.int32)[source]
    inner = jnp.arange(part_rows, dtype=jnp.int32)
    within = (fs % nr)[:, None, None] * part + inner
    feature_rows = (
        jnp.arange(nz, dtype=jnp.int32)[None, :, None] * (nf * own_rows)
        + (fs // nr)[:, None, None] * own_rows
        + within
    )
    feature_rows = jnp.where((inner < part) & (within < own_rows), feature_rows, -1).reshape(-1)
    select = (feature_heads[:, None] == feature_rows[None, :]).astype(BF)

    def vectors(layer):
        each = [
            small[:, layer, i * own_rows : (i + 1) * own_rows].reshape(width).astype(F32)
            for i in range(8)
        ]
        bias_up = small[:, layer, 8 * own_rows :].reshape(nz, nf, nr, piece)
        bias_up = lax.dynamic_index_in_dim(bias_up, fsdp, 1, keepdims=False)
        bias_up = lax.dynamic_index_in_dim(bias_up, replica, 1, keepdims=False)

        def mine(v):
            return lax.dynamic_slice_in_dim(
                jnp.pad(v, (0, group * span - width)), rank * span, span
            )

        bias_qkv = jnp.concatenate([mine(each[2]), jnp.zeros((span,), F32), mine(each[3])])
        bias_up = jnp.pad(bias_up, ((0, 0), (0, piece_rows - piece)))
        return each, bias_qkv, bias_up.reshape(units).astype(F32)

    vecs = [vectors(layer) for layer in range(layers)]

    def out_block(layer):
        return outs[:, layer].reshape(nz * part_rows, width)

    kept = []
    for layer in range(layers):
        qkv_w, up_w, down_w = weights[layer]
        (gain1, shift1, _, _, bias_out, gain2, shift2, bias_down), bias_qkv, bias_up = vecs[layer]
        unit1, inv1 = norm_parts(hidden)
        pieces = plan.gather_pieces(widen((unit1 * gain1 + shift1).astype(BF)))
        if layer == 0:
            grad_pieces = plan.gather_pieces(widen(after(grad.astype(BF), pieces)))
        normed, packed, lse, mixed = attend(plan, pieces, qkv_w, bias_qkv, codes, total, scale)
        out_w = out_block(layer)
        out_w = plan.gather_pieces(widen(after(out_w, pieces) if layer else out_w))
        weights[layer] = qkv_w, out_w, up_w, down_w
        mixed = jnp.concatenate(plan.exchange(mixed), axis=1)
        mixed = dot(mixed, select).astype(BF)
        block = nz * part_rows
        mixed_own = plan.exchange(
            jnp.concatenate([mixed[:, i * block : (i + 1) * block] for i in range(group)])
        )
        middle = hidden + (project(plan, mixed, out_w, width) + bias_out)
        unit2, inv2 = norm_parts(middle)
        pieces = plan.gather_pieces(widen((unit2 * gain2 + shift2).astype(BF)))
        if layer == layers - 1:
            normed_two, slope, activated = lift_units(plan, pieces, up_w, bias_up)
        else:
            normed_two, slope, activated, near, far = hidden_units(
                plan, pieces, up_w, bias_up, down_w
            )
        kept.append(
            (
                unit1,
                inv1,
                normed,
                packed,
                lse,
                jnp.concatenate(mixed_own),
                unit2,
                inv2,
                normed_two,
                slope,
                activated,
            )
        )
        if layer < layers - 1:
            hidden = middle + (plan.scatter_parts(near, far) + bias_down)

    def late_up(up, layer):
        up = plan.to_owners(up)
        if plan.cube:
            ranks = [[plan.rank_of(f, r) for r in range(nr)] for f in range(nf)]
            return into_layer(
                functools.partial(units_back_kernel, nz, nf, nr, piece, piece_rows, ranks),
                plan,
                up,
                (layers, own_rows, nf * nz * nr * piece),
                layer,
                into_up,
                [],
            )
        up = jnp.stack([up[plan.back[m]] for m in range(group)])
        up = up.reshape(nf, nr, own_rows, nz, piece_rows)[..., :piece].transpose(2, 3, 0, 1, 4)
        up = up.reshape(1, own_rows, -1).astype(F32)
        return up if into_up is None else jnp.concatenate([up, into_up])

    def late_qkv(qkv, layer):
        qkv = plan.to_owners(qkv)
        if plan.cube:
            return into_layer(
                functools.partial(heads_back_kernel, group, span),
                plan,
                qkv,
                (layers, own_rows, triple),
                layer,
                into_qkv,
                [pltpu.VMEM((own_rows, 3 * group * span), F32)],
            )
        qkv = qkv.reshape(group, own_rows, 3, span).transpose(1, 2, 0, 3)
        qkv = qkv.reshape(own_rows, 3, group * span)[:, :, :width]
        qkv = qkv.reshape(1, own_rows, triple).astype(F32)
        return qkv if into_qkv is None else jnp.concatenate([qkv, into_qkv])

    def late_rows(v, rows, kept, layer, previous):
        if not plan.cube:
            v = lax.all_gather(v, REPLICA, axis=0, tiled=False)
            v = v[:, :kept].reshape(nr * kept, width)[None, :rows].astype(F32)
            return v if previous is None else jnp.concatenate([v, previous])
        operands = [v, plan.swap_x(v)]
        in_specs = [pl.BlockSpec(v.shape, lambda i, s: (0, 0))] * 2
        operands = [replica.astype(jnp.int32).reshape(1)] + operands
        aliases = {}
        if previous is not None:
            operands.append(previous)
            in_specs.append(pl.BlockSpec(memory_space=pl.ANY))
            aliases = {3: 0}
        return pl.pallas_call(
            functools.partial(rows_back_kernel, kept),
            grid_spec=pltpu.PrefetchScalarGridSpec(
                num_scalar_prefetch=1,
                grid=(1,),
                in_specs=in_specs,
                out_specs=pl.BlockSpec((1, rows, width), lambda i, s: (layer, 0, 0)),
            ),
            out_shape=sds((layers, rows, width), F32),
            input_output_aliases=aliases,
            compiler_params=pltpu.CompilerParams(vmem_limit_bytes=44 * 1024 * 1024),
            cost_estimate=pl.CostEstimate(
                flops=0, bytes_accessed=12 * v.size, transcendentals=0
            ),
        )(*operands)

    def late_down(down, layer):
        return late_rows(down, own_hidden, piece, layer, into_down)

    def late_out(out, layer):
        return late_rows(out, own_rows, part, layer, into_out)

    into_qkv = into_up = into_down = into_out = None
    smalls = [None] * layers
    late = None
    for layer in reversed(range(layers)):
        qkv_w, out_w, up_w, down_w = weights[layer]
        (gain1, _, _, _, _, gain2, _, _), _, _ = vecs[layer]
        unit1, inv1, normed, packed, lse, mixed, unit2, inv2, normed_two, slope, activated = kept[
            layer
        ]
        g_low = grad.astype(BF)
        grad_down = down_grad(plan, activated, grad_pieces, width)
        if late is not None:
            above = layer + 1
            out = scatter_seq(down_grad(plan, *late[2], width))
            if above == layers - 1:
                output = plan.regroup(hidden.astype(BF), back=True)
            into_up = late_up(late[0], above)
            into_down = late_down(late[1], above)
            into_out = late_out(out, above)
            into_qkv = late_qkv(late[3], above)
        if late is None:
            grad_pieces, grad_down = lax.optimization_barrier((grad_pieces, grad_down))
        down = scatter_seq(grad_down, lead=True)
        g_lift, grad_b_up, near, far = hidden_back(
            plan, grad_pieces, slope, down_w, up_w
        )
        grad_up = wgrad(plan, normed_two, g_lift)
        g_n2 = plan.scatter_parts(near, far)
        up = scatter_seq(grad_up).reshape(nf, own_rows, units)
        g_mid = grad + norm_pull(g_n2, unit2, inv2, gain2)
        g_att = g_mid.astype(BF)
        g_mixed = project_back(plan, g_att, out_w)
        g_mixed = dot(g_mixed, select, 1, 1).astype(BF)
        g_mixed = jnp.concatenate(
            [g_mixed[:, i * span : (i + 1) * span] for i in range(group)]
        )
        g_mixed = plan.exchange(g_mixed)
        if late is None:
            parts = lower_units(plan, after(activated, g_lift), down_w)
            hidden = middle + (plan.scatter_parts(*parts, g_mixed) + bias_down)
        att_pieces = plan.gather_pieces(widen(g_att))
        g_packed, g_b, near, far = attend_back(
            plan, g_mixed, packed, lse, codes, qkv_w, total, scale
        )
        grad_qkv = wgrad(plan, normed, g_packed)
        g_n1 = plan.scatter_parts(near, far)
        qkv = scatter_seq(grad_qkv)
        qkv = qkv.reshape(nf, own_rows, 3 * span)
        if layer == 0:
            into_up = late_up(up, layer)
            into_down = late_down(down, layer)
        late = (up, down, (after(mixed, g_n1 if layer else grad_qkv), att_pieces), qkv)
        smalls[layer] = (
            jnp.sum(g_n1 * unit1, axis=0),
            jnp.sum(g_n1, axis=0),
            g_b,
            jnp.sum(g_att.astype(F32), axis=0),
            jnp.sum(g_n2 * unit2, axis=0),
            jnp.sum(g_n2, axis=0),
            jnp.sum(g_low.astype(F32), axis=0),
            grad_b_up,
        )
        grad = g_mid + norm_pull(g_n1, unit1, inv1, gain1)
        if layer:
            grad_pieces = plan.gather_pieces(widen(grad.astype(BF)))
    out = scatter_seq(down_grad(plan, *late[2], width))
    grad_tokens = plan.regroup(grad.astype(BF), back=True).astype(F32)
    into_qkv = late_qkv(after(late[3], (into_up, into_down)), 0)
    output = after(output, grad).astype(F32)
    into_out = late_out(out, 0)

    def scattered(layer):
        n1g, n1s, g_b, b_o, n2g, n2s, b_d, b_u = smalls[layer]

        def place(v):
            full = lax.dynamic_update_slice_in_dim(
                jnp.zeros((group * span,), F32), v, rank * span, 0
            )
            return full[:width]

        b_u = lax.dynamic_update_slice(
            jnp.zeros((nz, nf, nr, piece), F32),
            b_u.reshape(nz, 1, 1, piece_rows)[..., :piece],
            (0, fsdp, replica, 0),
        )
        rows = [n1g, n1s, place(g_b[:span]), place(g_b[2 * span :]), b_o, n2g, n2s, b_d]
        return jnp.concatenate(
            [v.reshape(nz * nf, own_rows) for v in rows] + [b_u.reshape(nz * nf, own_hidden)],
            axis=1,
        )

    flat = jnp.concatenate([scattered(layer) for layer in range(layers)], axis=1)
    wide = lanes(-(-flat.shape[1] // 2))
    flat = jnp.pad(flat, ((0, 0), (0, 2 * wide - flat.shape[1])))
    flat = plan.scatter_small(flat.reshape(nz, nf, 2, wide))
    flat = jnp.sum(plan.to_owners_small(flat), axis=0).reshape(-1)
    flat = flat[: layers * each_small].reshape(layers, each_small)
    vec = [flat[:, i * own_rows : (i + 1) * own_rows] for i in range(8)]
    return (
        output[None],
        grad_tokens[None],
        vec[0],
        vec[1],
        into_qkv,
        vec[2],
        vec[3],
        into_out,
        vec[4],
        vec[5],
        vec[6],
        into_up,
        flat[:, 8 * own_rows :],
        into_down,
        vec[7],
    )


def solution(mesh):
    plan = Plan(mesh)
    data = P((FSDP, REPLICA), SEQ, None)
    vector = P(None, (SEQ, FSDP))
    matrix = P(None, (SEQ, FSDP), None)
    weights = (
        vector,
        vector,
        matrix,
        vector,
        vector,
        matrix,
        vector,
        vector,
        vector,
        matrix,
        vector,
        matrix,
        vector,
    )
    in_specs = (data, data, P((FSDP, REPLICA), SEQ)) + weights
    out_specs = (data, data) + weights
    return jax.shard_map(
        functools.partial(shards, plan),
        mesh=mesh,
        in_specs=in_specs,
        out_specs=out_specs,
        check_vma=False,
    )
```

```python
import functools
import math

import jax
import jax.numpy as jnp
from jax import lax
from jax.experimental import pallas as pl
from jax.experimental.pallas import tpu as pltpu
from jax.sharding import PartitionSpec as P


HEADS = 25
HD = 64
BF = jnp.bfloat16
F32 = jnp.float32
CODE = 65536
LOW = -1e30
SEQ, FSDP, REPLICA = "seq", "fsdp", "replica"
QK, PV, PK = "sqhd,skhd->shqk", "shqk,skhd->sqhd", "shqk,sqhd->skhd"
ALL = (SEQ, FSDP, REPLICA)
GROUP = (FSDP, REPLICA)
OWNERS = (SEQ, FSDP)


def dot(a, b, ca=1, cb=0):
    return lax.dot_general(a, b, (((ca,), (cb,)), ((), ())), preferred_element_type=F32)


def norm_parts(v):
    mean = jnp.mean(v, axis=-1, keepdims=True)
    centred = v - mean
    spread = jnp.mean(centred * centred, axis=-1, keepdims=True)
    inv = lax.rsqrt(spread + 1e-05)
    return centred * inv, inv


def norm_pull(grad, unit, inv, gain):
    scaled = grad * gain
    first = jnp.mean(scaled, axis=-1, keepdims=True)
    second = jnp.mean(scaled * unit, axis=-1, keepdims=True)
    return inv * (scaled - first - unit * second)


def gelu_both(value):
    tanh = jnp.tanh(0.7978845608028654 * (value + 0.044715 * value * value * value))
    inner = 0.7978845608028654 * (1.0 + 3.0 * 0.044715 * value * value)
    half = 0.5 * (1.0 + tanh)
    return value * half, half + 0.5 * value * (1.0 - tanh * tanh) * inner


class Plan:
    def __init__(self, mesh):
        self.nz = mesh.shape[SEQ]
        self.nf = mesh.shape[FSDP]
        self.nr = mesh.shape[REPLICA]
        self.group = self.nf * self.nr
        self.cube = self.nf == 4 and self.nr == 2
        self.heads = 2 * -(-HEADS // (2 * self.group))
        self.span = self.heads * HD
        order = sorted(
            (self.rank_of(f, r), f * self.nr + r) for f in range(self.nf) for r in range(self.nr)
        )
        self.place = [member for _, member in order]
        self.back = [0] * self.group
        for rank, member in order:
            self.back[member] = rank

    def rank_of(self, f, r):
        half = self.group // 2
        if self.nf % 2:
            return f * self.nr + r
        return (f % 2) * half + (f // 2) * self.nr + r

    def rank(self):
        return self.rank_of(lax.axis_index(FSDP), lax.axis_index(REPLICA))

    def regroup(self, v, back=False):
        nz = self.nz
        pairs = []
        for z in range(nz):
            for g in range(self.group):
                goal = g % nz
                slot = (g // nz) * nz + (z ^ goal if nz & (nz - 1) == 0 else z)
                pairs.append((z * self.group + self.place[g], goal * self.group + self.place[slot]))
        if back:
            pairs = [(there, here) for here, there in pairs]
        return lax.ppermute(v, ALL, pairs)

    def swap_core(self, v):
        return lax.ppermute(v, FSDP, [(f, f ^ 1) for f in range(self.nf)])

    def swap_y(self, v):
        return lax.ppermute(v, FSDP, [(f, f ^ 2) for f in range(self.nf)])

    def swap_x(self, v):
        return lax.ppermute(v, REPLICA, [(r, r ^ 1) for r in range(self.nr)])

    def swap_xy(self, v):
        pairs = [
            (f * self.nr + r, (f ^ 2) * self.nr + (r ^ 1))
            for f in range(self.nf)
            for r in range(self.nr)
        ]
        return lax.ppermute(v, GROUP, pairs)

    def source(self):
        base = jnp.arange(self.group, dtype=jnp.int32)
        return base ^ self.rank() if self.cube else base

    def gather_pieces(self, v):
        if not self.cube:
            full = lax.all_gather(v, GROUP, axis=0, tiled=False)
            return [full[member] for member in self.place]
        near = [v, self.swap_x(v), self.swap_y(v), self.swap_xy(v)]
        return near + [self.swap_core(piece) for piece in near]

    def gather_doubling(self, v):
        if not self.cube:
            return jnp.concatenate(self.gather_pieces(v))
        for swap in (self.swap_x, self.swap_y, self.swap_core):
            v = jnp.concatenate([v, swap(v)])
        return v

    def scatter_parts(self, near, far, gate=None):
        if not self.cube:
            blocks = jnp.concatenate([near.astype(BF), far])
            rows = blocks.shape[0] // self.group
            blocks = blocks.reshape(self.group, rows, -1)[jnp.array(self.back)]
            blocks = blocks.reshape(self.group * rows, -1)
            return lax.psum_scatter(blocks, GROUP, scatter_dimension=0, tiled=True).astype(F32)
        rows, columns = near.shape[0] // 4, near.shape[1]
        own, to_x, to_y, to_xy = call(
            fold_kernel,
            [sds((rows, columns), F32)] + [sds((rows, lanes(columns)), BF)] * 3,
            [],
            0,
            [near, self.swap_core(far)],
        )
        parts = self.swap_xy(to_xy), self.swap_x(to_x), self.swap_y(to_y)
        if gate is not None:
            own = after(own, gate)
        parts = [part[:, :columns].astype(F32) for part in parts]
        return own + parts[0] + parts[1] + parts[2]

    def exchange(self, v):
        if not self.cube:
            v = v.reshape(self.group, -1, v.shape[1])[jnp.array(self.back)]
            v = lax.all_to_all(v, GROUP, split_axis=0, concat_axis=0, tiled=True)
            return [v[member] for member in self.place]
        rows = v.shape[0] // 8
        half = 4 * rows
        far = self.swap_core(v[half:])
        out = [[v[:rows], far[:rows]]]
        for i, swap in ((1, self.swap_x), (2, self.swap_y), (3, self.swap_xy)):
            both = swap(
                jnp.concatenate([v[i * rows : (i + 1) * rows], far[i * rows : (i + 1) * rows]])
            )
            out.append([both[:rows], both[rows:]])
        return [pair[0] for pair in out] + [pair[1] for pair in out]

    def flips(self, v):
        f = lax.axis_index(FSDP)
        v = v.reshape((2, 2) + v.shape[1:])
        v = jnp.where(f // 2 == 1, jnp.flip(v, 0), v)
        return jnp.where(f % 2 == 1, jnp.flip(v, 1), v)

    def gather_owners(self, v):
        if not self.cube or self.nz != 4:
            return lax.all_gather(v, OWNERS, axis=0, tiled=False)
        z, f = lax.axis_index(SEQ), lax.axis_index(FSDP)
        far = [
            lax.ppermute(v, SEQ, [(i, i ^ d) for i in range(4)]) if d else v for d in range(4)
        ]
        v = jnp.stack(far).reshape((2, 2) + v.shape)
        v = jnp.where(z // 2 == 1, jnp.flip(v, 0), v)
        v = jnp.where(z % 2 == 1, jnp.flip(v, 1), v)
        other = self.swap_core(v)
        v = jnp.stack([jnp.where(f % 2 == 0, v, other), jnp.where(f % 2 == 0, other, v)], axis=2)
        other = self.swap_y(v)
        v = jnp.stack([jnp.where(f // 2 == 0, v, other), jnp.where(f // 2 == 0, other, v)], axis=2)
        return v.reshape((16,) + v.shape[4:])

    def exchange_fsdp(self, v):
        if not self.cube:
            return lax.all_to_all(v, FSDP, split_axis=0, concat_axis=0, tiled=True)
        shape = v.shape
        v = self.flips(v)
        both = jnp.stack([v[:, 0], self.swap_core(v[:, 1])], axis=1)
        return self.flips(jnp.stack([both[0], self.swap_y(both[1])]).reshape(shape)).reshape(shape)

    def scatter_small(self, v):
        if not self.cube or self.nz != 4:
            return lax.psum_scatter(v, SEQ, scatter_dimension=0, tiled=False)
        z = lax.axis_index(SEQ)
        total = lax.dynamic_index_in_dim(v, z, 0, keepdims=False)
        for d in range(1, 4):
            other = lax.dynamic_index_in_dim(v, z ^ d, 0, keepdims=False)
            total = total + lax.ppermute(other, SEQ, [(i, i ^ d) for i in range(4)])
        return total

    def to_owners_small(self, v):
        if not self.cube:
            v = lax.all_to_all(v, FSDP, split_axis=0, concat_axis=0, tiled=True)
            v = lax.all_gather(v, REPLICA, axis=1, tiled=False)
            return jnp.stack([v[m // self.nr, m % self.nr] for m in self.place])
        v = self.flips(v)
        far = self.swap_core(v[:, 1])
        here = jnp.stack([v[0, 0], far[0]])
        there = jnp.stack([v[1, 0], far[1]])
        return jnp.stack(
            [here, self.swap_x(here), self.swap_y(there), self.swap_xy(there)], axis=1
        ).reshape((8,) + v.shape[2:])

    def to_owners(self, v):
        if not self.cube:
            return self.to_owners_small(v)
        nf, rows, columns = v.shape
        f = lax.axis_index(FSDP)
        pick = (f ^ jnp.arange(nf, dtype=jnp.int32)).astype(jnp.int32)
        pair = sds((2, rows, columns), BF)
        near, far = pl.pallas_call(
            pick_kernel,
            grid_spec=pltpu.PrefetchScalarGridSpec(
                num_scalar_prefetch=1,
                grid=(1,),
                in_specs=[pl.BlockSpec(v.shape, lambda i, s: (0, 0, 0))],
                out_specs=[pl.BlockSpec(pair.shape, lambda i, s: (0, 0, 0))] * 2,
            ),
            out_shape=[pair] * 2,
            compiler_params=pltpu.CompilerParams(vmem_limit_bytes=44 * 1024 * 1024),
        )(pick, v)
        here, there = call(pair_kernel, [pair] * 2, [], 0, [near, self.swap_core(far)])
        return [here, self.swap_x(here), self.swap_y(there), self.swap_xy(there)]


def pick_kernel(order, v, near, far):
    for y in range(2):
        near[y] = v[order[2 * y]]
        far[y] = v[order[2 * y + 1]]


def pair_kernel(near, far, here, there):
    for y, out in enumerate((here, there)):
        out[0] = near[y]
        out[1] = far[y]


def gather_seq(v, lead=False):
    if lead:
        return lax.all_gather(v[None], SEQ, axis=1, tiled=True)[0]
    return lax.all_gather(v, SEQ, axis=0, tiled=True)


def scatter_seq(v, lead=False):
    if lead:
        return lax.psum_scatter(v[None], SEQ, scatter_dimension=1, tiled=True)[0]
    return lax.psum_scatter(v, SEQ, scatter_dimension=0, tiled=True)


def call(kernel, outs, scratch, flops, operands, **more):
    params = pltpu.CompilerParams(vmem_limit_bytes=44 * 1024 * 1024)
    size = sum(math.prod(o.shape) * o.dtype.itemsize for o in list(outs) + list(operands))
    return pl.pallas_call(
        kernel,
        out_shape=tuple(outs),
        scratch_shapes=scratch,
        compiler_params=params,
        cost_estimate=pl.CostEstimate(
            flops=int(flops), bytes_accessed=int(size), transcendentals=0
        ),
        **more,
    )(*operands)


def lanes(columns):
    return -(-columns // 128) * 128


def widen(v):
    return jnp.pad(v, ((0, 0), (0, lanes(v.shape[1]) - v.shape[1])))


def sds(shape, dtype):
    return jax.ShapeDtypeStruct(shape, dtype)


def fold_kernel(near, far, own, to_x, to_y, to_xy):
    rows, columns = own.shape
    own[...] = near[:rows, :] + far[:rows, :columns].astype(F32)
    for i, out in ((1, to_x), (2, to_y), (3, to_xy)):
        at = slice(i * rows, (i + 1) * rows)
        out[:, :columns] = (near[at, :] + far[at, :columns].astype(F32)).astype(BF)


def wgrad_kernel(left, right, out):
    tall = out.shape[0]
    block = 256

    def body(i, carry):
        at = pl.ds(pl.multiple_of(i * block, block), block)
        out[at, :] = dot(left[:, at], right[...], 0, 0).astype(BF)
        return carry

    whole = tall // block
    lax.fori_loop(0, whole, body, 0)
    if tall % block:
        out[whole * block :, :] = dot(left[:, whole * block :], right[...], 0, 0).astype(BF)


def wgrad(plan, left, right):
    if not plan.cube:
        return dot(left, right, 0, 0).astype(BF)
    tall, width = left.shape[1], right.shape[1]
    return call(
        wgrad_kernel, [sds((tall, width), BF)], [], 2 * left.size * width, [left, right]
    )[0]


def after(v, other):
    return lax.optimization_barrier((v, other))[0]


def project_kernel(count, left, *refs):
    block, width = refs[0].shape[0], refs[-1].shape[1]
    total = dot(left[:, :block], refs[0][:, :width])
    for i in range(1, count):
        total = total + dot(left[:, i * block : (i + 1) * block], refs[i][:, :width])
    refs[-1][...] = total


def project(plan, left, pieces, width):
    if not plan.cube:
        return dot(left, jnp.concatenate(pieces)[:, :width])
    shape = sds((left.shape[0], width), F32)
    kernel = functools.partial(project_kernel, len(pieces))
    return call(kernel, [shape], [], 2 * left.size * shape.shape[1], [left, *pieces])[0]


def project_back_kernel(count, left, *refs):
    block, width = refs[0].shape[0], left.shape[1]
    for i in range(count):
        part = dot(left[...], refs[i][:, :width], 1, 1)
        refs[-1][:, i * block : (i + 1) * block] = part.astype(BF)


def project_back(plan, left, pieces):
    if not plan.cube:
        return dot(left, jnp.concatenate(pieces)[:, : left.shape[1]], 1, 1).astype(BF)
    shape = sds((left.shape[0], len(pieces) * pieces[0].shape[0]), BF)
    kernel = functools.partial(project_back_kernel, len(pieces))
    return call(kernel, [shape], [], 2 * left.size * shape.shape[1], [left, *pieces])[0]


def first_half(shape):
    return lax.broadcasted_iota(jnp.int32, shape, 1) < HD


def attend_kernel(count, total, span, scale, *refs):
    pieces = refs[:count]
    w, bias, code_col, code_row, full, packed, lse, mixed = refs[count:]
    rows = pieces[0].shape[0]
    for i, piece in enumerate(pieces):
        full[i * rows : (i + 1) * rows, :] = piece[:, : full.shape[1]]
    block = 2 * rows

    def project(i, carry):
        at = pl.ds(pl.multiple_of(i * block, block), block)
        packed[at, :] = (dot(full[at, :], w[...]) + bias[...]).astype(BF)
        return carry

    lax.fori_loop(0, count // 2, project, 0)
    blocks = total // rows
    left = first_half((rows, 2 * HD))
    lane = lax.broadcasted_iota(jnp.int32, (rows, 128), 1)

    def queries(i, carry):
        at = pl.ds(pl.multiple_of(i * rows, rows), rows)
        seq = i // blocks
        keys_at = pl.ds(pl.multiple_of(seq * total, total), total)
        code_q = code_col[at, :]
        code_k = code_row[pl.ds(seq, 1), :]
        allowed = (code_k <= code_q) & (code_k >= (code_q // CODE) * CODE)
        stats = jnp.zeros((rows, 128), F32)
        for pair in range(span // 128):
            q = packed[at, pair * 128 : pair * 128 + 128]
            k = packed[keys_at, span + pair * 128 : span + pair * 128 + 128]
            v = packed[keys_at, 2 * span + pair * 128 : 2 * span + pair * 128 + 128]
            both = []
            for side in range(2):
                own = left if side == 0 else ~left
                scores = dot(jnp.where(own, q, jnp.zeros_like(q)), k, 1, 1) * scale
                scores = jnp.where(allowed, scores, LOW)
                top = jnp.max(scores, axis=1, keepdims=True)
                expo = jnp.exp(scores - top)
                denom = jnp.sum(expo, axis=1, keepdims=True)
                probs = (expo * (1.0 / denom)).astype(BF)
                both.append(dot(probs, v))
                stats = jnp.where(lane == 2 * pair + side, top + jnp.log(denom), stats)
            mixed[at, pair * 128 : pair * 128 + 128] = jnp.where(left, both[0], both[1]).astype(BF)
        lse[:, at] = stats.T[: lse.shape[0], :]
        return carry

    lax.fori_loop(0, count, queries, 0)


def attend(plan, pieces, w, bias, codes, total, scale):
    rows, width = pieces[0].shape[0], w.shape[0]
    count, span = plan.group, plan.span
    if not plan.cube:
        full = jnp.concatenate(pieces)[:, :width]
        packed = (dot(full, w) + bias).astype(BF)
        q, k, v = (
            packed[:, i * span : (i + 1) * span].reshape(-1, total, plan.heads, HD)
            for i in range(3)
        )
        allowed = mask_of(codes, total)
        scores = jnp.einsum(QK, q, k, preferred_element_type=F32) * scale
        scores = jnp.where(allowed[:, None], scores, LOW)
        top = jnp.max(scores, axis=-1, keepdims=True)
        expo = jnp.exp(scores - top)
        denom = jnp.sum(expo, axis=-1, keepdims=True)
        probs = (expo / denom).astype(BF)
        mixed = jnp.einsum(PV, probs, v, preferred_element_type=F32)
        return full, packed, top + jnp.log(denom), mixed.reshape(-1, span).astype(BF)
    tall = count * rows
    return call(
        functools.partial(attend_kernel, count, total, span, scale),
        [
            sds((tall, width), BF),
            sds((tall, 3 * span), BF),
            sds((8, tall), F32),
            sds((tall, span), BF),
        ],
        [],
        2 * tall * width * 3 * span + 8 * tall * total * span,
        [*pieces, w, bias[None], codes.reshape(-1, 1), codes.reshape(-1, total)],
    )


def mask_of(codes, total):
    code = codes.reshape(-1, total)
    low = (code // CODE) * CODE
    return (code[:, None, :] <= code[:, :, None]) & (code[:, None, :] >= low[:, :, None])


def attend_back_kernel(count, total, span, scale, *refs):
    pieces = refs[:count]
    packed, lse, code_col, code_row, w, g_packed, g_bias, near, far, gm, g_k, g_v = refs[count:]
    rows = pieces[0].shape[0]
    for i, piece in enumerate(pieces):
        gm[i * rows : (i + 1) * rows, :] = piece[...]
    blocks = total // rows
    left = first_half((rows, 2 * HD))

    def sequence(seq, carry):
        keys_at = pl.ds(pl.multiple_of(seq * total, total), total)
        code_k = code_col[keys_at, :]
        for pair in range(span // 128):
            lanes = slice(pair * 128, pair * 128 + 128)
            k_lanes = slice(span + pair * 128, span + pair * 128 + 128)
            v_lanes = slice(2 * span + pair * 128, 2 * span + pair * 128 + 128)
            k = packed[keys_at, k_lanes]
            v = packed[keys_at, v_lanes]
            g_k[...] = jnp.zeros_like(g_k)
            g_v[...] = jnp.zeros_like(g_v)

            def queries(i, inner):
                at = pl.ds(pl.multiple_of(seq * total + i * rows, rows), rows)
                code_q = code_row[pl.ds(seq * blocks + i, 1), :]
                allowed = (code_k <= code_q) & (code_k >= (code_q // CODE) * CODE)
                q = packed[at, lanes]
                g = gm[at, lanes]
                both = []
                for side in range(2):
                    own = left if side == 0 else ~left
                    q_own = jnp.where(own, q, jnp.zeros_like(q))
                    g_own = jnp.where(own, g, jnp.zeros_like(g))
                    scores = dot(k, q_own, 1, 1) * scale
                    row = 2 * pair + side
                    probs = jnp.exp(jnp.where(allowed, scores, LOW) - lse[row : row + 1, at])
                    g_probs = dot(v, g_own, 1, 1)
                    each = jnp.sum(g_probs * probs, axis=0, keepdims=True)
                    g_scores = (probs * (g_probs - each)).astype(BF)
                    g_v[...] += dot(probs.astype(BF), g_own)
                    g_k[...] += dot(g_scores, q_own)
                    both.append(dot(g_scores, k, 0, 0))
                g_packed[at, lanes] = (jnp.where(left, both[0], both[1]) * scale).astype(BF)
                return inner

            lax.fori_loop(0, blocks, queries, 0)
            g_packed[keys_at, k_lanes] = (g_k[...] * scale).astype(BF)
            g_packed[keys_at, v_lanes] = g_v[...].astype(BF)
        return carry

    lax.fori_loop(0, count // blocks, sequence, 0)
    g_bias[...] = jnp.sum(g_packed[...].astype(F32), axis=0, keepdims=True)
    spread_out(g_packed, w, near, far, 2 * rows)


def spread_out(left, right, near, far, block):
    half = near.shape[0]

    def first(i, carry):
        at = pl.ds(pl.multiple_of(i * block, block), block)
        near[at, :] = dot(left[at, :], right[...], 1, 1)
        return carry

    def second(i, carry):
        at = pl.ds(pl.multiple_of(i * block, block), block)
        far[at, : near.shape[1]] = dot(
            left[pl.ds(pl.multiple_of(half + i * block, block), block), :], right[...], 1, 1
        ).astype(BF)
        return carry

    lax.fori_loop(0, half // block, first, 0)
    lax.fori_loop(0, half // block, second, 0)


def halves(v):
    half = v.shape[0] // 2
    return v[:half], v[half:].astype(BF)


def attend_back(plan, pieces, packed, lse, codes, w, total, scale):
    count, span = plan.group, plan.span
    rows = pieces[0].shape[0]
    width = w.shape[0]
    if not plan.cube:
        q, k, v = (
            packed[:, i * span : (i + 1) * span].reshape(-1, total, plan.heads, HD)
            for i in range(3)
        )
        gm = jnp.concatenate(pieces).reshape(-1, total, plan.heads, HD)
        allowed = mask_of(codes, total)
        scores = jnp.einsum(QK, q, k, preferred_element_type=F32) * scale
        probs = jnp.exp(jnp.where(allowed[:, None], scores, LOW) - lse)
        g_probs = jnp.einsum(QK, gm, v, preferred_element_type=F32)
        g_v = jnp.einsum(PK, probs.astype(BF), gm, preferred_element_type=F32)
        row = jnp.sum(g_probs * probs, axis=-1, keepdims=True)
        g_s = (probs * (g_probs - row)).astype(BF)
        g_q = jnp.einsum(PV, g_s, k, preferred_element_type=F32) * scale
        g_k = jnp.einsum(PK, g_s, q, preferred_element_type=F32) * scale
        g_packed = jnp.concatenate(
            [u.reshape(-1, span).astype(BF) for u in (g_q, g_k, g_v)], axis=1
        )
        near, far = halves(dot(g_packed, w, 1, 1))
        return g_packed, jnp.sum(g_packed.astype(F32), axis=0), near, far
    tall = count * rows
    g_packed, g_bias, near, far = call(
        functools.partial(attend_back_kernel, count, total, span, scale),
        [
            sds((tall, 3 * span), BF),
            sds((1, 3 * span), F32),
            sds((tall // 2, width), F32),
            sds((tall // 2, lanes(width)), BF),
        ],
        [pltpu.VMEM((tall, span), BF)] + [pltpu.VMEM((total, 128), F32)] * 2,
        2 * tall * width * 3 * span + 20 * tall * total * span,
        [*pieces, packed, lse, codes.reshape(-1, 1), codes.reshape(-1, rows), w],
    )
    return g_packed, g_bias[0], near, far


def hidden_kernel(count, *refs):
    pieces = refs[:count]
    up, bias, down, full, slope, activated, near, far = refs[count:]
    rows = pieces[0].shape[0]
    for i, piece in enumerate(pieces):
        full[i * rows : (i + 1) * rows, :] = piece[:, : full.shape[1]]
    block = 2 * rows
    half = near.shape[0]

    def lift(at):
        value, pull = gelu_both(dot(full[at, :], up[...]) + bias[...])
        value = value.astype(BF)
        activated[at, :] = value
        slope[at, :] = pull.astype(BF)
        return dot(value, down[...])

    def first(i, carry):
        at = pl.ds(pl.multiple_of(i * block, block), block)
        near[at, :] = lift(at)
        return carry

    def second(i, carry):
        at = pl.ds(pl.multiple_of(i * block, block), block)
        out = lift(pl.ds(pl.multiple_of(half + i * block, block), block))
        far[at, : near.shape[1]] = out.astype(BF)
        return carry

    lax.fori_loop(0, half // block, first, 0)
    lax.fori_loop(0, half // block, second, 0)


def lift_kernel(count, *refs):
    pieces = refs[:count]
    up, bias, full, slope, activated = refs[count:]
    rows = pieces[0].shape[0]
    for i, piece in enumerate(pieces):
        full[i * rows : (i + 1) * rows, :] = piece[:, : full.shape[1]]
    block = 2 * rows

    def lift(i, carry):
        at = pl.ds(pl.multiple_of(i * block, block), block)
        value, pull = gelu_both(dot(full[at, :], up[...]) + bias[...])
        activated[at, :] = value.astype(BF)
        slope[at, :] = pull.astype(BF)
        return carry

    lax.fori_loop(0, count // 2, lift, 0)


def lift_units(plan, pieces, up, bias):
    rows, width = pieces[0].shape[0], up.shape[0]
    if not plan.cube:
        full = jnp.concatenate(pieces)[:, :width]
        value, pull = gelu_both(dot(full, up) + bias)
        return full, pull.astype(BF), value.astype(BF)
    tall, units = plan.group * rows, up.shape[1]
    return call(
        functools.partial(lift_kernel, plan.group),
        [sds((tall, width), BF), sds((tall, units), BF), sds((tall, units), BF)],
        [],
        2 * tall * width * units,
        [*pieces, up, bias[None]],
    )


def lower_kernel(block, left, right, near, far):
    half, width = near.shape

    def first(i, carry):
        at = pl.ds(pl.multiple_of(i * block, block), block)
        near[at, :] = dot(left[at, :], right[...])
        return carry

    def second(i, carry):
        at = pl.ds(pl.multiple_of(i * block, block), block)
        rows = left[pl.ds(pl.multiple_of(half + i * block, block), block), :]
        far[at, :width] = dot(rows, right[...]).astype(BF)
        return carry

    lax.fori_loop(0, half // block, first, 0)
    lax.fori_loop(0, half // block, second, 0)


def lower_units(plan, activated, down):
    tall, width = activated.shape[0], down.shape[1]
    if not plan.cube:
        return halves(dot(activated, down))
    return call(
        functools.partial(lower_kernel, 2 * (tall // plan.group)),
        [sds((tall // 2, width), F32), sds((tall // 2, lanes(width)), BF)],
        [],
        2 * activated.size * width,
        [activated, down],
    )


def hidden_units(plan, pieces, up, bias, down):
    rows, width = pieces[0].shape[0], up.shape[0]
    if not plan.cube:
        full = jnp.concatenate(pieces)[:, :width]
        value, pull = gelu_both(dot(full, up) + bias)
        value = value.astype(BF)
        return (full, pull.astype(BF), value) + halves(dot(value, down))
    tall, units = plan.group * rows, up.shape[1]
    return call(
        functools.partial(hidden_kernel, plan.group),
        [
            sds((tall, width), BF),
            sds((tall, units), BF),
            sds((tall, units), BF),
            sds((tall // 2, width), F32),
            sds((tall // 2, lanes(width)), BF),
        ],
        [],
        4 * tall * width * units,
        [*pieces, up, bias[None], down],
    )


def hidden_back_kernel(count, *refs):
    pieces = refs[:count]
    slope, down, up, g_lift, g_bias, near, far, full = refs[count:]
    rows = pieces[0].shape[0]
    for i, piece in enumerate(pieces):
        full[i * rows : (i + 1) * rows, :] = piece[:, : full.shape[1]]
    block = 2 * rows

    def pull(i, carry):
        at = pl.ds(pl.multiple_of(i * block, block), block)
        g_lift[at, :] = (dot(full[at, :], down[...], 1, 1) * slope[at, :].astype(F32)).astype(BF)
        return carry

    lax.fori_loop(0, count // 2, pull, 0)
    spread_out(g_lift, up, near, far, block)
    g_bias[...] = jnp.sum(g_lift[...].astype(F32), axis=0, keepdims=True)


def hidden_back(plan, pieces, slope, down, up):
    rows, width = pieces[0].shape[0], up.shape[0]
    if not plan.cube:
        full = jnp.concatenate(pieces)[:, :width]
        g_lift = (dot(full, down, 1, 1) * slope.astype(F32)).astype(BF)
        return (g_lift, jnp.sum(g_lift.astype(F32), axis=0)) + halves(dot(g_lift, up, 1, 1))
    tall, units = plan.group * rows, up.shape[1]
    g_lift, g_bias, near, far = call(
        functools.partial(hidden_back_kernel, plan.group),
        [
            sds((tall, units), BF),
            sds((1, units), F32),
            sds((tall // 2, width), F32),
            sds((tall // 2, lanes(width)), BF),
        ],
        [pltpu.VMEM((tall, width), BF)],
        4 * tall * width * units,
        [*pieces, slope, down, up],
    )
    return g_lift, g_bias[0], near, far


def down_grad_kernel(count, *refs):
    left, out, full = refs[count:]
    rows = refs[0].shape[0]
    for i, piece in enumerate(refs[:count]):
        full[i * rows : (i + 1) * rows, :] = piece[:, : full.shape[1]]
    wgrad_kernel(left, full, out)


def down_grad(plan, left, pieces, width):
    if not plan.cube:
        return dot(left, jnp.concatenate(pieces)[:, :width], 0, 0).astype(BF)
    tall, units = left.shape
    return call(
        functools.partial(down_grad_kernel, plan.group),
        [sds((units, width), BF)],
        [pltpu.VMEM((tall, width), BF)],
        2 * left.size * width,
        [*pieces, left],
    )[0]


def head_columns_kernel(nf, ranks, span, x_ref, w_ref, out, wide):
    width = w_ref.shape[2] // 3
    padded = wide.shape[1] // 3
    w = w_ref[0].astype(F32)
    for i in range(3):
        wide[:, i * padded : i * padded + width] = w[:, i * width : (i + 1) * width]
        if padded > width:
            wide[:, i * padded + width : (i + 1) * padded] = jnp.zeros(
                (wide.shape[0], padded - width), F32
            )
    for x, row in enumerate(ranks):

        @pl.when(x_ref[0] == x)
        def _():
            for f in range(nf):
                for i in range(3):
                    start = i * padded + row[f] * span
                    out[0, f, :, i * span : (i + 1) * span] = wide[:, start : start + span].astype(
                        BF
                    )


def unit_columns_kernel(nz, nf, nr, piece, piece_rows, x_ref, w_ref, out):
    w = w_ref[0].astype(F32)
    for x in range(nr):

        @pl.when(x_ref[0] == x)
        def _():
            for f in range(nf):
                part = []
                for z in range(nz):
                    start = ((z * nf + f) * nr + x) * piece
                    part.append(w[:, start : start + piece])
                    if piece_rows > piece:
                        part.append(jnp.zeros((w.shape[0], piece_rows - piece), F32))
                out[0, f] = jnp.concatenate(part, axis=1).astype(BF)


def layered(kernel, x, w, columns, nf, scratch):
    layers, rows, full = w.shape
    return pl.pallas_call(
        kernel,
        grid_spec=pltpu.PrefetchScalarGridSpec(
            num_scalar_prefetch=1,
            grid=(layers,),
            in_specs=[pl.BlockSpec((1, rows, full), lambda i, s: (i, 0, 0))],
            out_specs=pl.BlockSpec((1, nf, rows, columns), lambda i, s: (i, 0, 0, 0)),
            scratch_shapes=scratch,
        ),
        out_shape=sds((layers, nf, rows, columns), BF),
        compiler_params=pltpu.CompilerParams(vmem_limit_bytes=44 * 1024 * 1024),
        cost_estimate=pl.CostEstimate(flops=0, bytes_accessed=4 * w.size, transcendentals=0),
    )(x, w)


def head_columns(plan, w):
    layers, rows, triple = w.shape
    nf, nr, span, group = plan.nf, plan.nr, plan.span, plan.group
    ranks = [[plan.rank_of(f, r) for f in range(nf)] for r in range(nr)]
    x = lax.axis_index(REPLICA)
    if not plan.cube:
        width = triple // 3
        v = w.reshape(layers, rows, 3, width)
        v = jnp.pad(v, ((0, 0), (0, 0), (0, 0), (0, group * span - width)))
        v = jnp.take(v.reshape(layers, rows, 3, group, span), jnp.array(ranks)[x], axis=3)
        return v.transpose(0, 3, 1, 2, 4).reshape(layers, nf, rows, 3 * span)
    return layered(
        functools.partial(head_columns_kernel, nf, ranks, span),
        x.astype(jnp.int32).reshape(1),
        w,
        3 * span,
        nf,
        [pltpu.VMEM((rows, 3 * group * span), F32)],
    )


def unit_columns(plan, w, piece, piece_rows):
    layers, rows, _ = w.shape
    nz, nf, nr = plan.nz, plan.nf, plan.nr
    x = lax.axis_index(REPLICA)
    if not plan.cube:
        v = w.reshape(layers, rows, nz, nf, nr, piece)
        v = lax.dynamic_index_in_dim(v, x, 4, keepdims=False)
        v = jnp.pad(v, ((0, 0),) * 4 + ((0, piece_rows - piece),))
        return v.transpose(0, 3, 1, 2, 4).reshape(layers, nf, rows, nz * piece_rows)
    return layered(
        functools.partial(unit_columns_kernel, nz, nf, nr, piece, piece_rows),
        x.astype(jnp.int32).reshape(1),
        w,
        nz * piece_rows,
        nf,
        [],
    )


def stacked(pairs, block):
    for i, pair in enumerate(pairs):
        for core in range(2):
            block[4 * core + i] = pair[core]


def heads_back_kernel(group, span, src_ref, *refs):
    out, wide, v_ref = refs[-3:]
    stacked(refs[:4], v_ref)
    width = out.shape[2] // 3
    padded = group * span
    for rank in range(group):
        block = v_ref[src_ref[rank]].astype(F32)
        for i in range(3):
            wide[:, i * padded + rank * span : i * padded + (rank + 1) * span] = block[
                :, i * span : (i + 1) * span
            ]
    for i in range(3):
        out[0, :, i * width : (i + 1) * width] = wide[:, i * padded : i * padded + width]


def units_back_kernel(nz, nf, nr, piece, piece_rows, ranks, src_ref, *refs):
    out, v_ref = refs[-2:]
    stacked(refs[:4], v_ref)
    for f in range(nf):
        blocks = [v_ref[src_ref[ranks[f][r]]].astype(F32) for r in range(nr)]
        for z in range(nz):
            part = [block[:, z * piece_rows : z * piece_rows + piece] for block in blocks]
            start = (z * nf + f) * nr * piece
            out[0, :, start : start + nr * piece] = jnp.concatenate(part, axis=1)


def into_layer(kernel, plan, pairs, shape, layer, previous, scratch):
    operands = [plan.source().astype(jnp.int32), *pairs]
    in_specs = [pl.BlockSpec(v.shape, lambda i, s: (0, 0, 0)) for v in pairs]
    scratch = scratch + [pltpu.VMEM((8,) + pairs[0].shape[1:], BF)]
    aliases = {}
    if previous is not None:
        operands.append(previous)
        in_specs.append(pl.BlockSpec(memory_space=pl.ANY))
        aliases = {5: 0}
    return pl.pallas_call(
        kernel,
        grid_spec=pltpu.PrefetchScalarGridSpec(
            num_scalar_prefetch=1,
            grid=(1,),
            in_specs=in_specs,
            out_specs=pl.BlockSpec((1,) + shape[1:], lambda i, s: (layer, 0, 0)),
            scratch_shapes=scratch,
        ),
        out_shape=sds(shape, F32),
        input_output_aliases=aliases,
        compiler_params=pltpu.CompilerParams(vmem_limit_bytes=44 * 1024 * 1024),
        cost_estimate=pl.CostEstimate(flops=0, bytes_accessed=48 * pairs[0].size, transcendentals=0),
    )(*operands)


def rows_back_kernel(kept, x_ref, own, other, *refs):
    out = refs[-1]
    for x in range(2):

        @pl.when(x_ref[0] == x)
        def _():
            first, second = (own, other) if x == 0 else (other, own)
            first, second = (v[...].astype(F32)[:kept] for v in (first, second))
            if kept % 8:
                out[0] = jnp.concatenate([first, second])
            else:
                out[0, :kept, :] = first
                out[0, kept:, :] = second


def shards(
    plan,
    tokens,
    cotangent,
    segments,
    norm1_gain,
    norm1_shift,
    w_qkv,
    b_query,
    b_value,
    w_out,
    b_out,
    norm2_gain,
    norm2_shift,
    w_up,
    b_up,
    w_down,
    b_down,
):
    nz, nf, nr, group, span = plan.nz, plan.nf, plan.nr, plan.group, plan.span
    layers, own_rows, triple = w_qkv.shape
    width = triple // 3
    own_hidden = w_down.shape[1]
    piece = own_hidden // nr
    part = -(-own_rows // nr)
    part_rows = -(-part // 16) * 16
    piece_rows = -(-piece // 16) * 16
    units = nz * piece_rows
    length = tokens.shape[1]
    total = length * nz
    scale = 1.0 / math.sqrt(HD)
    fsdp = lax.axis_index(FSDP)
    replica = lax.axis_index(REPLICA)
    seq = lax.axis_index(SEQ)
    rank = plan.rank()

    def down_of(down):
        down = lax.dynamic_slice_in_dim(down, replica * piece, piece, 0)
        return jnp.pad(down, ((0, piece_rows - piece), (0, 0)))

    def out_of(out):
        out = jnp.pad(out, ((0, nr * part + part_rows - own_rows), (0, 0)))
        out = lax.dynamic_slice_in_dim(out, replica * part, part_rows, 0)
        valid = lax.broadcasted_iota(jnp.int32, out.shape, 0)
        valid = (valid < part) & (valid + replica * part < own_rows)
        return jnp.where(valid, out, jnp.zeros_like(out))

    qkv_send = head_columns(plan, w_qkv)
    first = plan.exchange_fsdp(qkv_send[0]).reshape(nf * own_rows, 3 * span)
    hidden = plan.regroup(tokens[0]).astype(F32)
    small = jnp.concatenate(
        [norm1_gain, norm1_shift, b_query, b_value, b_out, norm2_gain, norm2_shift, b_down, b_up],
        axis=1,
    )
    each_small = small.shape[1]
    small = small.reshape(-1)
    flat_rows = -(-small.shape[0] // 2048) * 16
    small = jnp.pad(small, (0, flat_rows * 128 - small.shape[0])).reshape(flat_rows, 128)
    small = plan.gather_owners(small)
    small = small.reshape(nz * nf, flat_rows * 128)[:, : layers * each_small]
    small = small.reshape(nz * nf, layers, each_small)

    codes = segments[0] * CODE + seq * length + jnp.arange(length, dtype=jnp.int32)
    codes = plan.gather_doubling(plan.regroup(codes[None]))

    outs = jnp.concatenate([out_of(w_out[layer]) for layer in range(layers)])
    first, qkv_send, w_up, w_down, outs, small, codes = lax.optimization_barrier(
        (first, qkv_send, w_up, w_down, outs, small, codes)
    )
    grad = plan.regroup(after(cotangent[0], hidden)).astype(F32)
    up_send = unit_columns(plan, w_up, piece, piece_rows)
    prepared = []
    for layer in range(layers):
        qkv = first
        if layer:
            qkv = plan.exchange_fsdp(qkv_send[layer]).reshape(nf * own_rows, 3 * span)
        up = plan.exchange_fsdp(up_send[layer]).reshape(nf * own_rows, units)
        prepared.append((qkv, up, down_of(w_down[layer])))
    early = [prepared[0][1:], prepared[1:]]
    codes, early = lax.optimization_barrier((codes, early))
    prepared = [(first, *early[0])] + early[1]

    weights = []
    for layer, (qkv, up, down) in enumerate(prepared):
        qkv = gather_seq(qkv)
        if layer == 0:
            outs = gather_seq(outs).reshape(nz, layers, part_rows, width)
        up = gather_seq(up)
        down = gather_seq(down, lead=layer % 2 == 0)
        weights.append((qkv, up, down))

    source = plan.source()
    feature_heads = (source[:, None] * span + jnp.arange(span, dtype=jnp.int32)).reshape(-1)
    fs = jnp.array(plan.place, dtype=jnp.int32)[source]
    inner = jnp.arange(part_rows, dtype=jnp.int32)
    within = (fs % nr)[:, None, None] * part + inner
    feature_rows = (
        jnp.arange(nz, dtype=jnp.int32)[None, :, None] * (nf * own_rows)
        + (fs // nr)[:, None, None] * own_rows
        + within
    )
    feature_rows = jnp.where((inner < part) & (within < own_rows), feature_rows, -1).reshape(-1)
    select = (feature_heads[:, None] == feature_rows[None, :]).astype(BF)

    def vectors(layer):
        each = [
            small[:, layer, i * own_rows : (i + 1) * own_rows].reshape(width).astype(F32)
            for i in range(8)
        ]
        bias_up = small[:, layer, 8 * own_rows :].reshape(nz, nf, nr, piece)
        bias_up = lax.dynamic_index_in_dim(bias_up, fsdp, 1, keepdims=False)
        bias_up = lax.dynamic_index_in_dim(bias_up, replica, 1, keepdims=False)

        def mine(v):
            return lax.dynamic_slice_in_dim(
                jnp.pad(v, (0, group * span - width)), rank * span, span
            )

        bias_qkv = jnp.concatenate([mine(each[2]), jnp.zeros((span,), F32), mine(each[3])])
        bias_up = jnp.pad(bias_up, ((0, 0), (0, piece_rows - piece)))
        return each, bias_qkv, bias_up.reshape(units).astype(F32)

    vecs = [vectors(layer) for layer in range(layers)]

    def out_block(layer):
        return outs[:, layer].reshape(nz * part_rows, width)

    kept = []
    for layer in range(layers):
        qkv_w, up_w, down_w = weights[layer]
        (gain1, shift1, _, _, bias_out, gain2, shift2, bias_down), bias_qkv, bias_up = vecs[layer]
        unit1, inv1 = norm_parts(hidden)
        pieces = plan.gather_pieces(widen((unit1 * gain1 + shift1).astype(BF)))
        if layer == 0:
            grad_pieces = plan.gather_pieces(widen(after(grad.astype(BF), pieces)))
        normed, packed, lse, mixed = attend(plan, pieces, qkv_w, bias_qkv, codes, total, scale)
        out_w = out_block(layer)
        out_w = plan.gather_pieces(widen(after(out_w, pieces) if layer else out_w))
        weights[layer] = qkv_w, out_w, up_w, down_w
        mixed = jnp.concatenate(plan.exchange(mixed), axis=1)
        mixed = dot(mixed, select).astype(BF)
        block = nz * part_rows
        mixed_own = plan.exchange(
            jnp.concatenate([mixed[:, i * block : (i + 1) * block] for i in range(group)])
        )
        middle = hidden + (project(plan, mixed, out_w, width) + bias_out)
        unit2, inv2 = norm_parts(middle)
        pieces = plan.gather_pieces(widen((unit2 * gain2 + shift2).astype(BF)))
        if layer == layers - 1:
            normed_two, slope, activated = lift_units(plan, pieces, up_w, bias_up)
        else:
            normed_two, slope, activated, near, far = hidden_units(
                plan, pieces, up_w, bias_up, down_w
            )
        kept.append(
            (
                unit1,
                inv1,
                normed,
                packed,
                lse,
                jnp.concatenate(mixed_own),
                unit2,
                inv2,
                normed_two,
                slope,
                activated,
            )
        )
        if layer < layers - 1:
            hidden = middle + (plan.scatter_parts(near, far) + bias_down)

    def late_up(up, layer):
        up = plan.to_owners(up)
        if plan.cube:
            ranks = [[plan.rank_of(f, r) for r in range(nr)] for f in range(nf)]
            return into_layer(
                functools.partial(units_back_kernel, nz, nf, nr, piece, piece_rows, ranks),
                plan,
                up,
                (layers, own_rows, nf * nz * nr * piece),
                layer,
                into_up,
                [],
            )
        up = jnp.stack([up[plan.back[m]] for m in range(group)])
        up = up.reshape(nf, nr, own_rows, nz, piece_rows)[..., :piece].transpose(2, 3, 0, 1, 4)
        up = up.reshape(1, own_rows, -1).astype(F32)
        return up if into_up is None else jnp.concatenate([up, into_up])

    def late_qkv(qkv, layer):
        qkv = plan.to_owners(qkv)
        if plan.cube:
            return into_layer(
                functools.partial(heads_back_kernel, group, span),
                plan,
                qkv,
                (layers, own_rows, triple),
                layer,
                into_qkv,
                [pltpu.VMEM((own_rows, 3 * group * span), F32)],
            )
        qkv = qkv.reshape(group, own_rows, 3, span).transpose(1, 2, 0, 3)
        qkv = qkv.reshape(own_rows, 3, group * span)[:, :, :width]
        qkv = qkv.reshape(1, own_rows, triple).astype(F32)
        return qkv if into_qkv is None else jnp.concatenate([qkv, into_qkv])

    def late_rows(v, rows, kept, layer, previous):
        if not plan.cube:
            v = lax.all_gather(v, REPLICA, axis=0, tiled=False)
            v = v[:, :kept].reshape(nr * kept, width)[None, :rows].astype(F32)
            return v if previous is None else jnp.concatenate([v, previous])
        operands = [v, plan.swap_x(v)]
        in_specs = [pl.BlockSpec(v.shape, lambda i, s: (0, 0))] * 2
        operands = [replica.astype(jnp.int32).reshape(1)] + operands
        aliases = {}
        if previous is not None:
            operands.append(previous)
            in_specs.append(pl.BlockSpec(memory_space=pl.ANY))
            aliases = {3: 0}
        return pl.pallas_call(
            functools.partial(rows_back_kernel, kept),
            grid_spec=pltpu.PrefetchScalarGridSpec(
                num_scalar_prefetch=1,
                grid=(1,),
                in_specs=in_specs,
                out_specs=pl.BlockSpec((1, rows, width), lambda i, s: (layer, 0, 0)),
            ),
            out_shape=sds((layers, rows, width), F32),
            input_output_aliases=aliases,
            compiler_params=pltpu.CompilerParams(vmem_limit_bytes=44 * 1024 * 1024),
            cost_estimate=pl.CostEstimate(
                flops=0, bytes_accessed=12 * v.size, transcendentals=0
            ),
        )(*operands)

    def late_down(down, layer):
        return late_rows(down, own_hidden, piece, layer, into_down)

    def late_out(out, layer):
        return late_rows(out, own_rows, part, layer, into_out)

    into_qkv = into_up = into_down = into_out = None
    smalls = [None] * layers
    late = None
    for layer in reversed(range(layers)):
        qkv_w, out_w, up_w, down_w = weights[layer]
        (gain1, _, _, _, _, gain2, _, _), _, _ = vecs[layer]
        unit1, inv1, normed, packed, lse, mixed, unit2, inv2, normed_two, slope, activated = kept[
            layer
        ]
        g_low = grad.astype(BF)
        grad_down = down_grad(plan, activated, grad_pieces, width)
        if late is not None:
            above = layer + 1
            out = scatter_seq(down_grad(plan, *late[2], width))
            into_up = late_up(late[0], above)
            into_down = late_down(late[1], above)
            into_out = late_out(out, above)
            into_qkv = late_qkv(late[3], above)
        if late is None:
            grad_pieces, grad_down = lax.optimization_barrier((grad_pieces, grad_down))
        down = scatter_seq(grad_down, lead=True)
        g_lift, grad_b_up, near, far = hidden_back(
            plan, grad_pieces, slope, down_w, up_w
        )
        grad_up = wgrad(plan, normed_two, g_lift)
        g_n2 = plan.scatter_parts(near, far)
        up = scatter_seq(grad_up).reshape(nf, own_rows, units)
        g_mid = grad + norm_pull(g_n2, unit2, inv2, gain2)
        g_att = g_mid.astype(BF)
        g_mixed = project_back(plan, g_att, out_w)
        g_mixed = dot(g_mixed, select, 1, 1).astype(BF)
        g_mixed = jnp.concatenate(
            [g_mixed[:, i * span : (i + 1) * span] for i in range(group)]
        )
        g_mixed = plan.exchange(g_mixed)
        if layer == 0:
            high = layers - 1
            parts = lower_units(plan, after(kept[high][-1], g_lift), weights[high][3])
            hidden = middle + (plan.scatter_parts(*parts, g_mixed) + bias_down)
            output = plan.regroup(hidden.astype(BF), back=True)
        att_pieces = plan.gather_pieces(widen(g_att))
        g_packed, g_b, near, far = attend_back(
            plan, g_mixed, packed, lse, codes, qkv_w, total, scale
        )
        grad_qkv = wgrad(plan, normed, g_packed)
        g_n1 = plan.scatter_parts(near, far)
        qkv = scatter_seq(grad_qkv)
        qkv = qkv.reshape(nf, own_rows, 3 * span)
        if layer == 0:
            into_up = late_up(up, layer)
            into_down = late_down(down, layer)
        late = (up, down, (after(mixed, g_n1 if layer else grad_qkv), att_pieces), qkv)
        smalls[layer] = (
            jnp.sum(g_n1 * unit1, axis=0),
            jnp.sum(g_n1, axis=0),
            g_b,
            jnp.sum(g_att.astype(F32), axis=0),
            jnp.sum(g_n2 * unit2, axis=0),
            jnp.sum(g_n2, axis=0),
            jnp.sum(g_low.astype(F32), axis=0),
            grad_b_up,
        )
        grad = g_mid + norm_pull(g_n1, unit1, inv1, gain1)
        if layer:
            grad_pieces = plan.gather_pieces(widen(grad.astype(BF)))
    out = scatter_seq(down_grad(plan, *late[2], width))
    grad_tokens = plan.regroup(grad.astype(BF), back=True).astype(F32)
    into_qkv = late_qkv(late[3], 0)
    output = after(output, grad).astype(F32)
    into_out = late_out(out, 0)

    def scattered(layer):
        n1g, n1s, g_b, b_o, n2g, n2s, b_d, b_u = smalls[layer]

        def place(v):
            full = lax.dynamic_update_slice_in_dim(
                jnp.zeros((group * span,), F32), v, rank * span, 0
            )
            return full[:width]

        b_u = lax.dynamic_update_slice(
            jnp.zeros((nz, nf, nr, piece), F32),
            b_u.reshape(nz, 1, 1, piece_rows)[..., :piece],
            (0, fsdp, replica, 0),
        )
        rows = [n1g, n1s, place(g_b[:span]), place(g_b[2 * span :]), b_o, n2g, n2s, b_d]
        return jnp.concatenate(
            [v.reshape(nz * nf, own_rows) for v in rows] + [b_u.reshape(nz * nf, own_hidden)],
            axis=1,
        )

    flat = jnp.concatenate([scattered(layer) for layer in range(layers)], axis=1)
    wide = lanes(-(-flat.shape[1] // 2))
    flat = jnp.pad(flat, ((0, 0), (0, 2 * wide - flat.shape[1])))
    flat = plan.scatter_small(flat.reshape(nz, nf, 2, wide))
    flat = jnp.sum(plan.to_owners_small(flat), axis=0).reshape(-1)
    flat = flat[: layers * each_small].reshape(layers, each_small)
    vec = [flat[:, i * own_rows : (i + 1) * own_rows] for i in range(8)]
    return (
        output[None],
        grad_tokens[None],
        vec[0],
        vec[1],
        into_qkv,
        vec[2],
        vec[3],
        into_out,
        vec[4],
        vec[5],
        vec[6],
        into_up,
        flat[:, 8 * own_rows :],
        into_down,
        vec[7],
    )


def solution(mesh):
    plan = Plan(mesh)
    data = P((FSDP, REPLICA), SEQ, None)
    vector = P(None, (SEQ, FSDP))
    matrix = P(None, (SEQ, FSDP), None)
    weights = (
        vector,
        vector,
        matrix,
        vector,
        vector,
        matrix,
        vector,
        vector,
        vector,
        matrix,
        vector,
        matrix,
        vector,
    )
    in_specs = (data, data, P((FSDP, REPLICA), SEQ)) + weights
    out_specs = (data, data) + weights
    return jax.shard_map(
        functools.partial(shards, plan),
        mesh=mesh,
        in_specs=in_specs,
        out_specs=out_specs,
        check_vma=False,
    )
```
